256 devices in a mesh: req: 32 (over x, y, core), kv: 8 (over z).
Axes of the slice: x: 4, y: 4, z: 8, core: 2. Of those that a mesh axis runs over, the one named last changes fastest.
Arguments:
- hidden_in: bfloat16 [256, 4096], P(None, 'req'), may hold values from -15 to 15
- norm_gain: bfloat16 [2, 4096], P(None, 'req'), may hold values from 0.5 to 1.5
- q_gain: bfloat16 [2, 128], replicated, may hold values from 0.25 to 1.75
- k_gain: bfloat16 [2, 128], replicated, may hold values from 0.25 to 1.75
- w_query: bfloat16 [2, 4096, 4096], P(None, 'req', 'kv'), may hold values from -0.09375 to 0.09375
- w_key: bfloat16 [2, 4096, 1024], P(None, 'req', 'kv'), may hold values from -0.09375 to 0.09375
- w_value: bfloat16 [2, 4096, 1024], P(None, 'req', 'kv'), may hold values from -0.09375 to 0.09375
- w_out: bfloat16 [2, 4096, 4096], P(None, 'kv', 'req'), may hold values from -0.09375 to 0.09375
- cache_keys: bfloat16 [2, 1536, 128, 1024], P(None, 'req', None, 'kv'), may hold values from -180 to 180
- cache_values: bfloat16 [2, 1536, 128, 1024], P(None, 'req', None, 'kv'), may hold values from -4 to 4
- lengths: int32 [256], replicated, may hold values from 1 to 16384, as said below
- block_owner: int32 [1536], P('req'), may hold values from 0 to 255, as said below
- block_fill: int32 [1536], P('req'), may hold values from 0 to 128
Outputs:
- hidden_out: bfloat16 [256, 4096], P(None, 'req')
- new_keys: bfloat16 [2, 256, 1024], P(None, 'req', 'kv')
- new_values: bfloat16 [2, 256, 1024], P(None, 'req', 'kv')
The draws below stay inside these ranges and needn't reach their ends.
Inputs may be any that keep to these rules, and one draw needn't show every extreme that they name: `lengths`: the longest request has 16384 cached tokens. Exactly 4 requests have more than 128 cached tokens. `block_owner`: request r owns block (r // 8) * 48 + r % 8, whose fill is above 0; its other blocks lie anywhere among the remaining blocks of the pool. The fills of the blocks owned by r sum to lengths[r], and all of them but at most one are 128. A block with fill 0 holds nothing, whatever its owner.
All inputs are finite; a program needn't handle non-finite values.
Results may differ from the reference program's by a relative error of at most 0.024.
Values may be sent and summed in bfloat16 or wider, within the bound.
A program may use at most 64 MiB of HBM per device.

```python
import math
import jax
import jax.numpy as jnp
from jax import lax

D = 4096
QH = 32
KVH = 8
HD = 128
LAYERS = 2
BLOCK = 128
REQ_DEV = 8
BLK_DEV = 48
R = 256
NBLK = 1536
MAXB = 128
LONGS = 4
GROUP = 4


def pool_layout(key):
    device_count = NBLK // BLK_DEV
    spare_slots = BLK_DEV - REQ_DEV
    extra_slots = device_count * spare_slots
    key_parts = jax.random.split(jax.random.fold_in(key, 11), 5)
    request_order = jax.random.permutation(key_parts[0], R)
    long_requests = request_order[:LONGS]
    extra_count = jax.random.randint(key_parts[1], (LONGS,), MAXB // 4, MAXB + 1)
    extra_count = extra_count.at[0].set(MAXB) - 1
    tail_fill = jax.random.randint(key_parts[2], (R,), 1, BLOCK + 1)
    tail_fill = tail_fill.at[long_requests[0]].set(BLOCK)
    counts = jnp.ones((R,), jnp.int32).at[long_requests].add(extra_count)
    lengths = (counts - 1) * BLOCK + tail_fill
    first_fill = jnp.where(counts == 1, tail_fill, BLOCK)
    piece_ends = jnp.cumsum(extra_count)
    extra_total = piece_ends[LONGS - 1]
    extra_place = jnp.arange(extra_slots, dtype=jnp.int32)
    long_slot = jnp.minimum(jnp.sum((extra_place[:, None] >= piece_ends[None, :]).astype(jnp.int32), axis=1), LONGS - 1)
    owner_long = long_requests[long_slot]
    piece_index = extra_place - (piece_ends[long_slot] - extra_count[long_slot]) + 1
    live_slot = extra_place < extra_total
    fill_long = jnp.where(piece_index == counts[owner_long] - 1, tail_fill[owner_long], BLOCK)
    stray_owner = jax.random.randint(key_parts[3], (extra_slots,), 0, R)
    owner_extra = jnp.where(live_slot, owner_long, stray_owner)
    fill_extra = jnp.where(live_slot, fill_long, 0)
    shuffle = jax.random.permutation(key_parts[4], extra_slots)
    owner_placed = jnp.zeros((extra_slots,), jnp.int32).at[shuffle].set(owner_extra)
    fill_placed = jnp.zeros((extra_slots,), jnp.int32).at[shuffle].set(fill_extra)
    home_owner = jnp.arange(R, dtype=jnp.int32).reshape(device_count, REQ_DEV)
    owner_table = jnp.concatenate([home_owner, owner_placed.reshape(device_count, spare_slots)], axis=1).reshape(NBLK)
    fill_table = jnp.concatenate([first_fill.reshape(device_count, REQ_DEV), fill_placed.reshape(device_count, spare_slots)], axis=1).reshape(NBLK)
    return (lengths.astype(jnp.int32), owner_table.astype(jnp.int32), fill_table.astype(jnp.int32))


def draw_lengths(key, part):
    return pool_layout(key)[0]


def draw_block_owner(key, part):
    return pool_layout(key)[1]


def draw_block_fill(key, part):
    return pool_layout(key)[2]


def draw_hidden_in(key, part):
    key_parts = jax.random.split(jax.random.fold_in(key, 21), 3)
    col_scale = 3.0 ** (jnp.arange(D, dtype=jnp.float32) / D)[None, :]
    col_scale = col_scale * jnp.exp(jax.random.uniform(key_parts[0], (1, D), jnp.float32, 0.0, math.log(3.3)))
    row_scale = jnp.exp(jax.random.uniform(key_parts[1], (R, 1), jnp.float32, math.log(0.3), math.log(3.0)))
    base_draw = jax.random.truncated_normal(key_parts[2], -4.0, 4.0, (R, D), jnp.float32)
    return (0.1 * base_draw * row_scale * col_scale).astype(jnp.bfloat16)


def draw_cache_keys(key, part):
    key_parts = jax.random.split(jax.random.fold_in(key, 31), 1)
    full_shape = (LAYERS, NBLK, BLOCK, KVH * HD)
    result = 2.5 * jax.random.truncated_normal(key_parts[0], -4.0, 4.0, full_shape, jnp.float32)
    return result.astype(jnp.bfloat16)


def block_scale(key, dims, cuts, smallest, high):
    level, own = 1.0, jax.random.fold_in(key, 6)
    for axis_at, blocks in cuts:
        steps = jnp.exp(jax.random.uniform(jax.random.fold_in(own, axis_at), (blocks,), jnp.float32, smallest / len(cuts), high / len(cuts)))
        level = level * jnp.repeat(steps, dims[axis_at] // blocks).reshape([-1 if axis == axis_at else 1 for axis in range(len(dims))])
    return level


def scatter_about(rng, shape, scale, bound, shards=(), kind=jnp.bfloat16):
    loudness = block_scale(rng, shape, shards, -0.22, 0.18) if shards else 1.0
    entries = jax.random.normal(rng, shape, jnp.float32) * scale * loudness
    return jnp.minimum(jnp.maximum(entries, -bound), bound).astype(kind)


def setup_inputs(seed: int = 0) -> dict:
    keys = jax.random.split(jax.random.key(seed), 14)
    hidden_in = draw_hidden_in(jax.random.fold_in(keys[13], 71), 0)
    norm_gain = jnp.clip(1.0 + 0.1 * jax.random.normal(keys[1], (LAYERS, D), jnp.float32), 0.5, 1.5).astype(jnp.bfloat16)
    q_gain = jnp.clip(1.0 + 0.15 * jax.random.normal(keys[2], (LAYERS, HD), jnp.float32), 0.25, 1.75).astype(jnp.bfloat16)
    k_gain = jnp.clip(1.0 + 0.15 * jax.random.normal(keys[3], (LAYERS, HD), jnp.float32), 0.25, 1.75).astype(jnp.bfloat16)
    w_query = scatter_about(keys[4], (LAYERS, D, QH * HD), D ** -0.5, 0.09375, ((1, 32), (2, 8)))
    w_key = scatter_about(keys[5], (LAYERS, D, KVH * HD), D ** -0.5, 0.09375, ((1, 32), (2, 8)))
    w_value = scatter_about(keys[6], (LAYERS, D, KVH * HD), D ** -0.5, 0.09375, ((1, 32), (2, 8)))
    w_out = scatter_about(keys[7], (LAYERS, QH * HD, D), (QH * HD) ** -0.5, 0.09375, ((1, 8), (2, 32)))
    cache_keys = draw_cache_keys(jax.random.fold_in(keys[13], 71), 0)
    cache_values = scatter_about(keys[9], (LAYERS, NBLK, BLOCK, KVH * HD), 1.0, 4.0, ((1, 32), (3, 8)))
    lengths = draw_lengths(jax.random.fold_in(keys[13], 71), 0)
    block_owner = draw_block_owner(jax.random.fold_in(keys[13], 71), 0)
    block_fill = draw_block_fill(jax.random.fold_in(keys[13], 71), 0)
    return {"hidden_in": hidden_in, "norm_gain": norm_gain, "q_gain": q_gain, "k_gain": k_gain, "w_query": w_query, "w_key": w_key, "w_value": w_value, "w_out": w_out, "cache_keys": cache_keys, "cache_values": cache_values, "lengths": lengths, "block_owner": block_owner, "block_fill": block_fill}


EPS = 1e-06
THETA = 1000000.0
FLOOR = -1e+30

def head_norm_rope(values, head_gain, positions, head_dim):
    row_count = values.shape[0]
    head_count = values.shape[1] // head_dim
    pieces = values.reshape(row_count, head_count, head_dim)
    pieces = pieces * lax.rsqrt(lax.optimization_barrier(jnp.mean(pieces * pieces, axis=2, keepdims=True)) + EPS) * head_gain.astype(jnp.float32)
    half_dim = head_dim // 2
    frequency = THETA ** (-(jnp.arange(half_dim, dtype=jnp.float32) * 2.0 / head_dim))
    angles = positions.astype(jnp.float32)[:, None] * frequency[None, :]
    cosine = jnp.cos(angles)[:, None, :]
    sine_part = jnp.sin(angles)[:, None, :]
    lower_half = pieces[:, :, :half_dim]
    upper_half = pieces[:, :, half_dim:]
    turned = jnp.concatenate([lower_half * cosine - upper_half * sine_part, upper_half * cosine + lower_half * sine_part], axis=2)
    return turned.reshape(row_count, head_count * head_dim).astype(jnp.bfloat16)

def attend_all(queries, new_keys, new_values, layer_keys, layer_values, block_owner, block_fill):
    logit_scale_factor = 1.0 / math.sqrt(HD)
    request_count = queries.shape[0]
    query_heads = queries.astype(jnp.float32).reshape(request_count, KVH, GROUP, HD).transpose(1, 0, 2, 3)
    key_heads = new_keys.astype(jnp.float32).reshape(request_count, KVH, HD).transpose(1, 0, 2)
    value_heads = new_values.astype(jnp.float32).reshape(request_count, KVH, HD).transpose(1, 0, 2)
    live_mask = (jnp.arange(BLOCK, dtype=jnp.int32)[None, :] < block_fill[:, None])[:, None, :]

    def one_head(packed):
        head_queries, head_key, head_value, head_index = packed
        column = (head_index * HD).astype(jnp.int32)
        paged_key_rows = lax.dynamic_slice_in_dim(layer_keys, column, HD, 2).astype(jnp.float32)
        paged_value_rows = lax.dynamic_slice_in_dim(layer_values, column, HD, 2).astype(jnp.float32)
        selected_entry = head_queries[block_owner]
        attention_logits = jnp.einsum('ayn,awn->ayw', selected_entry, paged_key_rows) * logit_scale_factor
        attention_logits = jnp.where(live_mask, attention_logits, -jnp.inf)
        block_max = jnp.maximum(lax.optimization_barrier(jnp.max(attention_logits, axis=2)), FLOOR)
        weights = jnp.where(live_mask, jnp.exp(attention_logits - block_max[:, :, None]), 0.0)
        block_den = lax.optimization_barrier(jnp.sum(weights, axis=2))
        rounded_down = lax.optimization_barrier(weights.astype(jnp.bfloat16)).astype(jnp.float32)
        block_numerator = jnp.einsum('xje,xei->xji', rounded_down, paged_value_rows)
        own_score = lax.optimization_barrier(jnp.sum(head_queries * head_key[:, None, :], axis=2)) * logit_scale_factor
        request_max = jnp.maximum(jax.ops.segment_max(block_max, block_owner, num_segments=request_count), own_score)
        factor = jnp.exp(block_max - request_max[block_owner])
        own_factor = jnp.exp(own_score - request_max)
        denom = jax.ops.segment_sum(factor * block_den, block_owner, num_segments=request_count) + own_factor
        numer = jax.ops.segment_sum(factor[:, :, None] * block_numerator, block_owner, num_segments=request_count)
        numer = numer + own_factor[:, :, None] * head_value[:, None, :]
        return numer / denom[:, :, None]
    combined = lax.map(one_head, (query_heads, key_heads, value_heads, jnp.arange(KVH, dtype=jnp.int32)))
    return combined.transpose(1, 0, 2, 3).reshape(request_count, QH * HD)

def reference(hidden_in, norm_gain, q_gain, k_gain, w_query, w_key, w_value, w_out, cache_keys, cache_values, lengths, block_owner, block_fill):
    hidden = hidden_in
    key_list = []
    value_list = []
    for layer_index in range(LAYERS):
        wide = hidden.astype(jnp.float32)
        normed = (wide * lax.rsqrt(lax.optimization_barrier(jnp.mean(wide * wide, axis=1, keepdims=True)) + EPS) * norm_gain[layer_index].astype(jnp.float32)).astype(jnp.bfloat16)
        query_raw = jnp.dot(normed, w_query[layer_index], preferred_element_type=jnp.float32)
        key_raw = jnp.dot(normed, w_key[layer_index], preferred_element_type=jnp.float32)
        value_raw = jnp.dot(normed, w_value[layer_index], preferred_element_type=jnp.float32)
        queries = head_norm_rope(query_raw, q_gain[layer_index], lengths, HD)
        new_keys = head_norm_rope(key_raw, k_gain[layer_index], lengths, HD)
        new_values = value_raw.astype(jnp.bfloat16)
        attended = attend_all(queries, new_keys, new_values, cache_keys[layer_index], cache_values[layer_index], block_owner, block_fill).astype(jnp.bfloat16)
        branch = jnp.dot(attended, w_out[layer_index], preferred_element_type=jnp.float32)
        hidden = (wide + branch).astype(jnp.bfloat16)
        key_list.append(new_keys)
        value_list.append(new_values)
    return (hidden, jnp.stack(key_list), jnp.stack(value_list))
```

```python
import functools
import math

import jax
import jax.numpy as jnp
import numpy as np
from jax import lax
from jax.experimental import pallas as pl
from jax.experimental.pallas import tpu as pltpu
from jax.sharding import PartitionSpec as P

LAYERS = 2
EPS = 1e-06
THETA = 1000000.0
FLOOR = -1e30
CEIL = -1e29
TINY = 1e-30
MESH = pl.DeviceIdType.MESH
F32 = jnp.float32
BF16 = jnp.bfloat16

RS, SQ, QX, PX, HO, LO, LL, ZR, ZA, ZB = range(10)


def dot(a, b):
    return jnp.dot(a, b, preferred_element_type=F32)


def dot_nt(a, b):
    return lax.dot_general(a, b, (((1,), (1,)), ((), ())), preferred_element_type=F32)


def iota(shape, dim):
    return lax.broadcasted_iota(jnp.int32, shape, dim)


def kernel(
    n_chip,
    side,
    nz,
    width,
    x_in, norm_gain, q_gain, k_gain, w_query, w_key, w_value, w_out,
    cache_keys, cache_values, lengths, block_owner, block_fill, frequency,
    out, out_keys, out_values,
    x_own, x_sib, gains, q_gains, k_gains, wq, wk, wv, wo, keys, values,
    lens, owner, fill, freq,
    x_half, long_bias, home_bias, turn_cos, turn_sin, pick, spread,
    rs_s, rs_r, sq_s, sq_r, qx_s, qx_r, px_s, px_r,
    ho_s, ho_r, lo_s, lo_r, ll_s, ll_r, zr_s, zr_r, za_s, fin_s, fin_r,
    load_sem, init_send, init_recv, send_sem, recv_sem,
):
    half = 8 * n_chip
    part = half // nz
    blocks = cache_keys.shape[1]
    total = lens.shape[1]
    me = lax.axis_index("req")
    my_z = lax.axis_index("kv")
    core = me % 2
    chip = me // 2
    chip_x, chip_y = chip // side, chip % side
    sib = me + 1 - 2 * core

    def peer(t):
        px = (chip_x + t // side) % side
        py = (chip_y + t % side) % side
        return (px * side + py) * 2 + core

    def chip_of(t):
        px = (chip_x + t // side) % side
        py = (chip_y + t % side) % side
        return px * side + py

    barrier = pltpu.get_barrier_semaphore()

    def greet(req, kv):
        pl.semaphore_signal(
            barrier, inc=1, device_id={"req": req, "kv": kv}, device_id_type=MESH
        )

    def greet_chip(t, carry):
        greet(peer(t), my_z)
        return carry

    def greet_z(t, carry):
        greet(me, (my_z + t) % nz)
        greet(sib, (my_z + t) % nz)
        return carry

    lax.fori_loop(1, n_chip, greet_chip, 0)
    lax.fori_loop(1, nz, greet_z, 0)
    greet(sib, my_z)

    loads = [
        pltpu.make_async_copy(src, dst, load_sem.at[at])
        for at, (src, dst) in enumerate(
            [
                (lengths, lens),
                (frequency, freq),
                (norm_gain, gains.at[:, pl.ds(0, 128)]),
                (q_gain, q_gains),
                (k_gain, k_gains),
                (x_in, x_own),
                (w_query, wq.at[:, pl.ds(0, 128)]),
                (w_key, wk.at[:, pl.ds(0, 128)]),
                (w_value, wv.at[:, pl.ds(0, 128)]),
                (block_owner, owner),
                (block_fill, fill),
                (cache_keys.at[0], keys.at[0, pl.ds(0, blocks)]),
                (cache_values.at[0], values.at[0, pl.ds(0, blocks)]),
                (w_out, wo.at[:, 0]),
                (cache_keys.at[1], keys.at[1, pl.ds(0, blocks)]),
                (cache_values.at[1], values.at[1, pl.ds(0, blocks)]),
            ]
        )
    ]
    for copy in loads:
        copy.start()

    loads[0].wait()
    loads[1].wait()
    length_row = lens[...].astype(F32)
    request_row = iota((8, total), 1).astype(F32)
    is_long = jnp.where(length_row > 128.0, 1.0, 0.0)
    before = jnp.where(iota((total, total), 0) < iota((total, total), 1), 1.0, 0.0).astype(BF16)
    rank = dot(jnp.broadcast_to(is_long, (8, total)).astype(BF16), before)
    slot8 = iota((8, total), 0)
    long_hot = jnp.where(
        (rank.astype(jnp.int32) == slot8) & (slot8 < 4),
        jnp.broadcast_to(is_long, (8, total)),
        0.0,
    )
    own_hot = jnp.where(iota((8, total), 1) == 8 * me + slot8, 1.0, 0.0)
    long_id = jnp.sum(long_hot * request_row, axis=1, keepdims=True)
    long_at = jnp.sum(long_hot * length_row, axis=1, keepdims=True)
    own_at = jnp.sum(own_hot * length_row, axis=1, keepdims=True)
    own_keep = jnp.where(own_at > 128.0, 0.0, 1.0)
    row_of = iota((total, 128), 1)
    to_half = jnp.where(
        (iota((total, 128), 0) == (row_of // 8) * 16 + 8 * core + row_of % 8) & (row_of < half),
        1.0,
        0.0,
    ).astype(BF16)
    long_half = dot(long_hot.astype(BF16), to_half)
    own_half = jnp.where(iota((8, 128), 1) == 8 * chip + iota((8, 128), 0), 1.0, 0.0)
    pick[...] = jnp.concatenate([own_half, long_half], axis=0)
    four = jnp.where(iota((8, 128), 0) < 4, long_half, pltpu.roll(long_half, 4, 0))
    eye = jnp.where(iota((half, 128), 0) == iota((half, 128), 1), 1.0, 0.0)
    spread[...] = dot_nt(
        eye.astype(BF16), jnp.concatenate([four, four], axis=0).astype(BF16)
    ).astype(BF16)
    long_sel = jnp.concatenate([long_half, jnp.zeros((8, 128), F32)], axis=0).astype(BF16)
    long_sel = long_sel[:, :half]
    angle = jnp.concatenate([own_at, long_at], axis=0) * freq[...]
    turn_cos[...] = jnp.cos(angle)
    turn_sin[...] = jnp.where(iota((16, 128), 1) < 64, -jnp.sin(angle), jnp.sin(angle))

    def half_of(ref):
        rows = ref[...].astype(F32).reshape(n_chip, 2, 8, 128)
        return jnp.where(core == 0, rows[:, 0], rows[:, 1]).reshape(half, 128)

    loads[5].wait()
    x_first = half_of(x_own)

    pl.semaphore_wait(barrier, n_chip - 1 + 2 * (nz - 1) + 1)

    def remote(src, dst, send, recv, req, kv):
        return pltpu.make_async_remote_copy(
            src_ref=src,
            dst_ref=dst,
            send_sem=send,
            recv_sem=recv,
            device_id={"req": req, "kv": kv},
            device_id_type=MESH,
        )

    shares = [
        remote(src, dst, init_send.at[at], init_recv.at[at], sib, my_z)
        for at, (src, dst) in enumerate(
            [
                (x_in, x_sib),
                (norm_gain, gains.at[:, pl.ds(128, 128)]),
                (w_query.at[0], wq.at[0, pl.ds(128, 128)]),
                (w_key.at[0], wk.at[0, pl.ds(128, 128)]),
                (w_value.at[0], wv.at[0, pl.ds(128, 128)]),
                (w_out.at[0], wo.at[0, 1]),
                (w_query.at[1], wq.at[1, pl.ds(128, 128)]),
                (w_key.at[1], wk.at[1, pl.ds(128, 128)]),
                (w_value.at[1], wv.at[1, pl.ds(128, 128)]),
                (w_out.at[1], wo.at[1, 1]),
            ]
        )
    ]
    for copy in shares:
        copy.start()

    for at in (2, 3, 4, 6, 7, 8):
        loads[at].wait()
    shares[0].wait_recv()
    shares[1].wait_recv()
    x_half[0] = (
        jnp.concatenate([x_first, half_of(x_sib)], axis=1).astype(BF16).reshape(nz, part, 256)
    )
    for at in (2, 3, 4):
        shares[at].wait_recv()

    def normed_turned(t, scale, gain, cos, sin):
        t = t * scale
        t = t * lax.rsqrt(jnp.mean(t * t, axis=1, keepdims=True) + EPS) * gain
        return t * cos + pltpu.roll(t, 64, 1) * sin

    def arrived(ref, sem):
        pltpu.make_async_copy(ref, ref, sem).wait()

    def to_chips(pairs, layer):
        def step(t, carry):
            req = peer(t)
            for src, dst, phase in pairs(chip_of(t)):
                remote(
                    src, dst, send_sem.at[layer, phase], recv_sem.at[layer, phase], req, my_z
                ).start()
            return carry

        lax.fori_loop(1, n_chip, step, 0)

    logit = 1.0 / math.sqrt(128)
    others = pl.ds(0, n_chip - 1)
    row16 = iota((16, 128), 0)
    lane16 = iota((16, 128), 1)
    sub8 = iota((8, 128), 0)

    for layer in range(LAYERS):
        x = x_half[layer].reshape(half, 256).astype(F32)
        square = jnp.sum(x * x, axis=1, keepdims=True)
        square_row = jnp.sum(jnp.where(eye > 0.0, square, 0.0), axis=0, keepdims=True)
        sq_s[layer] = square_row
        sq_r[layer, chip] = square_row
        xg = (x * gains[pl.ds(layer, 1), :].astype(F32)).astype(BF16)
        xl = dot(long_sel, xg).astype(BF16)
        if layer == 1:
            for at in (6, 7, 8):
                shares[at].wait_recv()
        q = dot(xg, wq[layer])
        q_long = dot(xl, wq[layer])[0:8]
        kv = jnp.concatenate([dot(xg, wk[layer]), dot(xg, wv[layer])], axis=1)
        low = jnp.concatenate([pltpu.roll(kv, 4, 0), kv], axis=1).reshape(n_chip, 8, 512)
        low = jnp.where(
            iota((n_chip, 8, 512), 1) < 4,
            jnp.broadcast_to(q_long[None], (n_chip, 8, 512)),
            low,
        )
        message = jnp.concatenate([q.reshape(n_chip, 8, 512), low], axis=1).astype(BF16)
        rs_s[layer] = message
        to_chips(
            lambda to: [
                (rs_s.at[layer, to], rs_r.at[layer, chip], RS),
                (sq_s.at[layer], sq_r.at[layer, chip], SQ),
            ],
            layer,
        )
        rs_r[layer, chip] = rs_s[layer, chip]

        if layer == 0:
            loads[9].wait()
            loads[10].wait()
            lane8 = iota((8, 128), 1)

            def block_masks(b, carry):
                live = (lane8 < fill[b]) & (long_id == owner[b].astype(F32)) & (sub8 < 4)
                bias = jnp.where(live, 0.0, FLOOR)
                long_bias[:, pl.ds(pl.multiple_of(b * 128, 128), 128)] = jnp.where(
                    sub8 < 4, bias, pltpu.roll(bias, 4, 0)
                )
                return carry

            lax.fori_loop(0, blocks, block_masks, 0)
            live = (long_id == (8 * me + lane8).astype(F32)) & (lane8 < 8) & (sub8 < 4)
            bias = jnp.where(live, 0.0, FLOOR)
            long_bias[:, pl.ds(blocks * 128, 128)] = jnp.where(
                sub8 < 4, bias, pltpu.roll(bias, 4, 0)
            )
            for b in range(8):
                home_bias[:, pl.ds(b * 128, 128)] = jnp.where(
                    (sub8 == b) & (lane8 < fill[b]), 0.0, FLOOR
                )
            home_bias[:, pl.ds(1024, 128)] = jnp.where(sub8 == lane8, 0.0, FLOOR)
            zero = jnp.zeros((LAYERS, 128, 128), BF16)
            keys[:, blocks] = zero
            values[:, blocks] = zero
            loads[11].wait()
            loads[12].wait()
        else:
            loads[14].wait()
            loads[15].wait()

        arrived(sq_r.at[layer, others], recv_sem.at[layer, SQ])
        arrived(rs_r.at[layer, others], recv_sem.at[layer, RS])
        square_all = jnp.sum(sq_r[layer], axis=0)
        scale = lax.rsqrt(
            jnp.sum(pick[...] * square_all, axis=1, keepdims=True) / width + EPS
        )
        sums = jnp.sum(rs_r[layer].astype(F32), axis=0)
        q_gain_row = q_gains[pl.ds(layer, 1), :].astype(F32)
        turned = [
            normed_turned(
                sums[:, 128 * g : 128 * g + 128], scale, q_gain_row, turn_cos[...], turn_sin[...]
            )
            for g in range(4)
        ]
        q_far = [t[8:16] for t in turned]
        q_far = jnp.concatenate(
            [
                jnp.where(sub8 < 4, q_far[0], pltpu.roll(q_far[1], 4, 0)),
                jnp.where(sub8 < 4, q_far[2], pltpu.roll(q_far[3], 4, 0)),
            ],
            axis=0,
        ).astype(BF16)
        qx_s[layer] = q_far
        q_share = remote(
            qx_s.at[layer], qx_r.at[layer], send_sem.at[layer, QX], recv_sem.at[layer, QX],
            sib, my_z,
        )
        q_share.start()

        q_own = jnp.concatenate([t[0:8] for t in turned], axis=0).astype(BF16)
        low = sums[8:16]
        kv = jnp.where(iota((8, 256), 0) < 4, pltpu.roll(low[:, 0:256], 4, 0), low[:, 256:512])
        new_key = normed_turned(
            kv[:, 0:128],
            scale[0:8],
            k_gains[pl.ds(layer, 1), :].astype(F32),
            turn_cos[0:8, :],
            turn_sin[0:8, :],
        )
        new_value = kv[:, 128:256] * scale[0:8]
        out_keys[layer] = new_key.astype(BF16)
        out_values[layer] = new_value.astype(BF16)
        pad = jnp.zeros((8, 128), F32)
        keys[layer, blocks, 0:16] = jnp.concatenate([new_key, pad], axis=0).astype(BF16)
        values[layer, blocks, 0:16] = jnp.concatenate([new_value, pad], axis=0).astype(BF16)

        s = jnp.concatenate(
            [
                dot_nt(q_own, keys[layer, 0:8].reshape(1024, 128)),
                dot_nt(q_own, keys[layer, blocks]),
            ],
            axis=1,
        )
        s = s * logit + jnp.concatenate([home_bias[...]] * 4, axis=0)
        p = jnp.exp(s - jnp.max(s, axis=1, keepdims=True))
        den = jnp.sum(p, axis=1, keepdims=True)
        p = p.astype(BF16)
        num = dot(p[:, 0:1024], values[layer, 0:8].reshape(1024, 128)) + dot(
            p[:, 1024:1152], values[layer, blocks]
        )
        attended = (num * (jnp.concatenate([own_keep] * 4, axis=0) / den)).astype(BF16)
        ho_s[layer] = attended
        ho_r[layer, chip] = attended
        to_chips(lambda to: [(ho_s.at[layer], ho_r.at[layer, chip], HO)], layer)

        q_share.wait_recv()
        q_all = q_far + qx_r[layer]
        s = dot_nt(q_all, keys[layer].reshape((blocks + 1) * 128, 128))
        s = s * logit + jnp.concatenate([long_bias[...]] * 2, axis=0)
        top = jnp.maximum(jnp.max(s, axis=1, keepdims=True), CEIL)
        p = jnp.exp(s - top)
        den = jnp.sum(p, axis=1, keepdims=True)
        num = dot(p.astype(BF16), values[layer].reshape((blocks + 1) * 128, 128))
        level = jnp.where(den > 0.0, top + jnp.log(jnp.maximum(den, TINY)), FLOOR)
        level = jnp.broadcast_to(level, (16, 128))
        mean = num / jnp.maximum(den, TINY)
        px_s[layer] = jnp.concatenate([mean, level], axis=0)
        p_share = remote(
            px_s.at[layer], px_r.at[layer], send_sem.at[layer, PX], recv_sem.at[layer, PX],
            sib, my_z,
        )
        p_share.start()
        p_share.wait_recv()
        other_mean, other_level = px_r[layer, 0:16], px_r[layer, 16:32]
        top = jnp.maximum(level, other_level)
        mine, theirs = jnp.exp(level - top), jnp.exp(other_level - top)
        both = mine + theirs
        mean = ((mean * mine + other_mean * theirs) / both).astype(BF16)
        level = top + jnp.log(both)
        level_row = jnp.sum(jnp.where(row16 == lane16, level, 0.0), axis=0, keepdims=True)
        lo_s[layer] = mean
        lo_r[layer, chip] = mean
        ll_s[layer] = level_row
        ll_r[layer, chip] = level_row
        to_chips(
            lambda to: [
                (lo_s.at[layer], lo_r.at[layer, chip], LO),
                (ll_s.at[layer], ll_r.at[layer, chip], LL),
            ],
            layer,
        )

        if layer == 0:
            loads[13].wait()
        shares[5 if layer == 0 else 9].wait_recv()
        arrived(ho_r.at[layer, others], recv_sem.at[layer, HO])
        homes = ho_r[layer].astype(F32)
        homes = jnp.concatenate(
            [homes[:, 8 * g : 8 * g + 8].reshape(half, 128) for g in range(4)], axis=1
        )
        arrived(ll_r.at[layer, others], recv_sem.at[layer, LL])
        arrived(lo_r.at[layer, others], recv_sem.at[layer, LO])
        levels = ll_r[layer]
        weight = jnp.exp(levels - jnp.max(levels, axis=0, keepdims=True))
        weight = weight / jnp.sum(weight, axis=0, keepdims=True)
        weight = jnp.sum(
            jnp.where(
                iota((n_chip, 16, 128), 1) == iota((n_chip, 16, 128), 2),
                jnp.broadcast_to(weight, (n_chip, 16, 128)),
                0.0,
            ),
            axis=2,
            keepdims=True,
        )
        merged = jnp.sum(weight * lo_r[layer].astype(F32), axis=0)
        merged = jnp.concatenate(
            [jnp.where(row16 // 4 == g, merged, 0.0) for g in range(4)], axis=1
        ).astype(BF16)
        attended = (homes + dot(spread[...], merged)).astype(BF16)

        branch = jnp.concatenate(
            [dot(attended, wo[layer, 0]), dot(attended, wo[layer, 1])], axis=1
        )
        zr_s[layer] = branch.astype(BF16).reshape(nz, part, 256)

        def reduce_z(t, carry):
            to = (my_z + t) % nz
            remote(
                zr_s.at[layer, to], zr_r.at[layer, my_z],
                send_sem.at[layer, ZR], recv_sem.at[layer, ZR], me, to,
            ).start()
            return carry

        lax.fori_loop(1, nz, reduce_z, 0)
        zr_r[layer, my_z] = zr_s[layer, my_z]
        arrived(zr_r.at[layer, pl.ds(0, nz - 1)], recv_sem.at[layer, ZR])
        hidden = (
            x_half[layer, my_z].astype(F32) + jnp.sum(zr_r[layer].astype(F32), axis=0)
        ).astype(BF16)

        if layer + 1 < LAYERS:
            za_s[...] = hidden
            x_half[layer + 1, my_z] = hidden

            def gather_z(t, carry):
                to = (my_z + t) % nz
                remote(
                    za_s, x_half.at[layer + 1, my_z],
                    send_sem.at[layer, ZA], recv_sem.at[layer, ZA], me, to,
                ).start()
                return carry

            lax.fori_loop(1, nz, gather_z, 0)
            arrived(x_half.at[layer + 1, pl.ds(0, nz - 1)], recv_sem.at[layer, ZA])
        else:
            mine, theirs = hidden[:, 0:128], hidden[:, 128:256]
            fin_s[0] = mine
            fin_s[1] = theirs
            fin_r[0, my_z] = mine

            def finish_z(t, carry):
                to = (my_z + t) % nz
                remote(
                    fin_s.at[1], fin_r.at[1, my_z],
                    send_sem.at[layer, ZB], recv_sem.at[layer, ZB], sib, to,
                ).start()
                remote(
                    fin_s.at[0], fin_r.at[0, my_z],
                    send_sem.at[layer, ZA], recv_sem.at[layer, ZA], me, to,
                ).start()
                return carry

            lax.fori_loop(1, nz, finish_z, 0)
            remote(
                fin_s.at[1], fin_r.at[1, my_z],
                send_sem.at[layer, ZB], recv_sem.at[layer, ZB], sib, my_z,
            ).start()
            arrived(fin_r.at[0, pl.ds(0, nz - 1)], recv_sem.at[layer, ZA])
            arrived(fin_r.at[1], recv_sem.at[layer, ZB])
            near = fin_r[0].astype(F32).reshape(n_chip, 8, 128)
            far = fin_r[1].astype(F32).reshape(n_chip, 8, 128)
            out[...] = (
                jnp.concatenate(
                    [jnp.where(core == 0, near, far), jnp.where(core == 0, far, near)], axis=1
                )
                .reshape(total, 128)
                .astype(BF16)
            )

    for copy in shares:
        copy.wait_send()
    for layer in range(LAYERS):
        for ref, phase in (
            (rs_r.at[layer, others], RS),
            (sq_r.at[layer, others], SQ),
            (qx_r.at[layer], QX),
            (px_r.at[layer], PX),
            (ho_r.at[layer, others], HO),
            (lo_r.at[layer, others], LO),
            (ll_r.at[layer, others], LL),
            (zr_r.at[layer, pl.ds(0, nz - 1)], ZR),
        ):
            arrived(ref, send_sem.at[layer, phase])
        if layer + 1 < LAYERS:
            arrived(x_half.at[layer + 1, pl.ds(0, nz - 1)], send_sem.at[layer, ZA])
        else:
            arrived(fin_r.at[0, pl.ds(0, nz - 1)], send_sem.at[layer, ZA])
            arrived(fin_r.at[1], send_sem.at[layer, ZB])


def on_device(
    n_chip, side, nz, width,
    hidden_in, norm_gain, q_gain, k_gain, w_query, w_key, w_value, w_out,
    cache_keys, cache_values, lengths, block_owner, block_fill,
):
    half = 8 * n_chip
    part = half // nz
    blocks = cache_keys.shape[1]
    total = hidden_in.shape[0]
    heads = w_query.shape[2]
    exponent = np.concatenate([np.arange(64), np.arange(64)]) * 2.0 / 128
    frequency = jnp.asarray((THETA**-exponent).astype(np.float32)[None, :])
    vmem, sem = pltpu.VMEM, pltpu.SemaphoreType.DMA
    anywhere = pl.BlockSpec(memory_space=pl.ANY)
    onchip = pl.BlockSpec(memory_space=pltpu.VMEM)
    both = (LAYERS, n_chip)
    return pl.pallas_call(
        functools.partial(kernel, n_chip, side, nz, float(width)),
        out_shape=(
            jax.ShapeDtypeStruct((total, 128), BF16),
            jax.ShapeDtypeStruct((LAYERS, 8, 128), BF16),
            jax.ShapeDtypeStruct((LAYERS, 8, 128), BF16),
        ),
        in_specs=[anywhere] * 14,
        out_specs=(onchip, onchip, onchip),
        scratch_shapes=[
            vmem((total, 128), BF16),
            vmem((total, 128), BF16),
            vmem((LAYERS, 256), BF16),
            vmem((LAYERS, 128), BF16),
            vmem((LAYERS, 128), BF16),
            vmem((LAYERS, 256, heads), BF16),
            vmem((LAYERS, 256, 128), BF16),
            vmem((LAYERS, 256, 128), BF16),
            vmem((LAYERS, 2, heads, 128), BF16),
            vmem((LAYERS, blocks + 1, 128, 128), BF16),
            vmem((LAYERS, blocks + 1, 128, 128), BF16),
            vmem((1, total), jnp.int32),
            pltpu.SMEM((blocks,), jnp.int32),
            pltpu.SMEM((blocks,), jnp.int32),
            vmem((1, 128), F32),
            vmem((LAYERS, nz, part, 256), BF16),
            vmem((8, (blocks + 1) * 128), F32),
            vmem((8, 9 * 128), F32),
            vmem((16, 128), F32),
            vmem((16, 128), F32),
            vmem((16, 128), F32),
            vmem((half, 16), BF16),
            vmem((*both, 16, 512), BF16),
            vmem((*both, 16, 512), BF16),
            vmem((LAYERS, 1, 128), F32),
            vmem((*both, 1, 128), F32),
            vmem((LAYERS, 16, 128), BF16),
            vmem((LAYERS, 16, 128), BF16),
            vmem((LAYERS, 32, 128), F32),
            vmem((LAYERS, 32, 128), F32),
            vmem((LAYERS, 32, 128), BF16),
            vmem((*both, 32, 128), BF16),
            vmem((LAYERS, 16, 128), BF16),
            vmem((*both, 16, 128), BF16),
            vmem((LAYERS, 1, 128), F32),
            vmem((*both, 1, 128), F32),
            vmem((LAYERS, nz, part, 256), BF16),
            vmem((LAYERS, nz, part, 256), BF16),
            vmem((part, 256), BF16),
            vmem((2, part, 128), BF16),
            vmem((2, nz, part, 128), BF16),
            sem((16,)),
            sem((10,)),
            sem((10,)),
            sem((LAYERS, 10)),
            sem((LAYERS, 10)),
        ],
        compiler_params=pltpu.CompilerParams(
            collective_id=0, has_side_effects=True, vmem_limit_bytes=48 * 1024 * 1024
        ),
        name="attention_layers",
    )(
        hidden_in, norm_gain, q_gain, k_gain, w_query, w_key, w_value, w_out,
        cache_keys, cache_values, lengths.reshape(1, total), block_owner, block_fill, frequency,
    )


def solution(mesh):
    n_req, nz = mesh.shape["req"], mesh.shape["kv"]
    n_chip = n_req // 2
    side = math.isqrt(n_chip)
    in_specs = (
        P(None, "req"),
        P(None, "req"),
        P(),
        P(),
        P(None, "req", "kv"),
        P(None, "req", "kv"),
        P(None, "req", "kv"),
        P(None, "kv", "req"),
        P(None, "req", None, "kv"),
        P(None, "req", None, "kv"),
        P(),
        P("req"),
        P("req"),
    )
    out_specs = (P(None, "req"), P(None, "req", "kv"), P(None, "req", "kv"))
    return jax.shard_map(
        functools.partial(on_device, n_chip, side, nz, 128 * n_req),
        mesh=mesh,
        in_specs=in_specs,
        out_specs=out_specs,
        check_vma=False,
    )
```

```python
import functools
import math

import jax
import jax.numpy as jnp
import numpy as np
from jax import lax
from jax.experimental import pallas as pl
from jax.experimental.pallas import tpu as pltpu
from jax.sharding import PartitionSpec as P

LAYERS = 2
EPS = 1e-06
THETA = 1000000.0
FLOOR = -1e30
CEIL = -1e29
TINY = 1e-30
MESH = pl.DeviceIdType.MESH
F32 = jnp.float32
BF16 = jnp.bfloat16

RS, SQ, QX, PX, HO, LO, LL, ZR, ZA, ZB = range(10)


def dot(a, b):
    return jnp.dot(a, b, preferred_element_type=F32)


def dot_nt(a, b):
    return lax.dot_general(a, b, (((1,), (1,)), ((), ())), preferred_element_type=F32)


def iota(shape, dim):
    return lax.broadcasted_iota(jnp.int32, shape, dim)


def kernel(
    n_chip,
    side,
    nz,
    width,
    x_in, norm_gain, q_gain, k_gain, w_query, w_key, w_value, w_out,
    cache_keys, cache_values, lengths, block_owner, block_fill, frequency,
    out, out_keys, out_values,
    x_own, x_sib, gains, q_gains, k_gains, wq, wk, wv, wo, keys, values,
    lens, owner, fill, freq,
    x_half, long_bias, home_bias, turn_cos, turn_sin, pick, spread,
    rs_s, rs_r, sq_s, sq_r, qx_s, qx_r, px_s, px_r,
    ho_s, ho_r, lo_s, lo_r, ll_s, ll_r, zr_s, zr_r, za_s, fin_s, fin_r,
    load_sem, init_send, init_recv, send_sem, recv_sem,
):
    half = 8 * n_chip
    part = half // nz
    blocks = cache_keys.shape[1]
    total = lens.shape[1]
    me = lax.axis_index("req")
    my_z = lax.axis_index("kv")
    core = me % 2
    chip = me // 2
    chip_x, chip_y = chip // side, chip % side
    sib = me + 1 - 2 * core

    def peer(t):
        px = (chip_x + t // side) % side
        py = (chip_y + t % side) % side
        return (px * side + py) * 2 + core

    def chip_of(t):
        px = (chip_x + t // side) % side
        py = (chip_y + t % side) % side
        return px * side + py

    barrier = pltpu.get_barrier_semaphore()

    def greet(req, kv):
        pl.semaphore_signal(
            barrier, inc=1, device_id={"req": req, "kv": kv}, device_id_type=MESH
        )

    def greet_chip(t, carry):
        greet(peer(t), my_z)
        return carry

    def greet_z(t, carry):
        greet(me, (my_z + t) % nz)
        greet(sib, (my_z + t) % nz)
        return carry

    lax.fori_loop(1, n_chip, greet_chip, 0)
    lax.fori_loop(1, nz, greet_z, 0)
    greet(sib, my_z)

    loads = [
        pltpu.make_async_copy(src, dst, load_sem.at[at])
        for at, (src, dst) in enumerate(
            [
                (lengths, lens),
                (frequency, freq),
                (norm_gain, gains.at[:, pl.ds(0, 128)]),
                (q_gain, q_gains),
                (k_gain, k_gains),
                (x_in, x_own),
                (w_query, wq.at[:, pl.ds(0, 128)]),
                (w_key, wk.at[:, pl.ds(0, 128)]),
                (w_value, wv.at[:, pl.ds(0, 128)]),
                (block_owner, owner),
                (block_fill, fill),
                (cache_keys.at[0], keys.at[0, pl.ds(0, blocks)]),
                (cache_values.at[0], values.at[0, pl.ds(0, blocks)]),
                (w_out, wo.at[:, 0]),
                (cache_keys.at[1], keys.at[1, pl.ds(0, blocks)]),
                (cache_values.at[1], values.at[1, pl.ds(0, blocks)]),
            ]
        )
    ]
    for copy in loads:
        copy.start()

    loads[0].wait()
    loads[1].wait()
    length_row = lens[...].astype(F32)
    request_row = iota((8, total), 1).astype(F32)
    is_long = jnp.where(length_row > 128.0, 1.0, 0.0)
    before = jnp.where(iota((total, total), 0) < iota((total, total), 1), 1.0, 0.0).astype(BF16)
    rank = dot(jnp.broadcast_to(is_long, (8, total)).astype(BF16), before)
    slot8 = iota((8, total), 0)
    long_hot = jnp.where(
        (rank.astype(jnp.int32) == slot8) & (slot8 < 4),
        jnp.broadcast_to(is_long, (8, total)),
        0.0,
    )
    own_hot = jnp.where(iota((8, total), 1) == 8 * me + slot8, 1.0, 0.0)
    long_id = jnp.sum(long_hot * request_row, axis=1, keepdims=True)
    long_at = jnp.sum(long_hot * length_row, axis=1, keepdims=True)
    own_at = jnp.sum(own_hot * length_row, axis=1, keepdims=True)
    own_keep = jnp.where(own_at > 128.0, 0.0, 1.0)
    row_of = iota((total, 128), 1)
    to_half = jnp.where(
        (iota((total, 128), 0) == (row_of // 8) * 16 + 8 * core + row_of % 8) & (row_of < half),
        1.0,
        0.0,
    ).astype(BF16)
    long_half = dot(long_hot.astype(BF16), to_half)
    own_half = jnp.where(iota((8, 128), 1) == 8 * chip + iota((8, 128), 0), 1.0, 0.0)
    pick[...] = jnp.concatenate([own_half, long_half], axis=0)
    four = jnp.where(iota((8, 128), 0) < 4, long_half, pltpu.roll(long_half, 4, 0))
    eye = jnp.where(iota((half, 128), 0) == iota((half, 128), 1), 1.0, 0.0)
    spread[...] = dot_nt(
        eye.astype(BF16), jnp.concatenate([four, four], axis=0).astype(BF16)
    ).astype(BF16)
    long_sel = jnp.concatenate([long_half, jnp.zeros((8, 128), F32)], axis=0).astype(BF16)
    long_sel = long_sel[:, :half]
    angle = jnp.concatenate([own_at, long_at], axis=0) * freq[...]
    turn_cos[...] = jnp.cos(angle)
    turn_sin[...] = jnp.where(iota((16, 128), 1) < 64, -jnp.sin(angle), jnp.sin(angle))

    def half_of(ref):
        rows = ref[...].astype(F32).reshape(n_chip, 2, 8, 128)
        return jnp.where(core == 0, rows[:, 0], rows[:, 1]).reshape(half, 128)

    loads[5].wait()
    x_first = half_of(x_own)

    pl.semaphore_wait(barrier, n_chip - 1 + 2 * (nz - 1) + 1)

    def remote(src, dst, send, recv, req, kv):
        return pltpu.make_async_remote_copy(
            src_ref=src,
            dst_ref=dst,
            send_sem=send,
            recv_sem=recv,
            device_id={"req": req, "kv": kv},
            device_id_type=MESH,
        )

    shares = [
        remote(src, dst, init_send.at[at], init_recv.at[at], sib, my_z)
        for at, (src, dst) in enumerate(
            [
                (x_in, x_sib),
                (norm_gain, gains.at[:, pl.ds(128, 128)]),
                (w_query.at[0], wq.at[0, pl.ds(128, 128)]),
                (w_key.at[0], wk.at[0, pl.ds(128, 128)]),
                (w_value.at[0], wv.at[0, pl.ds(128, 128)]),
                (w_out.at[0], wo.at[0, 1]),
                (w_query.at[1], wq.at[1, pl.ds(128, 128)]),
                (w_key.at[1], wk.at[1, pl.ds(128, 128)]),
                (w_value.at[1], wv.at[1, pl.ds(128, 128)]),
                (w_out.at[1], wo.at[1, 1]),
            ]
        )
    ]
    for copy in shares:
        copy.start()

    for at in (2, 3, 4, 6, 7, 8):
        loads[at].wait()
    shares[0].wait_recv()
    shares[1].wait_recv()
    x_half[0] = (
        jnp.concatenate([x_first, half_of(x_sib)], axis=1).astype(BF16).reshape(nz, part, 256)
    )
    for at in (2, 3, 4):
        shares[at].wait_recv()

    def normed_turned(t, scale, gain, cos, sin):
        t = t * scale
        t = t * lax.rsqrt(jnp.mean(t * t, axis=1, keepdims=True) + EPS) * gain
        return t * cos + pltpu.roll(t, 64, 1) * sin

    def arrived(ref, sem):
        pltpu.make_async_copy(ref, ref, sem).wait()

    def to_chips(pairs, layer):
        def step(t, carry):
            req = peer(t)
            for src, dst, phase in pairs(chip_of(t)):
                remote(
                    src, dst, send_sem.at[layer, phase], recv_sem.at[layer, phase], req, my_z
                ).start()
            return carry

        lax.fori_loop(1, n_chip, step, 0)

    logit = 1.0 / math.sqrt(128)
    others = pl.ds(0, n_chip - 1)
    row16 = iota((16, 128), 0)
    lane16 = iota((16, 128), 1)
    sub8 = iota((8, 128), 0)

    for layer in range(LAYERS):
        x = x_half[layer].reshape(half, 256).astype(F32)
        square = jnp.sum(x * x, axis=1, keepdims=True)
        square_row = jnp.sum(jnp.where(eye > 0.0, square, 0.0), axis=0, keepdims=True)
        sq_s[layer] = square_row
        sq_r[layer, chip] = square_row
        xg = (x * gains[pl.ds(layer, 1), :].astype(F32)).astype(BF16)
        xl = dot(long_sel, xg).astype(BF16)
        if layer == 1:
            for at in (6, 7, 8):
                shares[at].wait_recv()
        q = dot(xg, wq[layer])
        q_long = dot(xl, wq[layer])[0:8]
        kv = jnp.concatenate([dot(xg, wk[layer]), dot(xg, wv[layer])], axis=1)
        low = jnp.concatenate([pltpu.roll(kv, 4, 0), kv], axis=1).reshape(n_chip, 8, 512)
        low = jnp.where(
            iota((n_chip, 8, 512), 1) < 4,
            jnp.broadcast_to(q_long[None], (n_chip, 8, 512)),
            low,
        )
        message = jnp.concatenate([q.reshape(n_chip, 8, 512), low], axis=1).astype(BF16)
        rs_s[layer] = message
        to_chips(
            lambda to: [
                (rs_s.at[layer, to], rs_r.at[layer, chip], RS),
                (sq_s.at[layer], sq_r.at[layer, chip], SQ),
            ],
            layer,
        )
        rs_r[layer, chip] = rs_s[layer, chip]

        if layer == 0:
            loads[9].wait()
            loads[10].wait()
            lane8 = iota((8, 128), 1)

            def block_masks(b, carry):
                live = (lane8 < fill[b]) & (long_id == owner[b].astype(F32)) & (sub8 < 4)
                bias = jnp.where(live, 0.0, FLOOR)
                long_bias[:, pl.ds(pl.multiple_of(b * 128, 128), 128)] = jnp.where(
                    sub8 < 4, bias, pltpu.roll(bias, 4, 0)
                )
                return carry

            lax.fori_loop(0, blocks, block_masks, 0)
            live = (long_id == (8 * me + lane8).astype(F32)) & (lane8 < 8) & (sub8 < 4)
            bias = jnp.where(live, 0.0, FLOOR)
            long_bias[:, pl.ds(blocks * 128, 128)] = jnp.where(
                sub8 < 4, bias, pltpu.roll(bias, 4, 0)
            )
            for b in range(8):
                home_bias[:, pl.ds(b * 128, 128)] = jnp.where(
                    (sub8 == b) & (lane8 < fill[b]), 0.0, FLOOR
                )
            home_bias[:, pl.ds(1024, 128)] = jnp.where(sub8 == lane8, 0.0, FLOOR)
            zero = jnp.zeros((LAYERS, 128, 128), BF16)
            keys[:, blocks] = zero
            values[:, blocks] = zero
            loads[11].wait()
            loads[12].wait()
        else:
            loads[14].wait()
            loads[15].wait()

        arrived(sq_r.at[layer, others], recv_sem.at[layer, SQ])
        arrived(rs_r.at[layer, others], recv_sem.at[layer, RS])
        square_all = jnp.sum(sq_r[layer], axis=0)
        scale = lax.rsqrt(
            jnp.sum(pick[...] * square_all, axis=1, keepdims=True) / width + EPS
        )
        sums = jnp.sum(rs_r[layer].astype(F32), axis=0)
        q_gain_row = q_gains[pl.ds(layer, 1), :].astype(F32)
        turned = [
            normed_turned(
                sums[:, 128 * g : 128 * g + 128], scale, q_gain_row, turn_cos[...], turn_sin[...]
            )
            for g in range(4)
        ]
        q_far = [t[8:16] for t in turned]
        q_far = jnp.concatenate(
            [
                jnp.where(sub8 < 4, q_far[0], pltpu.roll(q_far[1], 4, 0)),
                jnp.where(sub8 < 4, q_far[2], pltpu.roll(q_far[3], 4, 0)),
            ],
            axis=0,
        ).astype(BF16)
        qx_s[layer] = q_far
        q_share = remote(
            qx_s.at[layer], qx_r.at[layer], send_sem.at[layer, QX], recv_sem.at[layer, QX],
            sib, my_z,
        )
        q_share.start()

        q_own = jnp.concatenate([t[0:8] for t in turned], axis=0).astype(BF16)
        low = sums[8:16]
        kv = jnp.where(iota((8, 256), 0) < 4, pltpu.roll(low[:, 0:256], 4, 0), low[:, 256:512])
        new_key = normed_turned(
            kv[:, 0:128],
            scale[0:8],
            k_gains[pl.ds(layer, 1), :].astype(F32),
            turn_cos[0:8, :],
            turn_sin[0:8, :],
        )
        new_value = kv[:, 128:256] * scale[0:8]
        out_keys[layer] = new_key.astype(BF16)
        out_values[layer] = new_value.astype(BF16)
        pad = jnp.zeros((8, 128), F32)
        keys[layer, blocks, 0:16] = jnp.concatenate([new_key, pad], axis=0).astype(BF16)
        values[layer, blocks, 0:16] = jnp.concatenate([new_value, pad], axis=0).astype(BF16)

        s = jnp.concatenate(
            [
                dot_nt(q_own, keys[layer, 0:8].reshape(1024, 128)),
                dot_nt(q_own, keys[layer, blocks]),
            ],
            axis=1,
        )
        s = s * logit + jnp.concatenate([home_bias[...]] * 4, axis=0)
        p = jnp.exp(s - jnp.max(s, axis=1, keepdims=True))
        den = jnp.sum(p, axis=1, keepdims=True)
        p = p.astype(BF16)
        num = dot(p[:, 0:1024], values[layer, 0:8].reshape(1024, 128)) + dot(
            p[:, 1024:1152], values[layer, blocks]
        )
        attended = (num * (jnp.concatenate([own_keep] * 4, axis=0) / den)).astype(BF16)
        ho_s[layer] = attended
        ho_r[layer, chip] = attended
        to_chips(lambda to: [(ho_s.at[layer], ho_r.at[layer, chip], HO)], layer)

        q_share.wait_recv()
        q_all = q_far + qx_r[layer]
        s = dot_nt(q_all, keys[layer].reshape((blocks + 1) * 128, 128))
        s = s * logit + jnp.concatenate([long_bias[...]] * 2, axis=0)
        top = jnp.maximum(jnp.max(s, axis=1, keepdims=True), CEIL)
        p = jnp.exp(s - top)
        den = jnp.sum(p, axis=1, keepdims=True)
        num = dot(p.astype(BF16), values[layer].reshape((blocks + 1) * 128, 128))
        level = jnp.where(den > 0.0, top + jnp.log(jnp.maximum(den, TINY)), FLOOR)
        level = jnp.broadcast_to(level, (16, 128))
        mean = num / jnp.maximum(den, TINY)
        px_s[layer] = jnp.concatenate([mean, level], axis=0)
        p_share = remote(
            px_s.at[layer], px_r.at[layer], send_sem.at[layer, PX], recv_sem.at[layer, PX],
            sib, my_z,
        )
        p_share.start()
        p_share.wait_recv()
        other_mean, other_level = px_r[layer, 0:16], px_r[layer, 16:32]
        top = jnp.maximum(level, other_level)
        mine, theirs = jnp.exp(level - top), jnp.exp(other_level - top)
        both = mine + theirs
        mean = ((mean * mine + other_mean * theirs) / both).astype(BF16)
        level = top + jnp.log(both)
        level_row = jnp.sum(jnp.where(row16 == lane16, level, 0.0), axis=0, keepdims=True)
        lo_s[layer] = mean
        lo_r[layer, chip] = mean
        ll_s[layer] = level_row
        ll_r[layer, chip] = level_row
        to_chips(
            lambda to: [
                (lo_s.at[layer], lo_r.at[layer, chip], LO),
                (ll_s.at[layer], ll_r.at[layer, chip], LL),
            ],
            layer,
        )

        if layer == 0:
            loads[13].wait()
        shares[5 if layer == 0 else 9].wait_recv()
        arrived(ho_r.at[layer, others], recv_sem.at[layer, HO])
        homes = ho_r[layer].astype(F32)
        homes = jnp.concatenate(
            [homes[:, 8 * g : 8 * g + 8].reshape(half, 128) for g in range(4)], axis=1
        )
        arrived(ll_r.at[layer, others], recv_sem.at[layer, LL])
        arrived(lo_r.at[layer, others], recv_sem.at[layer, LO])
        levels = ll_r[layer]
        weight = jnp.exp(levels - jnp.max(levels, axis=0, keepdims=True))
        weight = weight / jnp.sum(weight, axis=0, keepdims=True)
        weight = jnp.sum(
            jnp.where(
                iota((n_chip, 16, 128), 1) == iota((n_chip, 16, 128), 2),
                jnp.broadcast_to(weight, (n_chip, 16, 128)),
                0.0,
            ),
            axis=2,
            keepdims=True,
        )
        merged = jnp.sum(weight * lo_r[layer].astype(F32), axis=0)
        merged = jnp.concatenate(
            [jnp.where(row16 // 4 == g, merged, 0.0) for g in range(4)], axis=1
        ).astype(BF16)
        attended = (homes + dot(spread[...], merged)).astype(BF16)

        branch = jnp.concatenate(
            [dot(attended, wo[layer, 0]), dot(attended, wo[layer, 1])], axis=1
        )
        zr_s[layer] = branch.astype(BF16).reshape(nz, part, 256)

        def reduce_z(t, carry):
            to = (my_z + t) % nz
            remote(
                zr_s.at[layer, to], zr_r.at[layer, my_z],
                send_sem.at[layer, ZR], recv_sem.at[layer, ZR], me, to,
            ).start()
            return carry

        lax.fori_loop(1, nz, reduce_z, 0)
        zr_r[layer, my_z] = zr_s[layer, my_z]
        arrived(zr_r.at[layer, pl.ds(0, nz - 1)], recv_sem.at[layer, ZR])
        hidden = (
            x_half[layer, my_z].astype(F32) + jnp.sum(zr_r[layer].astype(F32), axis=0)
        ).astype(BF16)

        if layer + 1 < LAYERS:
            za_s[...] = hidden
            x_half[layer + 1, my_z] = hidden

            def gather_z(t, carry):
                to = (my_z + t) % nz
                remote(
                    za_s, x_half.at[layer + 1, my_z],
                    send_sem.at[layer, ZA], recv_sem.at[layer, ZA], me, to,
                ).start()
                return carry

            lax.fori_loop(1, nz, gather_z, 0)
            arrived(x_half.at[layer + 1, pl.ds(0, nz - 1)], recv_sem.at[layer, ZA])
        else:
            mine, theirs = hidden[:, 0:128], hidden[:, 128:256]
            fin_s[0] = mine
            fin_s[1] = theirs
            fin_r[0, my_z] = mine

            def finish_z(t, carry):
                to = (my_z + t) % nz
                remote(
                    fin_s.at[1], fin_r.at[1, my_z],
                    send_sem.at[layer, ZB], recv_sem.at[layer, ZB], sib, to,
                ).start()
                remote(
                    fin_s.at[0], fin_r.at[0, my_z],
                    send_sem.at[layer, ZA], recv_sem.at[layer, ZA], me, to,
                ).start()
                return carry

            lax.fori_loop(1, nz, finish_z, 0)
            remote(
                fin_s.at[1], fin_r.at[1, my_z],
                send_sem.at[layer, ZB], recv_sem.at[layer, ZB], sib, my_z,
            ).start()
            arrived(fin_r.at[0, pl.ds(0, nz - 1)], recv_sem.at[layer, ZA])
            arrived(fin_r.at[1], recv_sem.at[layer, ZB])
            near = fin_r[0].astype(F32).reshape(n_chip, 8, 128)
            far = fin_r[1].astype(F32).reshape(n_chip, 8, 128)
            out[...] = (
                jnp.concatenate(
                    [jnp.where(core == 0, near, far), jnp.where(core == 0, far, near)], axis=1
                )
                .reshape(total, 128)
                .astype(BF16)
            )

    for copy in shares:
        copy.wait_send()
    for layer in range(LAYERS):
        for ref, phase in (
            (rs_r.at[layer, others], RS),
            (sq_r.at[layer, others], SQ),
            (qx_r.at[layer], QX),
            (px_r.at[layer], PX),
            (ho_r.at[layer, others], HO),
            (lo_r.at[layer, others], LO),
            (ll_r.at[layer, others], LL),
            (zr_r.at[layer, pl.ds(0, nz - 1)], ZR),
        ):
            arrived(ref, send_sem.at[layer, phase])
        if layer + 1 < LAYERS:
            arrived(x_half.at[layer + 1, pl.ds(0, nz - 1)], send_sem.at[layer, ZA])
        else:
            arrived(fin_r.at[0, pl.ds(0, nz - 1)], send_sem.at[layer, ZA])
            arrived(fin_r.at[1], send_sem.at[layer, ZB])


def on_device(
    n_chip, side, nz, width,
    hidden_in, norm_gain, q_gain, k_gain, w_query, w_key, w_value, w_out,
    cache_keys, cache_values, lengths, block_owner, block_fill,
):
    half = 8 * n_chip
    part = half // nz
    blocks = cache_keys.shape[1]
    total = hidden_in.shape[0]
    heads = w_query.shape[2]
    exponent = np.concatenate([np.arange(64), np.arange(64)]) * 2.0 / 128
    frequency = jnp.asarray((THETA**-exponent).astype(np.float32)[None, :])
    vmem, sem = pltpu.VMEM, pltpu.SemaphoreType.DMA
    anywhere = pl.BlockSpec(memory_space=pl.ANY)
    onchip = pl.BlockSpec(memory_space=pltpu.VMEM)
    both = (LAYERS, n_chip)
    return pl.pallas_call(
        functools.partial(kernel, n_chip, side, nz, float(width)),
        out_shape=(
            jax.ShapeDtypeStruct((total, 128), BF16),
            jax.ShapeDtypeStruct((LAYERS, 8, 128), BF16),
            jax.ShapeDtypeStruct((LAYERS, 8, 128), BF16),
        ),
        in_specs=[anywhere] * 14,
        out_specs=(onchip, onchip, onchip),
        scratch_shapes=[
            vmem((total, 128), BF16),
            vmem((total, 128), BF16),
            vmem((LAYERS, 256), BF16),
            vmem((LAYERS, 128), BF16),
            vmem((LAYERS, 128), BF16),
            vmem((LAYERS, 256, heads), BF16),
            vmem((LAYERS, 256, 128), BF16),
            vmem((LAYERS, 256, 128), BF16),
            vmem((LAYERS, 2, heads, 128), BF16),
            vmem((LAYERS, blocks + 1, 128, 128), BF16),
            vmem((LAYERS, blocks + 1, 128, 128), BF16),
            vmem((1, total), jnp.int32),
            pltpu.SMEM((blocks,), jnp.int32),
            pltpu.SMEM((blocks,), jnp.int32),
            vmem((1, 128), F32),
            vmem((LAYERS, nz, part, 256), BF16),
            vmem((8, (blocks + 1) * 128), F32),
            vmem((8, 9 * 128), F32),
            vmem((16, 128), F32),
            vmem((16, 128), F32),
            vmem((16, 128), F32),
            vmem((half, 16), BF16),
            vmem((*both, 16, 512), BF16),
            vmem((*both, 16, 512), BF16),
            vmem((LAYERS, 1, 128), F32),
            vmem((*both, 1, 128), F32),
            vmem((LAYERS, 16, 128), BF16),
            vmem((LAYERS, 16, 128), BF16),
            vmem((LAYERS, 32, 128), F32),
            vmem((LAYERS, 32, 128), F32),
            vmem((LAYERS, 32, 128), BF16),
            vmem((*both, 32, 128), BF16),
            vmem((LAYERS, 16, 128), BF16),
            vmem((*both, 16, 128), BF16),
            vmem((LAYERS, 1, 128), F32),
            vmem((*both, 1, 128), F32),
            vmem((LAYERS, nz, part, 256), BF16),
            vmem((LAYERS, nz, part, 256), BF16),
            vmem((part, 256), BF16),
            vmem((2, part, 128), BF16),
            vmem((2, nz, part, 128), BF16),
            sem((16,)),
            sem((10,)),
            sem((10,)),
            sem((LAYERS, 10)),
            sem((LAYERS, 10)),
        ],
        compiler_params=pltpu.CompilerParams(
            collective_id=0, has_side_effects=True, vmem_limit_bytes=67043328
        ),
        name="attention_layers",
    )(
        hidden_in, norm_gain, q_gain, k_gain, w_query, w_key, w_value, w_out,
        cache_keys, cache_values, lengths.reshape(1, total), block_owner, block_fill, frequency,
    )


def solution(mesh):
    n_req, nz = mesh.shape["req"], mesh.shape["kv"]
    n_chip = n_req // 2
    side = math.isqrt(n_chip)
    in_specs = (
        P(None, "req"),
        P(None, "req"),
        P(),
        P(),
        P(None, "req", "kv"),
        P(None, "req", "kv"),
        P(None, "req", "kv"),
        P(None, "kv", "req"),
        P(None, "req", None, "kv"),
        P(None, "req", None, "kv"),
        P(),
        P("req"),
        P("req"),
    )
    out_specs = (P(None, "req"), P(None, "req", "kv"), P(None, "req", "kv"))
    return jax.shard_map(
        functools.partial(on_device, n_chip, side, nz, 128 * n_req),
        mesh=mesh,
        in_specs=in_specs,
        out_specs=out_specs,
        check_vma=False,
    )
```

```python
import functools
import math

import jax
import jax.numpy as jnp
import numpy as np
from jax import lax
from jax.experimental import pallas as pl
from jax.experimental.pallas import tpu as pltpu
from jax.sharding import PartitionSpec as P

LAYERS = 2
EPS = 1e-06
THETA = 1000000.0
FLOOR = -1e30
CEIL = -1e29
TINY = 1e-30
MESH = pl.DeviceIdType.MESH
F32 = jnp.float32
BF16 = jnp.bfloat16

RS, SQ, RL, SL, XL, PX, HO, LO, LL, ZR, ZA, ZB = range(12)


def dot(a, b):
    return jnp.dot(a, b, preferred_element_type=F32)


def dot_nt(a, b):
    return lax.dot_general(a, b, (((1,), (1,)), ((), ())), preferred_element_type=F32)


def iota(shape, dim):
    return lax.broadcasted_iota(jnp.int32, shape, dim)


def kernel(
    n_chip,
    side,
    nz,
    width,
    x_in, norm_gain, q_gain, k_gain, w_query, w_key, w_value, w_out,
    cache_keys, cache_values, lengths, block_owner, block_fill, frequency,
    out, out_keys, out_values,
    x_own, x_sib, gains, q_gains, k_gains, wq, wk, wv, wo, keys, values,
    lens, owner, fill, freq,
    x_half, long_bias, home_bias, own_cos, own_sin, long_cos, long_sin, own_pick, spread,
    rs_s, rs_r, sq_s, sq_r, rl_s, rl_r, sl_s, sl_r, xl_s, xl_r, px_s, px_r,
    ho_s, ho_r, lo_s, lo_r, ll_s, ll_r, zr_s, zr_r, za_s, fin_s, new_s,
    load_sem, new_sem, init_send, init_recv, send_sem, recv_sem,
):
    half = 8 * n_chip
    owners = nz // 2
    part = half // owners
    blocks = cache_keys.shape[1]
    total = lens.shape[1]
    me = lax.axis_index("req")
    my_z = lax.axis_index("kv")
    core = lax.rem(me, 2)
    chip = lax.div(me, 2)
    chip_x, chip_y = lax.div(chip, side), lax.rem(chip, side)
    sib = me + 1 - 2 * core
    my_part = lax.rem(my_z, owners)

    def ring(d, n):
        return min(d, n - d)

    steps = sorted(
        [(dx, dy) for dx in range(side) for dy in range(side) if dx or dy],
        key=lambda d: -ring(d[0], side) - ring(d[1], side),
    )
    at_x = [lax.rem(chip_x + d, side) * side for d in range(side)]
    at_y = [lax.rem(chip_y + d, side) for d in range(side)]
    chips = [at_x[dx] + at_y[dy] for dx, dy in steps]
    peers = [2 * c + core for c in chips]
    z_at = [lax.rem(my_z + d, nz) for d in range(nz)]
    z_far = sorted(range(1, nz), key=lambda d: -ring(d, nz))
    z_near = {8: (6, 2, 7, 1), 2: ()}[nz]

    barrier = pltpu.get_barrier_semaphore()

    def greet(req, kv):
        pl.semaphore_signal(
            barrier, inc=1, device_id={"req": req, "kv": kv}, device_id_type=MESH
        )

    for req in peers:
        greet(req, my_z)
    for d in z_far:
        greet(me, z_at[d])
    for d in z_near:
        greet(sib, z_at[d])
    greet(sib, my_z)

    loads = [
        pltpu.make_async_copy(src, dst, load_sem.at[at])
        for at, (src, dst) in enumerate(
            [
                (lengths, lens),
                (frequency, freq),
                (norm_gain, gains.at[:, pl.ds(0, 128)]),
                (q_gain, q_gains),
                (k_gain, k_gains),
                (x_in, x_own),
                (w_query, wq.at[:, pl.ds(0, 128)]),
                (w_key, wk.at[:, pl.ds(0, 128)]),
                (w_value, wv.at[:, pl.ds(0, 128)]),
                (block_owner, owner),
                (block_fill, fill),
                (cache_keys.at[0], keys.at[0, pl.ds(0, blocks)]),
                (cache_values.at[0], values.at[0, pl.ds(0, blocks)]),
                (w_out, wo.at[:, 0]),
                (cache_keys.at[1], keys.at[1, pl.ds(0, blocks)]),
                (cache_values.at[1], values.at[1, pl.ds(0, blocks)]),
            ]
        )
    ]
    for copy in loads:
        copy.start()

    row16 = iota((16, 128), 0)
    lane16 = iota((16, 128), 1)
    sub8 = iota((8, 128), 0)
    lane8 = iota((8, 128), 1)

    def twice(t):
        return jnp.where(iota(t[0].shape, 0) < 4, t[0], pltpu.roll(t[1], 4, 0))

    loads[0].wait()
    loads[1].wait()
    length_row = lens[...].astype(F32)
    request_row = iota((8, total), 1).astype(F32)
    is_long = jnp.where(length_row > 128.0, 1.0, 0.0)
    before = jnp.where(iota((total, total), 0) < iota((total, total), 1), 1.0, 0.0).astype(BF16)
    rank = dot(jnp.broadcast_to(is_long, (8, total)).astype(BF16), before)
    slot8 = iota((8, total), 0)
    long_hot = jnp.where(
        (rank.astype(jnp.int32) == slot8) & (slot8 < 4),
        jnp.broadcast_to(is_long, (8, total)),
        0.0,
    )
    own_hot = jnp.where(iota((8, total), 1) == 8 * me + slot8, 1.0, 0.0)
    long_id = jnp.sum(long_hot * request_row, axis=1, keepdims=True)
    long_at = jnp.sum(long_hot * length_row, axis=1, keepdims=True)
    own_at = jnp.sum(own_hot * length_row, axis=1, keepdims=True)
    own_keep = jnp.where(own_at > 128.0, 0.0, 1.0)
    row_of = iota((total, 128), 1)
    to_half = jnp.where(
        (iota((total, 128), 0) == (row_of // 8) * 16 + 8 * core + row_of % 8) & (row_of < half),
        1.0,
        0.0,
    ).astype(BF16)
    long_half = dot(long_hot.astype(BF16), to_half)
    own_pick[...] = jnp.where(lane8 == 8 * chip + sub8, 1.0, 0.0)
    four = twice([long_half, long_half])
    eye = jnp.where(iota((half, 128), 0) == iota((half, 128), 1), 1.0, 0.0)
    spread[...] = dot_nt(
        eye.astype(BF16), jnp.concatenate([four, four], axis=0).astype(BF16)
    ).astype(BF16)
    long_sel = jnp.concatenate([long_half, jnp.zeros((8, 128), F32)], axis=0).astype(BF16)
    long_sel = long_sel[:, :half]
    long_any = jnp.concatenate([long_hot, jnp.zeros((8, total), F32)], axis=0).astype(BF16)
    long_pick = jnp.where(lane16 == row16 % 4, 1.0, 0.0)

    def turns(at, cos_ref, sin_ref):
        angle = at * freq[...]
        rows = angle.shape[0]
        sin = jnp.sin(angle)
        cos_ref[...] = jnp.cos(angle)
        sin_ref[...] = jnp.where(iota((rows, 128), 1) < 64, -sin, sin)

    turns(own_at, own_cos, own_sin)
    at4 = twice([jnp.broadcast_to(long_at, (8, 128))] * 2)
    turns(jnp.concatenate([at4, at4], axis=0), long_cos, long_sin)

    def half_of(ref):
        rows = ref[...].astype(F32).reshape(n_chip, 2, 8, 128)
        return jnp.where(core == 0, rows[:, 0], rows[:, 1]).reshape(half, 128)

    loads[5].wait()
    x_first = half_of(x_own)
    long_first = dot(long_any, x_own[...])

    pl.semaphore_wait(barrier, len(peers) + len(z_far) + len(z_near) + 1)

    def remote(src, dst, send, recv, req, kv):
        return pltpu.make_async_remote_copy(
            src_ref=src,
            dst_ref=dst,
            send_sem=send,
            recv_sem=recv,
            device_id={"req": req, "kv": kv},
            device_id_type=MESH,
        )

    shares = [
        remote(src, dst, init_send.at[at], init_recv.at[at], sib, my_z)
        for at, (src, dst) in enumerate(
            [
                (x_in, x_sib),
                (norm_gain, gains.at[:, pl.ds(128, 128)]),
                (w_query.at[0], wq.at[0, pl.ds(128, 128)]),
                (w_key.at[0], wk.at[0, pl.ds(128, 128)]),
                (w_value.at[0], wv.at[0, pl.ds(128, 128)]),
                (w_out.at[0], wo.at[0, 1]),
                (w_query.at[1], wq.at[1, pl.ds(128, 128)]),
                (w_key.at[1], wk.at[1, pl.ds(128, 128)]),
                (w_value.at[1], wv.at[1, pl.ds(128, 128)]),
                (w_out.at[1], wo.at[1, 1]),
            ]
        )
    ]
    for copy in shares:
        copy.start()

    for at in (2, 3, 4, 6, 7, 8):
        loads[at].wait()
    shares[0].wait_recv()
    shares[1].wait_recv()
    x_half[0] = (
        jnp.concatenate([x_first, half_of(x_sib)], axis=1).astype(BF16).reshape(owners, part, 256)
    )
    long_x = jnp.concatenate([long_first, dot(long_any, x_sib[...])], axis=1)
    for at in (2, 3, 4):
        shares[at].wait_recv()

    def normed_turned(t, gain, cos, sin):
        t = t * lax.rsqrt(jnp.mean(t * t, axis=1, keepdims=True) + EPS) * gain
        return t * cos + pltpu.roll(t, 64, 1) * sin

    def arrived(ref, sem):
        pltpu.make_async_copy(ref, ref, sem).wait()

    def to_chips(pairs, layer):
        for to, req in zip(chips, peers):
            for src, dst, phase in pairs(to):
                remote(
                    src, dst, send_sem.at[layer, phase], recv_sem.at[layer, phase], req, my_z
                ).start()

    def to_sib(src, dst, phase, layer):
        copy = remote(
            src, dst, send_sem.at[layer, phase], recv_sem.at[layer, phase], sib, my_z
        )
        copy.start()
        return copy

    def as_row(column, mask):
        return jnp.sum(jnp.where(mask, column, 0.0), axis=0, keepdims=True)

    logit = 1.0 / math.sqrt(128)
    others = pl.ds(0, n_chip - 1)
    on_diagonal = iota((half, 128), 0) == iota((half, 128), 1)

    def send_long(layer, long_x):
        square = jnp.sum(long_x * long_x, axis=1, keepdims=True)
        square_row = as_row(square, row16 == lane16)
        sl_s[layer] = square_row
        sl_r[layer, chip] = square_row
        gain = gains[pl.ds(layer, 1), :].astype(F32)
        q = dot((long_x * gain).astype(BF16), wq[layer])[0:8]
        q = [q[:, 128 * g : 128 * g + 128] for g in range(4)]
        q = jnp.concatenate([twice(q[0:2]), twice(q[2:4])], axis=0).astype(BF16)
        rl_s[layer] = q
        rl_r[layer, chip] = q
        to_chips(
            lambda to: [
                (rl_s.at[layer], rl_r.at[layer, chip], RL),
                (sl_s.at[layer], sl_r.at[layer, chip], SL),
            ],
            layer,
        )

    for layer in range(LAYERS):
        x = x_half[layer].reshape(half, 256)
        if layer == 0:
            send_long(layer, long_x)
        else:
            long_x = dot(long_sel, x)
            xl_s[...] = long_x.astype(BF16)
            x_share = to_sib(xl_s, xl_r, XL, layer)
        x = x.astype(F32)
        square = jnp.sum(x * x, axis=1, keepdims=True)
        square_row = as_row(square, on_diagonal)
        sq_s[layer] = square_row
        sq_r[layer, chip] = square_row
        xg = (x * gains[pl.ds(layer, 1), :].astype(F32)).astype(BF16)
        if layer == 1:
            for at in (6, 7, 8):
                shares[at].wait_recv()
        q = dot(xg, wq[layer])
        upper = q[:, 0:384].reshape(n_chip, 8, 384)
        lower = jnp.concatenate(
            [q[:, 384:512], dot(xg, wk[layer]), dot(xg, wv[layer])], axis=1
        ).reshape(n_chip, 8, 384)
        rs_s[layer] = jnp.concatenate([upper, lower], axis=1).astype(BF16)
        to_chips(
            lambda to: [
                (rs_s.at[layer, to], rs_r.at[layer, chip], RS),
                (sq_s.at[layer], sq_r.at[layer, chip], SQ),
            ],
            layer,
        )
        rs_r[layer, chip] = rs_s[layer, chip]

        if layer == 0:
            loads[9].wait()
            loads[10].wait()

            def block_masks(b, carry):
                live = (lane8 < fill[b]) & (long_id == owner[b].astype(F32)) & (sub8 < 4)
                bias = jnp.where(live, 0.0, FLOOR)
                long_bias[:, pl.ds(pl.multiple_of(b * 128, 128), 128)] = twice([bias, bias])
                return carry

            lax.fori_loop(0, blocks, block_masks, 0)
            live = (long_id == (8 * me + lane8).astype(F32)) & (lane8 < 8) & (sub8 < 4)
            bias = jnp.where(live, 0.0, FLOOR)
            long_bias[:, pl.ds(blocks * 128, 128)] = twice([bias, bias])
            for b in range(8):
                home_bias[:, pl.ds(b * 128, 128)] = jnp.where(
                    (sub8 == b) & (lane8 < fill[b]), 0.0, FLOOR
                )
            home_bias[:, pl.ds(1024, 128)] = jnp.where(sub8 == lane8, 0.0, FLOOR)
            zero = jnp.zeros((LAYERS, 128, 128), BF16)
            keys[:, blocks] = zero
            values[:, blocks] = zero
            loads[11].wait()
            loads[12].wait()
        else:
            x_share.wait_recv()
            theirs = xl_r[...].astype(F32)
            send_long(
                layer,
                long_x + jnp.concatenate([theirs[:, 128:256], theirs[:, 0:128]], axis=1),
            )
            loads[14].wait()
            loads[15].wait()

        arrived(sq_r.at[layer, others], recv_sem.at[layer, SQ])
        arrived(rs_r.at[layer, others], recv_sem.at[layer, RS])
        sums = jnp.sum(rs_r[layer].astype(F32), axis=0)
        scale = lax.rsqrt(
            jnp.sum(own_pick[...] * jnp.sum(sq_r[layer], axis=0), axis=1, keepdims=True) / width
            + EPS
        )
        q_gain_row = q_gains[pl.ds(layer, 1), :].astype(F32)
        new_key = normed_turned(
            sums[8:16, 128:256] * scale,
            k_gains[pl.ds(layer, 1), :].astype(F32),
            own_cos[...],
            own_sin[...],
        )
        new_value = sums[8:16, 256:384] * scale
        pad = jnp.zeros((8, 128), F32)
        keys[layer, blocks, 0:16] = jnp.concatenate([new_key, pad], axis=0).astype(BF16)
        values[layer, blocks, 0:16] = jnp.concatenate([new_value, pad], axis=0).astype(BF16)
        new_s[0, layer] = new_key.astype(BF16)
        new_s[1, layer] = new_value.astype(BF16)
        q_own = [
            normed_turned(t * scale, q_gain_row, own_cos[...], own_sin[...])
            for t in (
                sums[0:8, 0:128], sums[0:8, 128:256], sums[0:8, 256:384], sums[8:16, 0:128]
            )
        ]
        q_own = jnp.concatenate(q_own, axis=0).astype(BF16)

        arrived(sl_r.at[layer, others], recv_sem.at[layer, SL])
        arrived(rl_r.at[layer, others], recv_sem.at[layer, RL])
        scale = lax.rsqrt(
            jnp.sum(long_pick * jnp.sum(sl_r[layer], axis=0), axis=1, keepdims=True) / width
            + EPS
        )
        q_long = normed_turned(
            jnp.sum(rl_r[layer].astype(F32), axis=0) * scale,
            q_gain_row,
            long_cos[...],
            long_sin[...],
        ).astype(BF16)
        s = dot_nt(q_long, keys[layer].reshape((blocks + 1) * 128, 128))
        s = s * logit + jnp.concatenate([long_bias[...]] * 2, axis=0)
        top = jnp.maximum(jnp.max(s, axis=1, keepdims=True), CEIL)
        p = jnp.exp(s - top)
        den = jnp.sum(p, axis=1, keepdims=True)
        num = dot(p.astype(BF16), values[layer].reshape((blocks + 1) * 128, 128))
        level = jnp.where(den > 0.0, top + jnp.log(jnp.maximum(den, TINY)), FLOOR)
        level = jnp.broadcast_to(level, (16, 128))
        mean = num / jnp.maximum(den, TINY)
        px_s[layer] = jnp.concatenate([mean, level], axis=0)
        p_share = to_sib(px_s.at[layer], px_r.at[layer], PX, layer)

        s = jnp.concatenate(
            [
                dot_nt(q_own, keys[layer, 0:8].reshape(1024, 128)),
                dot_nt(q_own, keys[layer, blocks]),
            ],
            axis=1,
        )
        s = s * logit + jnp.concatenate([home_bias[...]] * 4, axis=0)
        p = jnp.exp(s - jnp.max(s, axis=1, keepdims=True))
        den = jnp.sum(p, axis=1, keepdims=True)
        p = p.astype(BF16)
        num = dot(p[:, 0:1024], values[layer, 0:8].reshape(1024, 128)) + dot(
            p[:, 1024:1152], values[layer, blocks]
        )
        attended = (num * (jnp.concatenate([own_keep] * 4, axis=0) / den)).astype(BF16)
        ho_s[layer] = attended
        ho_r[layer, chip] = attended
        to_chips(lambda to: [(ho_s.at[layer], ho_r.at[layer, chip], HO)], layer)

        p_share.wait_recv()
        other_mean, other_level = px_r[layer, 0:16], px_r[layer, 16:32]
        top = jnp.maximum(level, other_level)
        mine, theirs = jnp.exp(level - top), jnp.exp(other_level - top)
        both = mine + theirs
        mean = ((mean * mine + other_mean * theirs) / both).astype(BF16)
        level_row = as_row(top + jnp.log(both), row16 == lane16)
        lo_s[layer] = mean
        lo_r[layer, chip] = mean
        ll_s[layer] = level_row
        ll_r[layer, chip] = level_row
        to_chips(
            lambda to: [
                (lo_s.at[layer], lo_r.at[layer, chip], LO),
                (ll_s.at[layer], ll_r.at[layer, chip], LL),
            ],
            layer,
        )

        if layer == 0:
            loads[13].wait()
        else:
            news = [
                pltpu.make_async_copy(new_s.at[at], ref, new_sem.at[at])
                for at, ref in enumerate((out_keys, out_values))
            ]
            for copy in news:
                copy.start()
        shares[5 if layer == 0 else 9].wait_recv()
        arrived(ho_r.at[layer, others], recv_sem.at[layer, HO])
        homes = ho_r[layer].astype(F32)
        homes = jnp.concatenate(
            [homes[:, 8 * g : 8 * g + 8].reshape(half, 128) for g in range(4)], axis=1
        )
        arrived(ll_r.at[layer, others], recv_sem.at[layer, LL])
        levels = ll_r[layer]
        weight = jnp.exp(levels - jnp.max(levels, axis=0, keepdims=True))
        weight = weight / jnp.sum(weight, axis=0, keepdims=True)
        weight = jnp.sum(
            jnp.where(
                iota((n_chip, 16, 128), 1) == iota((n_chip, 16, 128), 2),
                jnp.broadcast_to(weight, (n_chip, 16, 128)),
                0.0,
            ),
            axis=2,
            keepdims=True,
        )
        arrived(lo_r.at[layer, others], recv_sem.at[layer, LO])
        merged = jnp.sum(weight * lo_r[layer].astype(F32), axis=0)
        merged = jnp.concatenate(
            [jnp.where(row16 // 4 == g, merged, 0.0) for g in range(4)], axis=1
        ).astype(BF16)
        attended = (homes + dot(spread[...], merged)).astype(BF16)

        branch = jnp.concatenate(
            [dot(attended, wo[layer, 0]), dot(attended, wo[layer, 1])], axis=1
        )
        zr_s[layer] = branch.astype(BF16).reshape(owners, part, 256)
        for d in z_far:
            remote(
                zr_s.at[layer, lax.rem(z_at[d], owners)], zr_r.at[layer, my_z],
                send_sem.at[layer, ZR], recv_sem.at[layer, ZR], me, z_at[d],
            ).start()
        zr_r[layer, my_z] = zr_s[layer, my_part]
        arrived(zr_r.at[layer, pl.ds(0, nz - 1)], recv_sem.at[layer, ZR])
        hidden = (
            x_half[layer, my_part].astype(F32) + jnp.sum(zr_r[layer].astype(F32), axis=0)
        ).astype(BF16)

        mid = part // 2
        rows_for = {1: (0, part), 7: (0, part), 6: (0, mid), 2: (mid, mid)}
        if layer + 1 < LAYERS:
            za_s[...] = hidden
            x_half[layer + 1, my_part] = hidden
            for d in z_near:
                rows = pl.ds(*rows_for[d])
                remote(
                    za_s.at[rows], x_half.at[layer + 1, my_part, rows],
                    send_sem.at[layer, ZA], recv_sem.at[layer, ZA], me, z_at[d],
                ).start()
            if owners > 1:
                arrived(x_half.at[layer + 1, pl.ds(0, owners - 1)], recv_sem.at[layer, ZA])
        else:
            fin_s[0] = hidden[:, 0:128]
            fin_s[1] = hidden[:, 128:256]
            start = pl.multiple_of(my_part * part, part)
            for d in z_near:
                first, count = rows_for[d]
                rows = pl.ds(first, count)
                to = out.at[core, pl.ds(pl.multiple_of(start + first, count), count)]
                remote(
                    fin_s.at[1, rows], to,
                    send_sem.at[layer, ZB], recv_sem.at[layer, ZB], sib, z_at[d],
                ).start()
                remote(
                    fin_s.at[0, rows], to,
                    send_sem.at[layer, ZA], recv_sem.at[layer, ZA], me, z_at[d],
                ).start()
            to = out.at[core, pl.ds(start, part)]
            remote(
                fin_s.at[1], to,
                send_sem.at[layer, ZB], recv_sem.at[layer, ZB], sib, my_z,
            ).start()
            mine = pltpu.make_async_copy(fin_s.at[0], to, new_sem.at[2])
            mine.start()
            mine.wait()
            for copy in news:
                copy.wait()
            most = pl.ds(0, half - part)
            if owners > 1:
                arrived(out.at[core, most], recv_sem.at[layer, ZA])
            arrived(out.at[1 - core], recv_sem.at[layer, ZB])

    for copy in shares:
        copy.wait_send()
    x_share.wait_send()
    for layer in range(LAYERS):
        for ref, phase in (
            (rs_r.at[layer, others], RS),
            (sq_r.at[layer, others], SQ),
            (rl_r.at[layer, others], RL),
            (sl_r.at[layer, others], SL),
            (px_r.at[layer], PX),
            (ho_r.at[layer, others], HO),
            (lo_r.at[layer, others], LO),
            (ll_r.at[layer, others], LL),
            (zr_r.at[layer, pl.ds(0, nz - 1)], ZR),
        ):
            arrived(ref, send_sem.at[layer, phase])
        if layer + 1 < LAYERS:
            if owners > 1:
                arrived(x_half.at[layer + 1, pl.ds(0, owners - 1)], send_sem.at[layer, ZA])
        else:
            if owners > 1:
                arrived(out.at[core, most], send_sem.at[layer, ZA])
            arrived(out.at[1 - core], send_sem.at[layer, ZB])


def finish(hidden, new_keys, new_values, out, out_keys, out_values, rows, k_rows, v_rows, sem):
    first = [
        pltpu.make_async_copy(hidden.at[0], rows.at[:, 0], sem.at[0]),
        pltpu.make_async_copy(hidden.at[1], rows.at[:, 1], sem.at[1]),
        pltpu.make_async_copy(new_keys, k_rows, sem.at[2]),
        pltpu.make_async_copy(new_values, v_rows, sem.at[3]),
    ]
    last = [
        pltpu.make_async_copy(rows, out, sem.at[4]),
        pltpu.make_async_copy(k_rows, out_keys, sem.at[5]),
        pltpu.make_async_copy(v_rows, out_values, sem.at[6]),
    ]
    for copy in first:
        copy.start()
    first[0].wait()
    first[1].wait()
    last[0].start()
    first[2].wait()
    last[1].start()
    first[3].wait()
    last[2].start()
    for copy in last:
        copy.wait()


def on_device(
    n_chip, side, nz, width,
    hidden_in, norm_gain, q_gain, k_gain, w_query, w_key, w_value, w_out,
    cache_keys, cache_values, lengths, block_owner, block_fill,
):
    half = 8 * n_chip
    owners = nz // 2
    part = half // owners
    blocks = cache_keys.shape[1]
    total = hidden_in.shape[0]
    heads = w_query.shape[2]
    exponent = np.concatenate([np.arange(64), np.arange(64)]) * 2.0 / 128
    frequency = jnp.asarray((THETA**-exponent).astype(np.float32)[None, :])
    vmem, sem = pltpu.VMEM, pltpu.SemaphoreType.DMA
    anywhere = pl.BlockSpec(memory_space=pl.ANY)
    both = (LAYERS, n_chip)
    news = jax.ShapeDtypeStruct((LAYERS, 8, 128), BF16)
    hidden, new_keys, new_values = pl.pallas_call(
        functools.partial(kernel, n_chip, side, nz, float(width)),
        out_shape=(jax.ShapeDtypeStruct((2, half, 128), BF16), news, news),
        in_specs=[anywhere] * 14,
        out_specs=(anywhere, anywhere, anywhere),
        scratch_shapes=[
            vmem((total, 128), BF16),
            vmem((total, 128), BF16),
            vmem((LAYERS, 256), BF16),
            vmem((LAYERS, 128), BF16),
            vmem((LAYERS, 128), BF16),
            vmem((LAYERS, 256, heads), BF16),
            vmem((LAYERS, 256, 128), BF16),
            vmem((LAYERS, 256, 128), BF16),
            vmem((LAYERS, 2, heads, 128), BF16),
            vmem((LAYERS, blocks + 1, 128, 128), BF16),
            vmem((LAYERS, blocks + 1, 128, 128), BF16),
            vmem((1, total), jnp.int32),
            pltpu.SMEM((blocks,), jnp.int32),
            pltpu.SMEM((blocks,), jnp.int32),
            vmem((1, 128), F32),
            vmem((LAYERS, owners, part, 256), BF16),
            vmem((8, (blocks + 1) * 128), F32),
            vmem((8, 9 * 128), F32),
            vmem((8, 128), F32),
            vmem((8, 128), F32),
            vmem((16, 128), F32),
            vmem((16, 128), F32),
            vmem((8, 128), F32),
            vmem((half, 16), BF16),
            vmem((*both, 16, 384), BF16),
            vmem((*both, 16, 384), BF16),
            vmem((LAYERS, 1, 128), F32),
            vmem((*both, 1, 128), F32),
            vmem((LAYERS, 16, 128), BF16),
            vmem((*both, 16, 128), BF16),
            vmem((LAYERS, 1, 128), F32),
            vmem((*both, 1, 128), F32),
            vmem((16, 256), BF16),
            vmem((16, 256), BF16),
            vmem((LAYERS, 32, 128), F32),
            vmem((LAYERS, 32, 128), F32),
            vmem((LAYERS, 32, 128), BF16),
            vmem((*both, 32, 128), BF16),
            vmem((LAYERS, 16, 128), BF16),
            vmem((*both, 16, 128), BF16),
            vmem((LAYERS, 1, 128), F32),
            vmem((*both, 1, 128), F32),
            vmem((LAYERS, owners, part, 256), BF16),
            vmem((LAYERS, nz, part, 256), BF16),
            vmem((part, 256), BF16),
            vmem((2, part, 128), BF16),
            vmem((2, LAYERS, 8, 128), BF16),
            sem((16,)),
            sem((3,)),
            sem((10,)),
            sem((10,)),
            sem((LAYERS, 12)),
            sem((LAYERS, 12)),
        ],
        compiler_params=pltpu.CompilerParams(
            collective_id=0, has_side_effects=True, vmem_limit_bytes=67043328
        ),
        name="attention_layers",
    )(
        hidden_in, norm_gain, q_gain, k_gain, w_query, w_key, w_value, w_out,
        cache_keys, cache_values, lengths.reshape(1, total), block_owner, block_fill, frequency,
    )
    out, new_keys, new_values = pl.pallas_call(
        finish,
        out_shape=(jax.ShapeDtypeStruct((n_chip, 2, 8, 128), BF16), news, news),
        in_specs=[anywhere] * 3,
        out_specs=(anywhere, anywhere, anywhere),
        scratch_shapes=[
            vmem((n_chip, 2, 8, 128), BF16),
            vmem((LAYERS, 8, 128), BF16),
            vmem((LAYERS, 8, 128), BF16),
            sem((7,)),
        ],
        name="finish",
    )(hidden.reshape(2, n_chip, 8, 128), new_keys, new_values)
    return out.reshape(total, 128), new_keys, new_values


def solution(mesh):
    n_req, nz = mesh.shape["req"], mesh.shape["kv"]
    n_chip = n_req // 2
    side = math.isqrt(n_chip)
    in_specs = (
        P(None, "req"),
        P(None, "req"),
        P(),
        P(),
        P(None, "req", "kv"),
        P(None, "req", "kv"),
        P(None, "req", "kv"),
        P(None, "kv", "req"),
        P(None, "req", None, "kv"),
        P(None, "req", None, "kv"),
        P(),
        P("req"),
        P("req"),
    )
    out_specs = (P(None, "req"), P(None, "req", "kv"), P(None, "req", "kv"))
    return jax.shard_map(
        functools.partial(on_device, n_chip, side, nz, 128 * n_req),
        mesh=mesh,
        in_specs=in_specs,
        out_specs=out_specs,
        check_vma=False,
    )
```

```python
import functools
import math

import jax
import jax.numpy as jnp
import numpy as np
from jax import lax
from jax.experimental import pallas as pl
from jax.experimental.pallas import tpu as pltpu
from jax.sharding import PartitionSpec as P

LAYERS = 2
EPS = 1e-06
THETA = 1000000.0
FLOOR = -1e30
CEIL = -1e29
TINY = 1e-30
MESH = pl.DeviceIdType.MESH
F32 = jnp.float32
BF16 = jnp.bfloat16

RS, SQ, RL, SL, XL, PX, HO, LO, LL, ZR, ZA, ZB = range(12)


def dot(a, b):
    return jnp.dot(a, b, preferred_element_type=F32)


def dot_nt(a, b):
    return lax.dot_general(a, b, (((1,), (1,)), ((), ())), preferred_element_type=F32)


def iota(shape, dim):
    return lax.broadcasted_iota(jnp.int32, shape, dim)


def kernel(
    n_chip,
    side,
    nz,
    width,
    x_in, norm_gain, q_gain, k_gain, w_query, w_key, w_value, w_out,
    cache_keys, cache_values, lengths, block_owner, block_fill, frequency,
    out, out_keys, out_values,
    x_own, x_sib, gains, q_gains, k_gains, wq, wk, wv, wo, keys, values,
    lens, owner, fill, freq,
    x_half, long_bias, new_bias, home_bias, own_cos, own_sin, long_cos, long_sin, own_pick, spread,
    rs_s, rs_r, sq_s, sq_r, rl_s, rl_r, sl_s, sl_r, xl_s, xl_r, px_s, px_r,
    ho_s, ho_r, lo_s, lo_r, ll_s, ll_r, zr_s, zr_r, za_s, fin_s,
    load_sem, init_send, init_recv, send_sem, recv_sem,
):
    half = 8 * n_chip
    owners = nz // 2
    part = half // owners
    blocks = cache_keys.shape[1]
    total = lens.shape[1]
    me = lax.axis_index("req")
    my_z = lax.axis_index("kv")
    core = lax.rem(me, 2)
    chip = lax.div(me, 2)
    chip_x, chip_y = lax.div(chip, side), lax.rem(chip, side)
    sib = me + 1 - 2 * core
    my_part = lax.rem(my_z, owners)

    def ring(d, n):
        return min(d, n - d)

    steps = sorted(
        [(dx, dy) for dx in range(side) for dy in range(side) if dx or dy],
        key=lambda d: -ring(d[0], side) - ring(d[1], side),
    )
    at_x = [lax.rem(chip_x + d, side) * side for d in range(side)]
    at_y = [lax.rem(chip_y + d, side) for d in range(side)]
    chips = [at_x[dx] + at_y[dy] for dx, dy in steps]
    peers = [2 * c + core for c in chips]
    z_at = [lax.rem(my_z + d, nz) for d in range(nz)]
    z_far = sorted(range(1, nz), key=lambda d: -ring(d, nz))
    z_near = {8: (6, 2, 7, 1), 2: ()}[nz]

    barrier = pltpu.get_barrier_semaphore()

    def greet(req, kv):
        pl.semaphore_signal(
            barrier, inc=1, device_id={"req": req, "kv": kv}, device_id_type=MESH
        )

    for req in peers:
        greet(req, my_z)
    for d in z_far:
        greet(me, z_at[d])
    for d in z_near:
        greet(sib, z_at[d])
    greet(sib, my_z)

    loads = [
        pltpu.make_async_copy(src, dst, load_sem.at[at])
        for at, (src, dst) in enumerate(
            [
                (lengths, lens),
                (frequency, freq),
                (norm_gain, gains.at[:, pl.ds(0, 128)]),
                (q_gain, q_gains),
                (k_gain, k_gains),
                (x_in, x_own),
                (w_query, wq.at[:, pl.ds(0, 128)]),
                (w_key, wk.at[:, pl.ds(0, 128)]),
                (w_value, wv.at[:, pl.ds(0, 128)]),
                (block_owner, owner),
                (block_fill, fill),
                (cache_keys.at[0], keys.at[0, pl.ds(0, blocks)]),
                (cache_values.at[0], values.at[0, pl.ds(0, blocks)]),
                (w_out, wo.at[:, 0]),
                (cache_keys.at[1], keys.at[1, pl.ds(0, blocks)]),
                (cache_values.at[1], values.at[1, pl.ds(0, blocks)]),
            ]
        )
    ]
    for copy in loads:
        copy.start()

    row16 = iota((16, 128), 0)
    lane16 = iota((16, 128), 1)
    sub8 = iota((8, 128), 0)
    lane8 = iota((8, 128), 1)

    def twice(t):
        return jnp.where(iota(t[0].shape, 0) < 4, t[0], pltpu.roll(t[1], 4, 0))

    loads[0].wait()
    loads[1].wait()
    length_row = lens[...].astype(F32)
    request_row = iota((8, total), 1).astype(F32)
    is_long = jnp.where(length_row > 128.0, 1.0, 0.0)
    before = jnp.where(iota((total, total), 0) < iota((total, total), 1), 1.0, 0.0).astype(BF16)
    rank = dot(jnp.broadcast_to(is_long, (8, total)).astype(BF16), before)
    slot8 = iota((8, total), 0)
    long_hot = jnp.where(
        (rank.astype(jnp.int32) == slot8) & (slot8 < 4),
        jnp.broadcast_to(is_long, (8, total)),
        0.0,
    )
    own_hot = jnp.where(iota((8, total), 1) == 8 * me + slot8, 1.0, 0.0)
    long_id = jnp.sum(long_hot * request_row, axis=1, keepdims=True)
    long_at = jnp.sum(long_hot * length_row, axis=1, keepdims=True)
    own_at = jnp.sum(own_hot * length_row, axis=1, keepdims=True)
    own_keep = jnp.where(own_at > 128.0, 0.0, 1.0)
    row_of = iota((total, 128), 1)
    to_half = jnp.where(
        (iota((total, 128), 0) == (row_of // 8) * 16 + 8 * core + row_of % 8) & (row_of < half),
        1.0,
        0.0,
    ).astype(BF16)
    long_half = dot(long_hot.astype(BF16), to_half)
    own_pick[...] = jnp.where(lane8 == 8 * chip + sub8, 1.0, 0.0)
    four = twice([long_half, long_half])
    eye = jnp.where(iota((half, 128), 0) == iota((half, 128), 1), 1.0, 0.0)
    spread[...] = dot_nt(
        eye.astype(BF16), jnp.concatenate([four, four], axis=0).astype(BF16)
    ).astype(BF16)
    long_sel = jnp.concatenate([long_half, jnp.zeros((8, 128), F32)], axis=0).astype(BF16)
    long_sel = long_sel[:, :half]
    chunk_sel = dot(
        long_sel,
        jnp.where(
            iota((half, part), 0) == my_part * part + iota((half, part), 1), 1.0, 0.0
        ).astype(BF16),
    ).astype(BF16)
    long_any = jnp.concatenate([long_hot, jnp.zeros((8, total), F32)], axis=0).astype(BF16)
    long_pick = jnp.where(lane16 == row16 % 4, 1.0, 0.0)

    def turns(at, cos_ref, sin_ref):
        angle = at * freq[...]
        rows = angle.shape[0]
        sin = jnp.sin(angle)
        cos_ref[...] = jnp.cos(angle)
        sin_ref[...] = jnp.where(iota((rows, 128), 1) < 64, -sin, sin)

    turns(own_at, own_cos, own_sin)
    at4 = twice([jnp.broadcast_to(long_at, (8, 128))] * 2)
    turns(jnp.concatenate([at4, at4], axis=0), long_cos, long_sin)

    def half_of(ref):
        rows = ref[...].astype(F32).reshape(n_chip, 2, 8, 128)
        return jnp.where(core == 0, rows[:, 0], rows[:, 1]).reshape(half, 128)

    loads[5].wait()
    x_first = half_of(x_own)
    long_first = dot(long_any, x_own[...])

    pl.semaphore_wait(barrier, len(peers) + len(z_far) + len(z_near) + 1)

    def remote(src, dst, send, recv, req, kv):
        return pltpu.make_async_remote_copy(
            src_ref=src,
            dst_ref=dst,
            send_sem=send,
            recv_sem=recv,
            device_id={"req": req, "kv": kv},
            device_id_type=MESH,
        )

    shares = [
        remote(src, dst, init_send.at[at], init_recv.at[at], sib, my_z)
        for at, (src, dst) in enumerate(
            [
                (x_in, x_sib),
                (norm_gain, gains.at[:, pl.ds(128, 128)]),
                (w_query.at[0], wq.at[0, pl.ds(128, 128)]),
                (w_key.at[0], wk.at[0, pl.ds(128, 128)]),
                (w_value.at[0], wv.at[0, pl.ds(128, 128)]),
                (w_out.at[0], wo.at[0, 1]),
                (w_query.at[1], wq.at[1, pl.ds(128, 128)]),
                (w_key.at[1], wk.at[1, pl.ds(128, 128)]),
                (w_value.at[1], wv.at[1, pl.ds(128, 128)]),
                (w_out.at[1], wo.at[1, 1]),
            ]
        )
    ]
    for copy in shares:
        copy.start()

    for at in (2, 3, 4, 6, 7, 8):
        loads[at].wait()
    shares[0].wait_recv()
    shares[1].wait_recv()
    x_half[0] = (
        jnp.concatenate([x_first, half_of(x_sib)], axis=1).astype(BF16).reshape(owners, part, 256)
    )
    long_x = jnp.concatenate([long_first, dot(long_any, x_sib[...])], axis=1)
    for at in (2, 3, 4):
        shares[at].wait_recv()

    def normed_turned(t, gain, cos, sin):
        t = t * lax.rsqrt(jnp.mean(t * t, axis=1, keepdims=True) + EPS) * gain
        return t * cos + pltpu.roll(t, 64, 1) * sin

    def arrived(ref, sem):
        pltpu.make_async_copy(ref, ref, sem).wait()

    def to_chips(pairs, layer):
        for to, req in zip(chips, peers):
            for src, dst, phase in pairs(to):
                remote(
                    src, dst, send_sem.at[layer, phase], recv_sem.at[layer, phase], req, my_z
                ).start()

    def to_sib(src, dst, phase, layer):
        copy = remote(
            src, dst, send_sem.at[layer, phase], recv_sem.at[layer, phase], sib, my_z
        )
        copy.start()
        return copy

    def as_row(column, mask):
        return jnp.sum(jnp.where(mask, column, 0.0), axis=0, keepdims=True)

    def softmax_mean(s, v):
        top = jnp.maximum(jnp.max(s, axis=1, keepdims=True), CEIL)
        p = jnp.exp(s - top)
        den = jnp.sum(p, axis=1, keepdims=True)
        num = dot(p.astype(BF16), v)
        level = jnp.where(den > 0.0, top + jnp.log(jnp.maximum(den, TINY)), FLOOR)
        return num / jnp.maximum(den, TINY), jnp.broadcast_to(level, (16, 128))

    logit = 1.0 / math.sqrt(128)
    others = pl.ds(0, n_chip - 1)
    on_diagonal = iota((half, 128), 0) == iota((half, 128), 1)

    def send_long(layer, long_x):
        square = jnp.sum(long_x * long_x, axis=1, keepdims=True)
        square_row = as_row(square, row16 == lane16)
        sl_s[layer] = square_row
        sl_r[layer, chip] = square_row
        gain = gains[pl.ds(layer, 1), :].astype(F32)
        q = dot((long_x * gain).astype(BF16), wq[layer])[0:8]
        q = [q[:, 128 * g : 128 * g + 128] for g in range(4)]
        q = jnp.concatenate([twice(q[0:2]), twice(q[2:4])], axis=0).astype(BF16)
        rl_s[layer] = q
        rl_r[layer, chip] = q
        to_chips(
            lambda to: [
                (rl_s.at[layer], rl_r.at[layer, chip], RL),
                (sl_s.at[layer], sl_r.at[layer, chip], SL),
            ],
            layer,
        )

    for layer in range(LAYERS):
        x = x_half[layer].reshape(half, 256)
        if layer == 1:
            for at in (6, 7, 8):
                shares[at].wait_recv()
            theirs = jnp.sum(xl_r[...].astype(F32), axis=0)
            long_x = dot(long_sel, x) + jnp.concatenate(
                [theirs[:, 128:256], theirs[:, 0:128]], axis=1
            )
        send_long(layer, long_x)
        x = x.astype(F32)
        square = jnp.sum(x * x, axis=1, keepdims=True)
        square_row = as_row(square, on_diagonal)
        sq_s[layer] = square_row
        sq_r[layer, chip] = square_row
        xg = (x * gains[pl.ds(layer, 1), :].astype(F32)).astype(BF16)
        q = dot(xg, wq[layer])
        upper = q[:, 0:384].reshape(n_chip, 8, 384)
        lower = jnp.concatenate(
            [q[:, 384:512], dot(xg, wk[layer]), dot(xg, wv[layer])], axis=1
        ).reshape(n_chip, 8, 384)
        rs_s[layer] = jnp.concatenate([upper, lower], axis=1).astype(BF16)
        to_chips(
            lambda to: [
                (rs_s.at[layer, to], rs_r.at[layer, chip], RS),
                (sq_s.at[layer], sq_r.at[layer, chip], SQ),
            ],
            layer,
        )
        rs_r[layer, chip] = rs_s[layer, chip]

        if layer == 0:
            loads[9].wait()
            loads[10].wait()

            def block_masks(b, carry):
                live = (lane8 < fill[b]) & (long_id == owner[b].astype(F32)) & (sub8 < 4)
                bias = jnp.where(live, 0.0, FLOOR)
                long_bias[:, pl.ds(pl.multiple_of(b * 128, 128), 128)] = twice([bias, bias])
                return carry

            lax.fori_loop(0, blocks, block_masks, 0)
            live = (long_id == (8 * me + lane8).astype(F32)) & (lane8 < 8) & (sub8 < 4)
            bias = jnp.where(live, 0.0, FLOOR)
            new_bias[...] = twice([bias, bias])
            for b in range(8):
                home_bias[:, pl.ds(b * 128, 128)] = jnp.where(
                    (sub8 == b) & (lane8 < fill[b]), 0.0, FLOOR
                )
            home_bias[:, pl.ds(1024, 128)] = jnp.where(sub8 == lane8, 0.0, FLOOR)
            zero = jnp.zeros((LAYERS, 128, 128), BF16)
            keys[:, blocks] = zero
            values[:, blocks] = zero
            loads[11].wait()
            loads[12].wait()
        else:
            loads[14].wait()
            loads[15].wait()

        q_gain_row = q_gains[pl.ds(layer, 1), :].astype(F32)
        arrived(sl_r.at[layer, others], recv_sem.at[layer, SL])
        arrived(rl_r.at[layer, others], recv_sem.at[layer, RL])
        scale = lax.rsqrt(
            jnp.sum(long_pick * jnp.sum(sl_r[layer], axis=0), axis=1, keepdims=True) / width
            + EPS
        )
        q_long = normed_turned(
            jnp.sum(rl_r[layer].astype(F32), axis=0) * scale,
            q_gain_row,
            long_cos[...],
            long_sin[...],
        ).astype(BF16)
        s = dot_nt(q_long, keys[layer, 0:blocks].reshape(blocks * 128, 128))
        s = s * logit + jnp.concatenate([long_bias[...]] * 2, axis=0)
        mean, level = softmax_mean(s, values[layer, 0:blocks].reshape(blocks * 128, 128))
        px_s[layer] = jnp.concatenate([mean, level], axis=0)
        p_share = to_sib(px_s.at[layer], px_r.at[layer], PX, layer)

        arrived(sq_r.at[layer, others], recv_sem.at[layer, SQ])
        arrived(rs_r.at[layer, others], recv_sem.at[layer, RS])
        sums = jnp.sum(rs_r[layer].astype(F32), axis=0)
        scale = lax.rsqrt(
            jnp.sum(own_pick[...] * jnp.sum(sq_r[layer], axis=0), axis=1, keepdims=True) / width
            + EPS
        )
        new_key = normed_turned(
            sums[8:16, 128:256] * scale,
            k_gains[pl.ds(layer, 1), :].astype(F32),
            own_cos[...],
            own_sin[...],
        )
        new_value = sums[8:16, 256:384] * scale
        pad = jnp.zeros((8, 128), F32)
        keys[layer, blocks, 0:16] = jnp.concatenate([new_key, pad], axis=0).astype(BF16)
        values[layer, blocks, 0:16] = jnp.concatenate([new_value, pad], axis=0).astype(BF16)
        out_keys[layer] = new_key.astype(BF16)
        out_values[layer] = new_value.astype(BF16)
        q_own = [
            normed_turned(t * scale, q_gain_row, own_cos[...], own_sin[...])
            for t in (
                sums[0:8, 0:128], sums[0:8, 128:256], sums[0:8, 256:384], sums[8:16, 0:128]
            )
        ]
        q_own = jnp.concatenate(q_own, axis=0).astype(BF16)

        s = dot_nt(q_long, keys[layer, blocks])
        s = s * logit + jnp.concatenate([new_bias[...]] * 2, axis=0)
        new_mean, new_level = softmax_mean(s, values[layer, blocks])

        s = jnp.concatenate(
            [
                dot_nt(q_own, keys[layer, 0:8].reshape(1024, 128)),
                dot_nt(q_own, keys[layer, blocks]),
            ],
            axis=1,
        )
        s = s * logit + jnp.concatenate([home_bias[...]] * 4, axis=0)
        p = jnp.exp(s - jnp.max(s, axis=1, keepdims=True))
        den = jnp.sum(p, axis=1, keepdims=True)
        p = p.astype(BF16)
        num = dot(p[:, 0:1024], values[layer, 0:8].reshape(1024, 128)) + dot(
            p[:, 1024:1152], values[layer, blocks]
        )
        attended = (num * (jnp.concatenate([own_keep] * 4, axis=0) / den)).astype(BF16)
        ho_s[layer] = attended
        ho_r[layer, chip] = attended
        to_chips(lambda to: [(ho_s.at[layer], ho_r.at[layer, chip], HO)], layer)

        p_share.wait_recv()
        other_mean, other_level = px_r[layer, 0:16], px_r[layer, 16:32]
        top = jnp.maximum(jnp.maximum(level, new_level), other_level)
        mine, fresh = jnp.exp(level - top), jnp.exp(new_level - top)
        theirs = jnp.exp(other_level - top)
        every = mine + fresh + theirs
        mean = ((mean * mine + new_mean * fresh + other_mean * theirs) / every).astype(BF16)
        level_row = as_row(top + jnp.log(every), row16 == lane16)
        lo_s[layer] = mean
        lo_r[layer, chip] = mean
        ll_s[layer] = level_row
        ll_r[layer, chip] = level_row
        to_chips(
            lambda to: [
                (lo_s.at[layer], lo_r.at[layer, chip], LO),
                (ll_s.at[layer], ll_r.at[layer, chip], LL),
            ],
            layer,
        )

        if layer == 0:
            loads[13].wait()
        shares[5 if layer == 0 else 9].wait_recv()
        arrived(ho_r.at[layer, others], recv_sem.at[layer, HO])
        homes = ho_r[layer].astype(F32)
        homes = jnp.concatenate(
            [homes[:, 8 * g : 8 * g + 8].reshape(half, 128) for g in range(4)], axis=1
        )
        arrived(ll_r.at[layer, others], recv_sem.at[layer, LL])
        levels = ll_r[layer]
        weight = jnp.exp(levels - jnp.max(levels, axis=0, keepdims=True))
        weight = weight / jnp.sum(weight, axis=0, keepdims=True)
        weight = jnp.sum(
            jnp.where(
                iota((n_chip, 16, 128), 1) == iota((n_chip, 16, 128), 2),
                jnp.broadcast_to(weight, (n_chip, 16, 128)),
                0.0,
            ),
            axis=2,
            keepdims=True,
        )
        arrived(lo_r.at[layer, others], recv_sem.at[layer, LO])
        merged = jnp.sum(weight * lo_r[layer].astype(F32), axis=0)
        merged = jnp.concatenate(
            [jnp.where(row16 // 4 == g, merged, 0.0) for g in range(4)], axis=1
        ).astype(BF16)
        attended = (homes + dot(spread[...], merged)).astype(BF16)

        branch = jnp.concatenate(
            [dot(attended, wo[layer, 0]), dot(attended, wo[layer, 1])], axis=1
        )
        zr_s[layer] = branch.astype(BF16).reshape(owners, part, 256)
        for d in z_far:
            remote(
                zr_s.at[layer, lax.rem(z_at[d], owners)], zr_r.at[layer, my_z],
                send_sem.at[layer, ZR], recv_sem.at[layer, ZR], me, z_at[d],
            ).start()
        zr_r[layer, my_z] = zr_s[layer, my_part]
        arrived(zr_r.at[layer, pl.ds(0, nz - 1)], recv_sem.at[layer, ZR])
        hidden = (
            x_half[layer, my_part].astype(F32) + jnp.sum(zr_r[layer].astype(F32), axis=0)
        ).astype(BF16)

        mid = part // 2
        rows_for = {1: (0, part), 7: (0, part), 6: (0, mid), 2: (mid, mid)}
        if layer + 1 < LAYERS:
            za_s[...] = hidden
            x_half[layer + 1, my_part] = hidden
            xl_s[...] = dot(chunk_sel, hidden).astype(BF16)
            for d in z_near:
                if d != 6:
                    remote(
                        xl_s, xl_r.at[my_part],
                        send_sem.at[layer, XL], recv_sem.at[layer, XL], sib, z_at[d],
                    ).start()
                rows = pl.ds(*rows_for[d])
                remote(
                    za_s.at[rows], x_half.at[layer + 1, my_part, rows],
                    send_sem.at[layer, ZA], recv_sem.at[layer, ZA], me, z_at[d],
                ).start()
            remote(
                xl_s, xl_r.at[my_part],
                send_sem.at[layer, XL], recv_sem.at[layer, XL], sib, my_z,
            ).start()
            if owners > 1:
                arrived(x_half.at[layer + 1, pl.ds(0, owners - 1)], recv_sem.at[layer, ZA])
            arrived(xl_r, recv_sem.at[layer, XL])
        else:
            fin_s[0] = hidden[:, 0:128]
            fin_s[1] = hidden[:, 128:256]
            start = pl.multiple_of(my_part * part, part)
            for d in z_near:
                first, count = rows_for[d]
                rows = pl.ds(first, count)
                to = out.at[core, pl.ds(pl.multiple_of(start + first, count), count)]
                remote(
                    fin_s.at[1, rows], to,
                    send_sem.at[layer, ZB], recv_sem.at[layer, ZB], sib, z_at[d],
                ).start()
                remote(
                    fin_s.at[0, rows], to,
                    send_sem.at[layer, ZA], recv_sem.at[layer, ZA], me, z_at[d],
                ).start()
            to = out.at[core, pl.ds(start, part)]
            remote(
                fin_s.at[1], to,
                send_sem.at[layer, ZB], recv_sem.at[layer, ZB], sib, my_z,
            ).start()
            out[core, pl.ds(start, part)] = hidden[:, 0:128]
            most = pl.ds(0, half - part)
            if owners > 1:
                arrived(out.at[core, most], recv_sem.at[layer, ZA])
            arrived(out.at[1 - core], recv_sem.at[layer, ZB])

    for copy in shares:
        copy.wait_send()
    for layer in range(LAYERS):
        for ref, phase in (
            (rs_r.at[layer, others], RS),
            (sq_r.at[layer, others], SQ),
            (rl_r.at[layer, others], RL),
            (sl_r.at[layer, others], SL),
            (px_r.at[layer], PX),
            (ho_r.at[layer, others], HO),
            (lo_r.at[layer, others], LO),
            (ll_r.at[layer, others], LL),
            (zr_r.at[layer, pl.ds(0, nz - 1)], ZR),
        ):
            arrived(ref, send_sem.at[layer, phase])
        if layer + 1 < LAYERS:
            arrived(xl_r, send_sem.at[layer, XL])
            if owners > 1:
                arrived(x_half.at[layer + 1, pl.ds(0, owners - 1)], send_sem.at[layer, ZA])
        else:
            if owners > 1:
                arrived(out.at[core, most], send_sem.at[layer, ZA])
            arrived(out.at[1 - core], send_sem.at[layer, ZB])


def finish(hidden, new_keys, new_values, out, out_keys, out_values, sem):
    copies = [
        pltpu.make_async_copy(hidden.at[0], out.at[:, 0], sem.at[0]),
        pltpu.make_async_copy(hidden.at[1], out.at[:, 1], sem.at[1]),
        pltpu.make_async_copy(new_keys, out_keys, sem.at[2]),
        pltpu.make_async_copy(new_values, out_values, sem.at[3]),
    ]
    for copy in copies:
        copy.start()
    for copy in copies:
        copy.wait()


def on_device(
    n_chip, side, nz, width,
    hidden_in, norm_gain, q_gain, k_gain, w_query, w_key, w_value, w_out,
    cache_keys, cache_values, lengths, block_owner, block_fill,
):
    half = 8 * n_chip
    owners = nz // 2
    part = half // owners
    blocks = cache_keys.shape[1]
    total = hidden_in.shape[0]
    heads = w_query.shape[2]
    exponent = np.concatenate([np.arange(64), np.arange(64)]) * 2.0 / 128
    frequency = jnp.asarray((THETA**-exponent).astype(np.float32)[None, :])
    vmem, sem = pltpu.VMEM, pltpu.SemaphoreType.DMA
    anywhere = pl.BlockSpec(memory_space=pl.ANY)
    both = (LAYERS, n_chip)
    onchip = pl.BlockSpec(memory_space=pltpu.VMEM)
    news = jax.ShapeDtypeStruct((LAYERS, 8, 128), BF16)
    chip_news = vmem((LAYERS, 8, 128), BF16)
    hidden, new_keys, new_values = pl.pallas_call(
        functools.partial(kernel, n_chip, side, nz, float(width)),
        out_shape=(vmem((2, half, 128), BF16), chip_news, chip_news),
        in_specs=[anywhere] * 14,
        out_specs=(onchip, onchip, onchip),
        scratch_shapes=[
            vmem((total, 128), BF16),
            vmem((total, 128), BF16),
            vmem((LAYERS, 256), BF16),
            vmem((LAYERS, 128), BF16),
            vmem((LAYERS, 128), BF16),
            vmem((LAYERS, 256, heads), BF16),
            vmem((LAYERS, 256, 128), BF16),
            vmem((LAYERS, 256, 128), BF16),
            vmem((LAYERS, 2, heads, 128), BF16),
            vmem((LAYERS, blocks + 1, 128, 128), BF16),
            vmem((LAYERS, blocks + 1, 128, 128), BF16),
            vmem((1, total), jnp.int32),
            pltpu.SMEM((blocks,), jnp.int32),
            pltpu.SMEM((blocks,), jnp.int32),
            vmem((1, 128), F32),
            vmem((LAYERS, owners, part, 256), BF16),
            vmem((8, blocks * 128), F32),
            vmem((8, 128), F32),
            vmem((8, 9 * 128), F32),
            vmem((8, 128), F32),
            vmem((8, 128), F32),
            vmem((16, 128), F32),
            vmem((16, 128), F32),
            vmem((8, 128), F32),
            vmem((half, 16), BF16),
            vmem((*both, 16, 384), BF16),
            vmem((*both, 16, 384), BF16),
            vmem((LAYERS, 1, 128), F32),
            vmem((*both, 1, 128), F32),
            vmem((LAYERS, 16, 128), BF16),
            vmem((*both, 16, 128), BF16),
            vmem((LAYERS, 1, 128), F32),
            vmem((*both, 1, 128), F32),
            vmem((16, 256), BF16),
            vmem((owners, 16, 256), BF16),
            vmem((LAYERS, 32, 128), F32),
            vmem((LAYERS, 32, 128), F32),
            vmem((LAYERS, 32, 128), BF16),
            vmem((*both, 32, 128), BF16),
            vmem((LAYERS, 16, 128), BF16),
            vmem((*both, 16, 128), BF16),
            vmem((LAYERS, 1, 128), F32),
            vmem((*both, 1, 128), F32),
            vmem((LAYERS, owners, part, 256), BF16),
            vmem((LAYERS, nz, part, 256), BF16),
            vmem((part, 256), BF16),
            vmem((2, part, 128), BF16),
            sem((16,)),
            sem((10,)),
            sem((10,)),
            sem((LAYERS, 12)),
            sem((LAYERS, 12)),
        ],
        compiler_params=pltpu.CompilerParams(
            collective_id=0, has_side_effects=True, vmem_limit_bytes=60000 * 1024
        ),
        name="attention_layers",
    )(
        hidden_in, norm_gain, q_gain, k_gain, w_query, w_key, w_value, w_out,
        cache_keys, cache_values, lengths.reshape(1, total), block_owner, block_fill, frequency,
    )
    out, new_keys, new_values = pl.pallas_call(
        finish,
        out_shape=(jax.ShapeDtypeStruct((n_chip, 2, 8, 128), BF16), news, news),
        in_specs=[onchip] * 3,
        out_specs=(anywhere, anywhere, anywhere),
        scratch_shapes=[sem((4,))],
        compiler_params=pltpu.CompilerParams(vmem_limit_bytes=1024 * 1024),
        name="finish",
    )(hidden.reshape(2, n_chip, 8, 128), new_keys, new_values)
    return out.reshape(total, 128), new_keys, new_values


def solution(mesh):
    n_req, nz = mesh.shape["req"], mesh.shape["kv"]
    n_chip = n_req // 2
    side = math.isqrt(n_chip)
    in_specs = (
        P(None, "req"),
        P(None, "req"),
        P(),
        P(),
        P(None, "req", "kv"),
        P(None, "req", "kv"),
        P(None, "req", "kv"),
        P(None, "kv", "req"),
        P(None, "req", None, "kv"),
        P(None, "req", None, "kv"),
        P(),
        P("req"),
        P("req"),
    )
    out_specs = (P(None, "req"), P(None, "req", "kv"), P(None, "req", "kv"))
    return jax.shard_map(
        functools.partial(on_device, n_chip, side, nz, 128 * n_req),
        mesh=mesh,
        in_specs=in_specs,
        out_specs=out_specs,
        check_vma=False,
    )
```

```python
import functools
import math

import jax
import jax.numpy as jnp
import numpy as np
from jax import lax
from jax.experimental import pallas as pl
from jax.experimental.pallas import tpu as pltpu
from jax.sharding import PartitionSpec as P

LAYERS = 2
EPS = 1e-06
THETA = 1000000.0
FLOOR = -1e30
CEIL = -1e29
TINY = 1e-30
MESH = pl.DeviceIdType.MESH
F32 = jnp.float32
BF16 = jnp.bfloat16

RS, SQ, RL, SL, LZ, LW, PX, HO, LL, ZR, ZA, ZB = range(12)


def dot(a, b):
    return jnp.dot(a, b, preferred_element_type=F32)


def dot_nt(a, b):
    return lax.dot_general(a, b, (((1,), (1,)), ((), ())), preferred_element_type=F32)


def iota(shape, dim):
    return lax.broadcasted_iota(jnp.int32, shape, dim)


def kernel(
    n_chip,
    side,
    nz,
    width,
    x_in, norm_gain, q_gain, k_gain, w_query, w_key, w_value, w_out,
    cache_keys, cache_values, lengths, block_owner, block_fill, frequency,
    out, out_keys, out_values,
    x_own, x_sib, gains, q_gains, k_gains, wq, wk, wv, wo, keys, values,
    lens, owner, fill, freq,
    x_half, long_bias, new_bias, home_bias, own_cos, own_sin, long_cos, long_sin, own_pick, spread,
    rs_s, rs_r, sq_s, sq_r, rl_s, rl_r, sl_s, sl_r, lz_s, lz_r, px_s, px_r,
    ho_s, ho_r, ll_s, ll_r, zr_s, zr_r, za_s, fin_s,
    load_sem, init_send, init_recv, send_sem, recv_sem,
):
    half = 8 * n_chip
    owners = nz // 2
    part = half // owners
    blocks = cache_keys.shape[1]
    total = lens.shape[1]
    me = lax.axis_index("req")
    my_z = lax.axis_index("kv")
    core = lax.rem(me, 2)
    chip = lax.div(me, 2)
    chip_x, chip_y = lax.div(chip, side), lax.rem(chip, side)
    sib = me + 1 - 2 * core
    my_part = lax.rem(my_z, owners)

    def ring(d, n):
        return min(d, n - d)

    steps = sorted(
        [(dx, dy) for dx in range(side) for dy in range(side) if dx or dy],
        key=lambda d: -ring(d[0], side) - ring(d[1], side),
    )
    at_x = [lax.rem(chip_x + d, side) * side for d in range(side)]
    at_y = [lax.rem(chip_y + d, side) for d in range(side)]
    chips = [at_x[dx] + at_y[dy] for dx, dy in steps]
    peers = [2 * c + core for c in chips]
    z_at = [lax.rem(my_z + d, nz) for d in range(nz)]
    z_far = sorted(range(1, nz), key=lambda d: -ring(d, nz))
    z_near = {8: (6, 2, 7, 1), 2: ()}[nz]

    barrier = pltpu.get_barrier_semaphore()

    def greet(req, kv):
        pl.semaphore_signal(
            barrier, inc=1, device_id={"req": req, "kv": kv}, device_id_type=MESH
        )

    for req in peers:
        greet(req, my_z)
    for d in z_far:
        greet(me, z_at[d])
        greet(sib, z_at[d])
    greet(sib, my_z)

    loads = [
        pltpu.make_async_copy(src, dst, load_sem.at[at])
        for at, (src, dst) in enumerate(
            [
                (lengths, lens),
                (frequency, freq),
                (norm_gain, gains.at[:, pl.ds(0, 128)]),
                (q_gain, q_gains),
                (k_gain, k_gains),
                (x_in, x_own),
                (w_query, wq.at[:, pl.ds(0, 128)]),
                (w_key, wk.at[:, pl.ds(0, 128)]),
                (w_value, wv.at[:, pl.ds(0, 128)]),
                (block_owner, owner),
                (block_fill, fill),
                (cache_keys.at[0], keys.at[0, pl.ds(0, blocks)]),
                (cache_values.at[0], values.at[0, pl.ds(0, blocks)]),
                (w_out, wo.at[:, 0]),
                (cache_keys.at[1], keys.at[1, pl.ds(0, blocks)]),
                (cache_values.at[1], values.at[1, pl.ds(0, blocks)]),
            ]
        )
    ]
    for copy in loads:
        copy.start()

    row16 = iota((16, 128), 0)
    lane16 = iota((16, 128), 1)
    sub8 = iota((8, 128), 0)
    lane8 = iota((8, 128), 1)

    def twice(t):
        return jnp.where(iota(t[0].shape, 0) < 4, t[0], pltpu.roll(t[1], 4, 0))

    loads[0].wait()
    loads[1].wait()
    length_row = lens[...].astype(F32)
    request_row = iota((8, total), 1).astype(F32)
    is_long = jnp.where(length_row > 128.0, 1.0, 0.0)
    before = jnp.where(iota((total, total), 0) < iota((total, total), 1), 1.0, 0.0).astype(BF16)
    rank = dot(jnp.broadcast_to(is_long, (8, total)).astype(BF16), before)
    slot8 = iota((8, total), 0)
    long_hot = jnp.where(
        (rank.astype(jnp.int32) == slot8) & (slot8 < 4),
        jnp.broadcast_to(is_long, (8, total)),
        0.0,
    )
    own_hot = jnp.where(iota((8, total), 1) == 8 * me + slot8, 1.0, 0.0)
    long_id = jnp.sum(long_hot * request_row, axis=1, keepdims=True)
    long_at = jnp.sum(long_hot * length_row, axis=1, keepdims=True)
    own_at = jnp.sum(own_hot * length_row, axis=1, keepdims=True)
    own_keep = jnp.where(own_at > 128.0, 0.0, 1.0)
    row_of = iota((total, 128), 1)
    to_half = jnp.where(
        (iota((total, 128), 0) == (row_of // 8) * 16 + 8 * core + row_of % 8) & (row_of < half),
        1.0,
        0.0,
    ).astype(BF16)
    long_half = dot(long_hot.astype(BF16), to_half)
    own_pick[...] = jnp.where(lane8 == 8 * chip + sub8, 1.0, 0.0)
    four = twice([long_half, long_half])
    eye = jnp.where(iota((half, 128), 0) == iota((half, 128), 1), 1.0, 0.0)
    spread[...] = dot_nt(
        eye.astype(BF16), jnp.concatenate([four, four], axis=0).astype(BF16)
    ).astype(BF16)
    long_sel = jnp.concatenate([long_half, jnp.zeros((8, 128), F32)], axis=0).astype(BF16)
    long_sel = long_sel[:, :half]
    long_any = jnp.concatenate([long_hot, jnp.zeros((8, total), F32)], axis=0).astype(BF16)
    long_pick = jnp.where(lane16 == row16 % 4, 1.0, 0.0)

    def turns(at, cos_ref, sin_ref):
        angle = at * freq[...]
        rows = angle.shape[0]
        sin = jnp.sin(angle)
        cos_ref[...] = jnp.cos(angle)
        sin_ref[...] = jnp.where(iota((rows, 128), 1) < 64, -sin, sin)

    turns(own_at, own_cos, own_sin)
    at4 = twice([jnp.broadcast_to(long_at, (8, 128))] * 2)
    turns(jnp.concatenate([at4, at4], axis=0), long_cos, long_sin)

    def half_of(ref):
        rows = ref[...].astype(F32).reshape(n_chip, 2, 8, 128)
        return jnp.where(core == 0, rows[:, 0], rows[:, 1]).reshape(half, 128)

    loads[5].wait()
    x_first = half_of(x_own)
    long_first = dot(long_any, x_own[...])

    pl.semaphore_wait(barrier, len(peers) + 2 * len(z_far) + 1)

    def remote(src, dst, send, recv, req, kv):
        return pltpu.make_async_remote_copy(
            src_ref=src,
            dst_ref=dst,
            send_sem=send,
            recv_sem=recv,
            device_id={"req": req, "kv": kv},
            device_id_type=MESH,
        )

    shares = [
        remote(src, dst, init_send.at[at], init_recv.at[at], sib, my_z)
        for at, (src, dst) in enumerate(
            [
                (x_in, x_sib),
                (norm_gain, gains.at[:, pl.ds(128, 128)]),
                (w_query.at[0], wq.at[0, pl.ds(128, 128)]),
                (w_key.at[0], wk.at[0, pl.ds(128, 128)]),
                (w_value.at[0], wv.at[0, pl.ds(128, 128)]),
                (w_out.at[0], wo.at[0, 1]),
                (w_query.at[1], wq.at[1, pl.ds(128, 128)]),
                (w_key.at[1], wk.at[1, pl.ds(128, 128)]),
                (w_value.at[1], wv.at[1, pl.ds(128, 128)]),
                (w_out.at[1], wo.at[1, 1]),
            ]
        )
    ]
    for copy in shares:
        copy.start()

    for at in (2, 3, 4, 6, 7, 8):
        loads[at].wait()
    shares[0].wait_recv()
    shares[1].wait_recv()
    x_half[0] = (
        jnp.concatenate([x_first, half_of(x_sib)], axis=1).astype(BF16).reshape(owners, part, 256)
    )
    long_x = jnp.concatenate([long_first, dot(long_any, x_sib[...])], axis=1)
    for at in (2, 3, 4):
        shares[at].wait_recv()

    def normed_turned(t, gain, cos, sin):
        t = t * lax.rsqrt(jnp.mean(t * t, axis=1, keepdims=True) + EPS) * gain
        return t * cos + pltpu.roll(t, 64, 1) * sin

    def arrived(ref, sem):
        pltpu.make_async_copy(ref, ref, sem).wait()

    def to_chips(pairs, layer):
        for to, req in zip(chips, peers):
            for src, dst, phase in pairs(to):
                remote(
                    src, dst, send_sem.at[layer, phase], recv_sem.at[layer, phase], req, my_z
                ).start()

    def to_sib(src, dst, phase, layer):
        copy = remote(
            src, dst, send_sem.at[layer, phase], recv_sem.at[layer, phase], sib, my_z
        )
        copy.start()
        return copy

    def as_row(column, mask):
        return jnp.sum(jnp.where(mask, column, 0.0), axis=0, keepdims=True)

    def softmax_mean(s, v):
        top = jnp.maximum(jnp.max(s, axis=1, keepdims=True), CEIL)
        p = jnp.exp(s - top)
        den = jnp.sum(p, axis=1, keepdims=True)
        num = dot(p.astype(BF16), v)
        level = jnp.where(den > 0.0, top + jnp.log(jnp.maximum(den, TINY)), FLOOR)
        return num / jnp.maximum(den, TINY), jnp.broadcast_to(level, (16, 128))

    logit = 1.0 / math.sqrt(128)
    others = pl.ds(0, n_chip - 1)
    on_diagonal = iota((half, 128), 0) == iota((half, 128), 1)

    def send_long(layer, long_x):
        square = jnp.sum(long_x * long_x, axis=1, keepdims=True)
        square_row = as_row(square, row16 == lane16)
        sl_s[layer] = square_row
        sl_r[layer, chip] = square_row
        gain = gains[pl.ds(layer, 1), :].astype(F32)
        q = dot((long_x * gain).astype(BF16), wq[layer])[0:8]
        q = [q[:, 128 * g : 128 * g + 128] for g in range(4)]
        q = jnp.concatenate([twice(q[0:2]), twice(q[2:4])], axis=0).astype(BF16)
        rl_s[layer] = q
        rl_r[layer, chip] = q
        to_chips(
            lambda to: [
                (rl_s.at[layer], rl_r.at[layer, chip], RL),
                (sl_s.at[layer], sl_r.at[layer, chip], SL),
            ],
            layer,
        )

    for layer in range(LAYERS):
        x = x_half[layer].reshape(half, 256)
        if layer == 0:
            send_long(layer, long_x)
        x = x.astype(F32)
        square = jnp.sum(x * x, axis=1, keepdims=True)
        square_row = as_row(square, on_diagonal)
        sq_s[layer] = square_row
        sq_r[layer, chip] = square_row
        xg = (x * gains[pl.ds(layer, 1), :].astype(F32)).astype(BF16)
        q = dot(xg, wq[layer])
        upper = q[:, 0:384].reshape(n_chip, 8, 384)
        lower = jnp.concatenate(
            [q[:, 384:512], dot(xg, wk[layer]), dot(xg, wv[layer])], axis=1
        ).reshape(n_chip, 8, 384)
        rs_s[layer] = jnp.concatenate([upper, lower], axis=1).astype(BF16)
        to_chips(
            lambda to: [
                (rs_s.at[layer, to], rs_r.at[layer, chip], RS),
                (sq_s.at[layer], sq_r.at[layer, chip], SQ),
            ],
            layer,
        )
        rs_r[layer, chip] = rs_s[layer, chip]

        if layer == 0:
            loads[9].wait()
            loads[10].wait()

            def block_masks(b, carry):
                live = (lane8 < fill[b]) & (long_id == owner[b].astype(F32)) & (sub8 < 4)
                bias = jnp.where(live, 0.0, FLOOR)
                long_bias[:, pl.ds(pl.multiple_of(b * 128, 128), 128)] = twice([bias, bias])
                return carry

            lax.fori_loop(0, blocks, block_masks, 0)
            live = (long_id == (8 * me + lane8).astype(F32)) & (lane8 < 8) & (sub8 < 4)
            bias = jnp.where(live, 0.0, FLOOR)
            new_bias[...] = twice([bias, bias])
            for b in range(8):
                home_bias[:, pl.ds(b * 128, 128)] = jnp.where(
                    (sub8 == b) & (lane8 < fill[b]), 0.0, FLOOR
                )
            home_bias[:, pl.ds(1024, 128)] = jnp.where(sub8 == lane8, 0.0, FLOOR)
            zero = jnp.zeros((LAYERS, 128, 128), BF16)
            keys[:, blocks] = zero
            values[:, blocks] = zero
            loads[11].wait()
            loads[12].wait()
        else:
            loads[14].wait()
            loads[15].wait()

        q_gain_row = q_gains[pl.ds(layer, 1), :].astype(F32)
        arrived(sl_r.at[layer, others], recv_sem.at[layer, SL])
        arrived(rl_r.at[layer, others], recv_sem.at[layer, RL])
        scale = lax.rsqrt(
            jnp.sum(long_pick * jnp.sum(sl_r[layer], axis=0), axis=1, keepdims=True) / width
            + EPS
        )
        q_long = normed_turned(
            jnp.sum(rl_r[layer].astype(F32), axis=0) * scale,
            q_gain_row,
            long_cos[...],
            long_sin[...],
        ).astype(BF16)
        s = dot_nt(q_long, keys[layer, 0:blocks].reshape(blocks * 128, 128))
        s = s * logit + jnp.concatenate([long_bias[...]] * 2, axis=0)
        mean, level = softmax_mean(s, values[layer, 0:blocks].reshape(blocks * 128, 128))
        px_s[layer] = jnp.concatenate([mean, level], axis=0)
        p_share = to_sib(px_s.at[layer], px_r.at[layer], PX, layer)

        arrived(sq_r.at[layer, others], recv_sem.at[layer, SQ])
        arrived(rs_r.at[layer, others], recv_sem.at[layer, RS])
        sums = jnp.sum(rs_r[layer].astype(F32), axis=0)
        scale = lax.rsqrt(
            jnp.sum(own_pick[...] * jnp.sum(sq_r[layer], axis=0), axis=1, keepdims=True) / width
            + EPS
        )
        new_key = normed_turned(
            sums[8:16, 128:256] * scale,
            k_gains[pl.ds(layer, 1), :].astype(F32),
            own_cos[...],
            own_sin[...],
        )
        new_value = sums[8:16, 256:384] * scale
        pad = jnp.zeros((8, 128), F32)
        keys[layer, blocks, 0:16] = jnp.concatenate([new_key, pad], axis=0).astype(BF16)
        values[layer, blocks, 0:16] = jnp.concatenate([new_value, pad], axis=0).astype(BF16)
        out_keys[layer] = new_key.astype(BF16)
        out_values[layer] = new_value.astype(BF16)
        q_own = [
            normed_turned(t * scale, q_gain_row, own_cos[...], own_sin[...])
            for t in (
                sums[0:8, 0:128], sums[0:8, 128:256], sums[0:8, 256:384], sums[8:16, 0:128]
            )
        ]
        q_own = jnp.concatenate(q_own, axis=0).astype(BF16)

        s = dot_nt(q_long, keys[layer, blocks])
        s = s * logit + jnp.concatenate([new_bias[...]] * 2, axis=0)
        new_mean, new_level = softmax_mean(s, values[layer, blocks])

        s = jnp.concatenate(
            [
                dot_nt(q_own, keys[layer, 0:8].reshape(1024, 128)),
                dot_nt(q_own, keys[layer, blocks]),
            ],
            axis=1,
        )
        s = s * logit + jnp.concatenate([home_bias[...]] * 4, axis=0)
        p = jnp.exp(s - jnp.max(s, axis=1, keepdims=True))
        den = jnp.sum(p, axis=1, keepdims=True)
        p = p.astype(BF16)
        num = dot(p[:, 0:1024], values[layer, 0:8].reshape(1024, 128)) + dot(
            p[:, 1024:1152], values[layer, blocks]
        )
        attended = (num * (jnp.concatenate([own_keep] * 4, axis=0) / den)).astype(BF16)
        ho_s[layer, 0:32] = attended
        ho_r[layer, chip, 0:32] = attended

        p_share.wait_recv()
        other_mean, other_level = px_r[layer, 0:16], px_r[layer, 16:32]
        top = jnp.maximum(jnp.maximum(level, new_level), other_level)
        mine, fresh = jnp.exp(level - top), jnp.exp(new_level - top)
        theirs = jnp.exp(other_level - top)
        every = mine + fresh + theirs
        mean = ((mean * mine + new_mean * fresh + other_mean * theirs) / every).astype(BF16)
        level_row = as_row(top + jnp.log(every), row16 == lane16)
        ho_s[layer, 32:48] = mean
        ho_r[layer, chip, 32:48] = mean
        ll_s[layer] = level_row
        ll_r[layer, chip] = level_row
        to_chips(
            lambda to: [
                (ho_s.at[layer], ho_r.at[layer, chip], HO),
                (ll_s.at[layer], ll_r.at[layer, chip], LL),
            ],
            layer,
        )

        if layer == 0:
            loads[13].wait()
        shares[5 if layer == 0 else 9].wait_recv()
        arrived(ho_r.at[layer, others], recv_sem.at[layer, HO])
        homes = ho_r[layer, :, 0:32].astype(F32)
        homes = jnp.concatenate(
            [homes[:, 8 * g : 8 * g + 8].reshape(half, 128) for g in range(4)], axis=1
        )
        arrived(ll_r.at[layer, others], recv_sem.at[layer, LL])
        levels = ll_r[layer]
        weight = jnp.exp(levels - jnp.max(levels, axis=0, keepdims=True))
        weight = weight / jnp.sum(weight, axis=0, keepdims=True)
        weight = jnp.sum(
            jnp.where(
                iota((n_chip, 16, 128), 1) == iota((n_chip, 16, 128), 2),
                jnp.broadcast_to(weight, (n_chip, 16, 128)),
                0.0,
            ),
            axis=2,
            keepdims=True,
        )
        merged = jnp.sum(weight * ho_r[layer, :, 32:48].astype(F32), axis=0)
        merged = jnp.concatenate(
            [jnp.where(row16 // 4 == g, merged, 0.0) for g in range(4)], axis=1
        ).astype(BF16)
        attended = (homes + dot(spread[...], merged)).astype(BF16)

        branch = jnp.concatenate(
            [dot(attended, wo[layer, 0]), dot(attended, wo[layer, 1])], axis=1
        )
        branch = branch.astype(BF16)
        zr_s[layer] = branch.reshape(owners, part, 256)
        if layer + 1 < LAYERS:
            long_branch = dot(long_sel, branch).astype(BF16)
            lz_s[...] = long_branch
            lz_r[0, my_z] = long_branch
        for d in z_far:
            remote(
                zr_s.at[layer, lax.rem(z_at[d], owners)], zr_r.at[layer, my_z],
                send_sem.at[layer, ZR], recv_sem.at[layer, ZR], me, z_at[d],
            ).start()
        if layer + 1 < LAYERS:
            for d in z_far:
                remote(
                    lz_s, lz_r.at[0, my_z],
                    send_sem.at[layer, LZ], recv_sem.at[layer, LZ], me, z_at[d],
                ).start()
                remote(
                    lz_s, lz_r.at[1, my_z],
                    send_sem.at[layer, LW], recv_sem.at[layer, LW], sib, z_at[d],
                ).start()
            remote(
                lz_s, lz_r.at[1, my_z],
                send_sem.at[layer, LW], recv_sem.at[layer, LW], sib, my_z,
            ).start()
        zr_r[layer, my_z] = zr_s[layer, my_part]
        arrived(zr_r.at[layer, pl.ds(0, nz - 1)], recv_sem.at[layer, ZR])
        hidden = (
            x_half[layer, my_part].astype(F32) + jnp.sum(zr_r[layer].astype(F32), axis=0)
        ).astype(BF16)

        mid = part // 2
        rows_for = {1: (0, part), 7: (0, part), 6: (0, mid), 2: (mid, mid)}
        if layer + 1 < LAYERS:
            za_s[...] = hidden
            x_half[layer + 1, my_part] = hidden
            for d in z_near:
                rows = pl.ds(*rows_for[d])
                remote(
                    za_s.at[rows], x_half.at[layer + 1, my_part, rows],
                    send_sem.at[layer, ZA], recv_sem.at[layer, ZA], me, z_at[d],
                ).start()
            arrived(lz_r.at[0, pl.ds(0, nz - 1)], recv_sem.at[layer, LZ])
            arrived(lz_r.at[1], recv_sem.at[layer, LW])
            theirs = jnp.sum(lz_r[1].astype(F32), axis=0)
            long_x = long_x + (
                jnp.sum(lz_r[0].astype(F32), axis=0)
                + jnp.concatenate([theirs[:, 128:256], theirs[:, 0:128]], axis=1)
            )
            for at in (6, 7, 8):
                shares[at].wait_recv()
            send_long(layer + 1, long_x.astype(BF16).astype(F32))
            if owners > 1:
                arrived(x_half.at[layer + 1, pl.ds(0, owners - 1)], recv_sem.at[layer, ZA])
        else:
            fin_s[0] = hidden[:, 0:128]
            fin_s[1] = hidden[:, 128:256]
            start = pl.multiple_of(my_part * part, part)
            for d in z_near:
                first, count = rows_for[d]
                rows = pl.ds(first, count)
                to = out.at[core, pl.ds(pl.multiple_of(start + first, count), count)]
                remote(
                    fin_s.at[1, rows], to,
                    send_sem.at[layer, ZB], recv_sem.at[layer, ZB], sib, z_at[d],
                ).start()
                remote(
                    fin_s.at[0, rows], to,
                    send_sem.at[layer, ZA], recv_sem.at[layer, ZA], me, z_at[d],
                ).start()
            to = out.at[core, pl.ds(start, part)]
            remote(
                fin_s.at[1], to,
                send_sem.at[layer, ZB], recv_sem.at[layer, ZB], sib, my_z,
            ).start()
            out[core, pl.ds(start, part)] = hidden[:, 0:128]
            most = pl.ds(0, half - part)
            if owners > 1:
                arrived(out.at[core, most], recv_sem.at[layer, ZA])
            arrived(out.at[1 - core], recv_sem.at[layer, ZB])

    for copy in shares:
        copy.wait_send()
    for layer in range(LAYERS):
        for ref, phase in (
            (rs_r.at[layer, others], RS),
            (sq_r.at[layer, others], SQ),
            (rl_r.at[layer, others], RL),
            (sl_r.at[layer, others], SL),
            (px_r.at[layer], PX),
            (ho_r.at[layer, others], HO),
            (ll_r.at[layer, others], LL),
            (zr_r.at[layer, pl.ds(0, nz - 1)], ZR),
        ):
            arrived(ref, send_sem.at[layer, phase])
        if layer + 1 < LAYERS:
            arrived(lz_r.at[0, pl.ds(0, nz - 1)], send_sem.at[layer, LZ])
            arrived(lz_r.at[1], send_sem.at[layer, LW])
            if owners > 1:
                arrived(x_half.at[layer + 1, pl.ds(0, owners - 1)], send_sem.at[layer, ZA])
        else:
            if owners > 1:
                arrived(out.at[core, most], send_sem.at[layer, ZA])
            arrived(out.at[1 - core], send_sem.at[layer, ZB])


def finish(hidden, new_keys, new_values, out, out_keys, out_values, sem):
    copies = [
        pltpu.make_async_copy(hidden.at[0], out.at[:, 0], sem.at[0]),
        pltpu.make_async_copy(hidden.at[1], out.at[:, 1], sem.at[1]),
        pltpu.make_async_copy(new_keys, out_keys, sem.at[2]),
        pltpu.make_async_copy(new_values, out_values, sem.at[3]),
    ]
    for copy in copies:
        copy.start()
    for copy in copies:
        copy.wait()


def on_device(
    n_chip, side, nz, width,
    hidden_in, norm_gain, q_gain, k_gain, w_query, w_key, w_value, w_out,
    cache_keys, cache_values, lengths, block_owner, block_fill,
):
    half = 8 * n_chip
    owners = nz // 2
    part = half // owners
    blocks = cache_keys.shape[1]
    total = hidden_in.shape[0]
    heads = w_query.shape[2]
    exponent = np.concatenate([np.arange(64), np.arange(64)]) * 2.0 / 128
    frequency = jnp.asarray((THETA**-exponent).astype(np.float32)[None, :])
    vmem, sem = pltpu.VMEM, pltpu.SemaphoreType.DMA
    anywhere = pl.BlockSpec(memory_space=pl.ANY)
    both = (LAYERS, n_chip)
    onchip = pl.BlockSpec(memory_space=pltpu.VMEM)
    news = jax.ShapeDtypeStruct((LAYERS, 8, 128), BF16)
    chip_news = vmem((LAYERS, 8, 128), BF16)
    hidden, new_keys, new_values = pl.pallas_call(
        functools.partial(kernel, n_chip, side, nz, float(width)),
        out_shape=(vmem((2, half, 128), BF16), chip_news, chip_news),
        in_specs=[anywhere] * 14,
        out_specs=(onchip, onchip, onchip),
        scratch_shapes=[
            vmem((total, 128), BF16),
            vmem((total, 128), BF16),
            vmem((LAYERS, 256), BF16),
            vmem((LAYERS, 128), BF16),
            vmem((LAYERS, 128), BF16),
            vmem((LAYERS, 256, heads), BF16),
            vmem((LAYERS, 256, 128), BF16),
            vmem((LAYERS, 256, 128), BF16),
            vmem((LAYERS, 2, heads, 128), BF16),
            vmem((LAYERS, blocks + 1, 128, 128), BF16),
            vmem((LAYERS, blocks + 1, 128, 128), BF16),
            vmem((1, total), jnp.int32),
            pltpu.SMEM((blocks,), jnp.int32),
            pltpu.SMEM((blocks,), jnp.int32),
            vmem((1, 128), F32),
            vmem((LAYERS, owners, part, 256), BF16),
            vmem((8, blocks * 128), F32),
            vmem((8, 128), F32),
            vmem((8, 9 * 128), F32),
            vmem((8, 128), F32),
            vmem((8, 128), F32),
            vmem((16, 128), F32),
            vmem((16, 128), F32),
            vmem((8, 128), F32),
            vmem((half, 16), BF16),
            vmem((*both, 16, 384), BF16),
            vmem((*both, 16, 384), BF16),
            vmem((LAYERS, 1, 128), F32),
            vmem((*both, 1, 128), F32),
            vmem((LAYERS, 16, 128), BF16),
            vmem((*both, 16, 128), BF16),
            vmem((LAYERS, 1, 128), F32),
            vmem((*both, 1, 128), F32),
            vmem((16, 256), BF16),
            vmem((2, nz, 16, 256), BF16),
            vmem((LAYERS, 32, 128), F32),
            vmem((LAYERS, 32, 128), F32),
            vmem((LAYERS, 48, 128), BF16),
            vmem((*both, 48, 128), BF16),
            vmem((LAYERS, 1, 128), F32),
            vmem((*both, 1, 128), F32),
            vmem((LAYERS, owners, part, 256), BF16),
            vmem((LAYERS, nz, part, 256), BF16),
            vmem((part, 256), BF16),
            vmem((2, part, 128), BF16),
            sem((16,)),
            sem((10,)),
            sem((10,)),
            sem((LAYERS, 12)),
            sem((LAYERS, 12)),
        ],
        compiler_params=pltpu.CompilerParams(
            collective_id=0, has_side_effects=True, vmem_limit_bytes=60000 * 1024
        ),
        name="attention_layers",
    )(
        hidden_in, norm_gain, q_gain, k_gain, w_query, w_key, w_value, w_out,
        cache_keys, cache_values, lengths.reshape(1, total), block_owner, block_fill, frequency,
    )
    out, new_keys, new_values = pl.pallas_call(
        finish,
        out_shape=(jax.ShapeDtypeStruct((n_chip, 2, 8, 128), BF16), news, news),
        in_specs=[onchip] * 3,
        out_specs=(anywhere, anywhere, anywhere),
        scratch_shapes=[sem((4,))],
        compiler_params=pltpu.CompilerParams(vmem_limit_bytes=1024 * 1024),
        name="finish",
    )(hidden.reshape(2, n_chip, 8, 128), new_keys, new_values)
    return out.reshape(total, 128), new_keys, new_values


def solution(mesh):
    n_req, nz = mesh.shape["req"], mesh.shape["kv"]
    n_chip = n_req // 2
    side = math.isqrt(n_chip)
    in_specs = (
        P(None, "req"),
        P(None, "req"),
        P(),
        P(),
        P(None, "req", "kv"),
        P(None, "req", "kv"),
        P(None, "req", "kv"),
        P(None, "kv", "req"),
        P(None, "req", None, "kv"),
        P(None, "req", None, "kv"),
        P(),
        P("req"),
        P("req"),
    )
    out_specs = (P(None, "req"), P(None, "req", "kv"), P(None, "req", "kv"))
    return jax.shard_map(
        functools.partial(on_device, n_chip, side, nz, 128 * n_req),
        mesh=mesh,
        in_specs=in_specs,
        out_specs=out_specs,
        check_vma=False,
    )
```

```python
import functools
import math

import jax
import jax.numpy as jnp
import numpy as np
from jax import lax
from jax.experimental import pallas as pl
from jax.experimental.pallas import tpu as pltpu
from jax.sharding import PartitionSpec as P

LAYERS = 2
EPS = 1e-06
THETA = 1000000.0
FLOOR = -1e30
CEIL = -1e29
TINY = 1e-30
MESH = pl.DeviceIdType.MESH
F32 = jnp.float32
BF16 = jnp.bfloat16

RS, SQ, RL, SL, LZ, LW, PX, HO, LL, ZR, ZA, ZB = range(12)


def dot(a, b):
    return jnp.dot(a, b, preferred_element_type=F32)


def dot_nt(a, b):
    return lax.dot_general(a, b, (((1,), (1,)), ((), ())), preferred_element_type=F32)


def iota(shape, dim):
    return lax.broadcasted_iota(jnp.int32, shape, dim)


def kernel(
    n_chip,
    side,
    nz,
    width,
    x_in, norm_gain, q_gain, k_gain, w_query, w_key, w_value, w_out,
    cache_keys, cache_values, lengths, block_owner, block_fill, frequency,
    out, out_keys, out_values,
    x_own, x_sib, gains, q_gains, k_gains, wq, wk, wv, wo, keys, values,
    lens, owner, fill, freq,
    x_half, long_bias, new_bias, home_bias, own_cos, own_sin, long_cos, long_sin, own_pick, spread,
    rs_s, rs_r, sq_s, sq_r, rl_s, rl_r, sl_s, sl_r, lz_s, lz_r, px_s, px_r,
    ho_s, ho_r, ll_s, ll_r, zr_s, zr_r, za_s, fin_s,
    load_sem, init_send, init_recv, send_sem, recv_sem,
):
    half = 8 * n_chip
    owners = nz // 2
    part = half // owners
    blocks = cache_keys.shape[1]
    total = lens.shape[1]
    me = lax.axis_index("req")
    my_z = lax.axis_index("kv")
    core = lax.rem(me, 2)
    chip = lax.div(me, 2)
    chip_x, chip_y = lax.div(chip, side), lax.rem(chip, side)
    sib = me + 1 - 2 * core
    my_part = lax.rem(my_z, owners)

    def ring(d, n):
        return min(d, n - d)

    steps = sorted(
        [(dx, dy) for dx in range(side) for dy in range(side) if dx or dy],
        key=lambda d: -ring(d[0], side) - ring(d[1], side),
    )
    at_x = [lax.rem(chip_x + d, side) * side for d in range(side)]
    at_y = [lax.rem(chip_y + d, side) for d in range(side)]
    chips = [at_x[dx] + at_y[dy] for dx, dy in steps]
    peers = [2 * c + core for c in chips]
    z_at = [lax.rem(my_z + d, nz) for d in range(nz)]
    z_far = sorted(range(1, nz), key=lambda d: -ring(d, nz))
    z_near = {8: (6, 2, 7, 1), 2: ()}[nz]

    barrier = pltpu.get_barrier_semaphore()

    def greet(req, kv):
        pl.semaphore_signal(
            barrier, inc=1, device_id={"req": req, "kv": kv}, device_id_type=MESH
        )

    for req in peers:
        greet(req, my_z)
    for d in z_far:
        greet(me, z_at[d])
        greet(sib, z_at[d])
    greet(sib, my_z)

    loads = [
        pltpu.make_async_copy(src, dst, load_sem.at[at])
        for at, (src, dst) in enumerate(
            [
                (lengths, lens),
                (frequency, freq),
                (norm_gain, gains.at[:, pl.ds(0, 128)]),
                (q_gain, q_gains),
                (k_gain, k_gains),
                (x_in, x_own),
                (w_query, wq.at[:, pl.ds(0, 128)]),
                (w_key, wk.at[:, pl.ds(0, 128)]),
                (w_value, wv.at[:, pl.ds(0, 128)]),
                (block_owner, owner),
                (block_fill, fill),
                (cache_keys.at[0], keys.at[0, pl.ds(0, blocks)]),
                (cache_values.at[0], values.at[0, pl.ds(0, blocks)]),
                (w_out, wo.at[:, 0]),
                (cache_keys.at[1], keys.at[1, pl.ds(0, blocks)]),
                (cache_values.at[1], values.at[1, pl.ds(0, blocks)]),
            ]
        )
    ]
    for copy in loads:
        copy.start()

    row16 = iota((16, 128), 0)
    lane16 = iota((16, 128), 1)
    sub8 = iota((8, 128), 0)
    lane8 = iota((8, 128), 1)

    def twice(t):
        return jnp.where(iota(t[0].shape, 0) < 4, t[0], pltpu.roll(t[1], 4, 0))

    loads[0].wait()
    loads[1].wait()
    length_row = lens[...].astype(F32)
    request_row = iota((8, total), 1).astype(F32)
    is_long = jnp.where(length_row > 128.0, 1.0, 0.0)
    before = jnp.where(iota((total, total), 0) < iota((total, total), 1), 1.0, 0.0).astype(BF16)
    rank = dot(jnp.broadcast_to(is_long, (8, total)).astype(BF16), before)
    slot8 = iota((8, total), 0)
    long_hot = jnp.where(
        (rank.astype(jnp.int32) == slot8) & (slot8 < 4),
        jnp.broadcast_to(is_long, (8, total)),
        0.0,
    )
    own_hot = jnp.where(iota((8, total), 1) == 8 * me + slot8, 1.0, 0.0)
    long_id = jnp.sum(long_hot * request_row, axis=1, keepdims=True)
    long_at = jnp.sum(long_hot * length_row, axis=1, keepdims=True)
    own_at = jnp.sum(own_hot * length_row, axis=1, keepdims=True)
    own_keep = jnp.where(own_at > 128.0, 0.0, 1.0)
    row_of = iota((total, 128), 1)
    to_half = jnp.where(
        (iota((total, 128), 0) == (row_of // 8) * 16 + 8 * core + row_of % 8) & (row_of < half),
        1.0,
        0.0,
    ).astype(BF16)
    long_half = dot(long_hot.astype(BF16), to_half)
    own_pick[...] = jnp.where(lane8 == 8 * chip + sub8, 1.0, 0.0)
    four = twice([long_half, long_half])
    eye = jnp.where(iota((half, 128), 0) == iota((half, 128), 1), 1.0, 0.0)
    spread[...] = dot_nt(
        eye.astype(BF16), jnp.concatenate([four, four], axis=0).astype(BF16)
    ).astype(BF16)
    long_sel = jnp.concatenate([long_half, jnp.zeros((8, 128), F32)], axis=0).astype(BF16)
    long_sel = long_sel[:, :half]
    long_any = jnp.concatenate([long_hot, jnp.zeros((8, total), F32)], axis=0).astype(BF16)
    long_pick = jnp.where(lane16 == row16 % 4, 1.0, 0.0)

    def turns(at, cos_ref, sin_ref):
        angle = at * freq[...]
        rows = angle.shape[0]
        sin = jnp.sin(angle)
        cos_ref[...] = jnp.cos(angle)
        sin_ref[...] = jnp.where(iota((rows, 128), 1) < 64, -sin, sin)

    turns(own_at, own_cos, own_sin)
    at4 = twice([jnp.broadcast_to(long_at, (8, 128))] * 2)
    turns(jnp.concatenate([at4, at4], axis=0), long_cos, long_sin)

    def half_of(ref):
        rows = ref[...].astype(F32).reshape(n_chip, 2, 8, 128)
        return jnp.where(core == 0, rows[:, 0], rows[:, 1]).reshape(half, 128)

    loads[5].wait()
    x_first = half_of(x_own)
    long_first = dot(long_any, x_own[...])

    pl.semaphore_wait(barrier, len(peers) + 2 * len(z_far) + 1)

    def remote(src, dst, send, recv, req, kv):
        return pltpu.make_async_remote_copy(
            src_ref=src,
            dst_ref=dst,
            send_sem=send,
            recv_sem=recv,
            device_id={"req": req, "kv": kv},
            device_id_type=MESH,
        )

    shares = [
        remote(src, dst, init_send.at[at], init_recv.at[at], sib, my_z)
        for at, (src, dst) in enumerate(
            [
                (x_in, x_sib),
                (norm_gain, gains.at[:, pl.ds(128, 128)]),
                (w_query.at[0], wq.at[0, pl.ds(128, 128)]),
                (w_key.at[0], wk.at[0, pl.ds(128, 128)]),
                (w_value.at[0], wv.at[0, pl.ds(128, 128)]),
                (w_out.at[0], wo.at[0, 1]),
                (w_query.at[1], wq.at[1, pl.ds(128, 128)]),
                (w_key.at[1], wk.at[1, pl.ds(128, 128)]),
                (w_value.at[1], wv.at[1, pl.ds(128, 128)]),
                (w_out.at[1], wo.at[1, 1]),
            ]
        )
    ]
    for copy in shares:
        copy.start()

    for at in (2, 3, 4, 6, 7, 8):
        loads[at].wait()
    shares[0].wait_recv()
    shares[1].wait_recv()
    x_half[0] = (
        jnp.concatenate([x_first, half_of(x_sib)], axis=1).astype(BF16).reshape(owners, part, 256)
    )
    long_x = jnp.concatenate([long_first, dot(long_any, x_sib[...])], axis=1)
    for at in (2, 3, 4):
        shares[at].wait_recv()

    def normed_turned(t, gain, cos, sin):
        t = t * lax.rsqrt(jnp.mean(t * t, axis=1, keepdims=True) + EPS) * gain
        return t * cos + pltpu.roll(t, 64, 1) * sin

    def arrived(ref, sem):
        pltpu.make_async_copy(ref, ref, sem).wait()

    def to_chips(pairs, layer):
        for to, req in zip(chips, peers):
            for src, dst, phase in pairs(to):
                remote(
                    src, dst, send_sem.at[layer, phase], recv_sem.at[layer, phase], req, my_z
                ).start()

    def to_sib(src, dst, phase, layer):
        copy = remote(
            src, dst, send_sem.at[layer, phase], recv_sem.at[layer, phase], sib, my_z
        )
        copy.start()
        return copy

    def as_row(column, mask):
        return jnp.sum(jnp.where(mask, column, 0.0), axis=0, keepdims=True)

    def softmax_mean(s, v):
        top = jnp.maximum(jnp.max(s, axis=1, keepdims=True), CEIL)
        p = jnp.exp(s - top)
        den = jnp.sum(p, axis=1, keepdims=True)
        num = dot(p.astype(BF16), v)
        level = jnp.where(den > 0.0, top + jnp.log(jnp.maximum(den, TINY)), FLOOR)
        return num / jnp.maximum(den, TINY), jnp.broadcast_to(level, (16, 128))

    logit = 1.0 / math.sqrt(128)
    others = pl.ds(0, n_chip - 1)
    on_diagonal = iota((half, 128), 0) == iota((half, 128), 1)

    def send_long(layer, long_x):
        square = jnp.sum(long_x * long_x, axis=1, keepdims=True)
        square_row = as_row(square, row16 == lane16)
        sl_s[layer] = square_row
        sl_r[layer, chip] = square_row
        gain = gains[pl.ds(layer, 1), :].astype(F32)
        q = dot((long_x * gain).astype(BF16), wq[layer])[0:8]
        q = [q[:, 128 * g : 128 * g + 128] for g in range(4)]
        q = jnp.concatenate([twice(q[0:2]), twice(q[2:4])], axis=0).astype(BF16)
        rl_s[layer] = q
        rl_r[layer, chip] = q
        to_chips(
            lambda to: [
                (rl_s.at[layer], rl_r.at[layer, chip], RL),
                (sl_s.at[layer], sl_r.at[layer, chip], SL),
            ],
            layer,
        )

    for layer in range(LAYERS):
        x = x_half[layer].reshape(half, 256)
        if layer == 0:
            send_long(layer, long_x)
        x = x.astype(F32)
        square = jnp.sum(x * x, axis=1, keepdims=True)
        square_row = as_row(square, on_diagonal)
        sq_s[layer] = square_row
        sq_r[layer, chip] = square_row
        xg = (x * gains[pl.ds(layer, 1), :].astype(F32)).astype(BF16)
        q = dot(xg, wq[layer])
        upper = q[:, 0:384].reshape(n_chip, 8, 384)
        lower = jnp.concatenate(
            [q[:, 384:512], dot(xg, wk[layer]), dot(xg, wv[layer])], axis=1
        ).reshape(n_chip, 8, 384)
        rs_s[layer] = jnp.concatenate([upper, lower], axis=1).astype(BF16)
        to_chips(
            lambda to: [
                (rs_s.at[layer, to], rs_r.at[layer, chip], RS),
                (sq_s.at[layer], sq_r.at[layer, chip], SQ),
            ],
            layer,
        )
        rs_r[layer, chip] = rs_s[layer, chip]

        if layer == 0:
            loads[9].wait()
            loads[10].wait()

            def block_masks(b, carry):
                live = (lane8 < fill[b]) & (long_id == owner[b].astype(F32)) & (sub8 < 4)
                bias = jnp.where(live, 0.0, FLOOR)
                long_bias[:, pl.ds(pl.multiple_of(b * 128, 128), 128)] = twice([bias, bias])
                return carry

            lax.fori_loop(0, blocks, block_masks, 0)
            live = (long_id == (8 * me + lane8).astype(F32)) & (lane8 < 8) & (sub8 < 4)
            bias = jnp.where(live, 0.0, FLOOR)
            new_bias[...] = twice([bias, bias])
            for b in range(8):
                home_bias[:, pl.ds(b * 128, 128)] = jnp.where(
                    (sub8 == b) & (lane8 < fill[b]), 0.0, FLOOR
                )
            home_bias[:, pl.ds(1024, 128)] = jnp.where(sub8 == lane8, 0.0, FLOOR)
            zero = jnp.zeros((LAYERS, 128, 128), BF16)
            keys[:, blocks] = zero
            values[:, blocks] = zero
            loads[11].wait()
            loads[12].wait()
        else:
            loads[14].wait()
            loads[15].wait()

        q_gain_row = q_gains[pl.ds(layer, 1), :].astype(F32)
        arrived(sl_r.at[layer, others], recv_sem.at[layer, SL])
        arrived(rl_r.at[layer, others], recv_sem.at[layer, RL])
        scale = lax.rsqrt(
            jnp.sum(long_pick * jnp.sum(sl_r[layer], axis=0), axis=1, keepdims=True) / width
            + EPS
        )
        q_long = normed_turned(
            jnp.sum(rl_r[layer].astype(F32), axis=0) * scale,
            q_gain_row,
            long_cos[...],
            long_sin[...],
        ).astype(BF16)
        s = dot_nt(q_long, keys[layer, 0:blocks].reshape(blocks * 128, 128))
        s = s * logit + jnp.concatenate([long_bias[...]] * 2, axis=0)
        mean, level = softmax_mean(s, values[layer, 0:blocks].reshape(blocks * 128, 128))
        px_s[layer] = jnp.concatenate([mean, level], axis=0)
        p_share = to_sib(px_s.at[layer], px_r.at[layer], PX, layer)

        arrived(sq_r.at[layer, others], recv_sem.at[layer, SQ])
        arrived(rs_r.at[layer, others], recv_sem.at[layer, RS])
        sums = jnp.sum(rs_r[layer].astype(F32), axis=0)
        scale = lax.rsqrt(
            jnp.sum(own_pick[...] * jnp.sum(sq_r[layer], axis=0), axis=1, keepdims=True) / width
            + EPS
        )
        new_key = normed_turned(
            sums[8:16, 128:256] * scale,
            k_gains[pl.ds(layer, 1), :].astype(F32),
            own_cos[...],
            own_sin[...],
        )
        new_value = sums[8:16, 256:384] * scale
        pad = jnp.zeros((8, 128), F32)
        keys[layer, blocks, 0:16] = jnp.concatenate([new_key, pad], axis=0).astype(BF16)
        values[layer, blocks, 0:16] = jnp.concatenate([new_value, pad], axis=0).astype(BF16)
        out_keys[layer] = new_key.astype(BF16)
        out_values[layer] = new_value.astype(BF16)
        q_own = [
            normed_turned(t * scale, q_gain_row, own_cos[...], own_sin[...])
            for t in (
                sums[0:8, 0:128], sums[0:8, 128:256], sums[0:8, 256:384], sums[8:16, 0:128]
            )
        ]
        q_own = jnp.concatenate(q_own, axis=0).astype(BF16)

        s = dot_nt(q_long, keys[layer, blocks])
        s = s * logit + jnp.concatenate([new_bias[...]] * 2, axis=0)
        new_mean, new_level = softmax_mean(s, values[layer, blocks])

        s = jnp.concatenate(
            [
                dot_nt(q_own, keys[layer, 0:8].reshape(1024, 128)),
                dot_nt(q_own, keys[layer, blocks]),
            ],
            axis=1,
        )
        s = s * logit + jnp.concatenate([home_bias[...]] * 4, axis=0)
        p = jnp.exp(s - jnp.max(s, axis=1, keepdims=True))
        den = jnp.sum(p, axis=1, keepdims=True)
        p = p.astype(BF16)
        num = dot(p[:, 0:1024], values[layer, 0:8].reshape(1024, 128)) + dot(
            p[:, 1024:1152], values[layer, blocks]
        )
        attended = (num * (jnp.concatenate([own_keep] * 4, axis=0) / den)).astype(BF16)
        ho_s[layer, 0:32] = attended
        ho_r[layer, chip, 0:32] = attended

        p_share.wait_recv()
        other_mean, other_level = px_r[layer, 0:16], px_r[layer, 16:32]
        top = jnp.maximum(jnp.maximum(level, new_level), other_level)
        mine, fresh = jnp.exp(level - top), jnp.exp(new_level - top)
        theirs = jnp.exp(other_level - top)
        every = mine + fresh + theirs
        mean = ((mean * mine + new_mean * fresh + other_mean * theirs) / every).astype(BF16)
        level_row = as_row(top + jnp.log(every), row16 == lane16)
        ho_s[layer, 32:48] = mean
        ho_r[layer, chip, 32:48] = mean
        ll_s[layer] = level_row
        ll_r[layer, chip] = level_row
        to_chips(
            lambda to: [
                (ho_s.at[layer], ho_r.at[layer, chip], HO),
                (ll_s.at[layer], ll_r.at[layer, chip], LL),
            ],
            layer,
        )

        if layer == 0:
            loads[13].wait()
        shares[5 if layer == 0 else 9].wait_recv()
        arrived(ho_r.at[layer, others], recv_sem.at[layer, HO])
        homes = ho_r[layer, :, 0:32].astype(F32)
        homes = jnp.concatenate(
            [homes[:, 8 * g : 8 * g + 8].reshape(half, 128) for g in range(4)], axis=1
        )
        arrived(ll_r.at[layer, others], recv_sem.at[layer, LL])
        levels = ll_r[layer]
        weight = jnp.exp(levels - jnp.max(levels, axis=0, keepdims=True))
        weight = weight / jnp.sum(weight, axis=0, keepdims=True)
        weight = jnp.sum(
            jnp.where(
                iota((n_chip, 16, 128), 1) == iota((n_chip, 16, 128), 2),
                jnp.broadcast_to(weight, (n_chip, 16, 128)),
                0.0,
            ),
            axis=2,
            keepdims=True,
        )
        merged = jnp.sum(weight * ho_r[layer, :, 32:48].astype(F32), axis=0)
        merged = jnp.concatenate(
            [jnp.where(row16 // 4 == g, merged, 0.0) for g in range(4)], axis=1
        ).astype(BF16)
        attended = (homes + dot(spread[...], merged)).astype(BF16)

        branch = jnp.concatenate(
            [dot(attended, wo[layer, 0]), dot(attended, wo[layer, 1])], axis=1
        )
        branch = branch.astype(BF16)
        zr_s[layer] = branch.reshape(owners, part, 256)
        if layer + 1 < LAYERS:
            long_branch = dot(long_sel, branch)[0:8]
            long_branch = twice([long_branch[:, 0:128], long_branch[:, 128:256]]).astype(BF16)
            lz_s[...] = long_branch
            lz_r[0, my_z] = long_branch
        for d in z_far:
            remote(
                zr_s.at[layer, lax.rem(z_at[d], owners)], zr_r.at[layer, my_z],
                send_sem.at[layer, ZR], recv_sem.at[layer, ZR], me, z_at[d],
            ).start()
        if layer + 1 < LAYERS:
            for d in z_far:
                remote(
                    lz_s, lz_r.at[0, my_z],
                    send_sem.at[layer, LZ], recv_sem.at[layer, LZ], me, z_at[d],
                ).start()
                remote(
                    lz_s, lz_r.at[1, my_z],
                    send_sem.at[layer, LW], recv_sem.at[layer, LW], sib, z_at[d],
                ).start()
            remote(
                lz_s, lz_r.at[1, my_z],
                send_sem.at[layer, LW], recv_sem.at[layer, LW], sib, my_z,
            ).start()
        zr_r[layer, my_z] = zr_s[layer, my_part]
        arrived(zr_r.at[layer, pl.ds(0, nz - 1)], recv_sem.at[layer, ZR])
        hidden = (
            x_half[layer, my_part].astype(F32) + jnp.sum(zr_r[layer].astype(F32), axis=0)
        ).astype(BF16)

        mid = part // 2
        rows_for = {1: (0, part), 7: (0, part), 6: (0, mid), 2: (mid, mid)}
        if layer + 1 < LAYERS:
            za_s[...] = hidden
            x_half[layer + 1, my_part] = hidden
            for d in z_near:
                rows = pl.ds(*rows_for[d])
                remote(
                    za_s.at[rows], x_half.at[layer + 1, my_part, rows],
                    send_sem.at[layer, ZA], recv_sem.at[layer, ZA], me, z_at[d],
                ).start()
            arrived(lz_r.at[0, pl.ds(0, nz - 1)], recv_sem.at[layer, LZ])
            arrived(lz_r.at[1], recv_sem.at[layer, LW])
            mine = jnp.sum(lz_r[0].astype(F32), axis=0)
            theirs = jnp.sum(lz_r[1].astype(F32), axis=0)
            far = pltpu.roll(theirs, 4, 0)
            near = pltpu.roll(mine, 4, 0)
            gained = jnp.concatenate([mine + far, near + theirs], axis=1)
            gained = jnp.where(iota((8, 256), 0) < 4, gained, 0.0)
            long_x = long_x + jnp.concatenate([gained, jnp.zeros((8, 256), F32)], axis=0)
            for at in (6, 7, 8):
                shares[at].wait_recv()
            send_long(layer + 1, long_x.astype(BF16).astype(F32))
            if owners > 1:
                arrived(x_half.at[layer + 1, pl.ds(0, owners - 1)], recv_sem.at[layer, ZA])
        else:
            fin_s[0] = hidden[:, 0:128]
            fin_s[1] = hidden[:, 128:256]
            start = pl.multiple_of(my_part * part, part)
            for d in z_near:
                first, count = rows_for[d]
                rows = pl.ds(first, count)
                to = out.at[core, pl.ds(pl.multiple_of(start + first, count), count)]
                remote(
                    fin_s.at[1, rows], to,
                    send_sem.at[layer, ZB], recv_sem.at[layer, ZB], sib, z_at[d],
                ).start()
                remote(
                    fin_s.at[0, rows], to,
                    send_sem.at[layer, ZA], recv_sem.at[layer, ZA], me, z_at[d],
                ).start()
            to = out.at[core, pl.ds(start, part)]
            remote(
                fin_s.at[1], to,
                send_sem.at[layer, ZB], recv_sem.at[layer, ZB], sib, my_z,
            ).start()
            out[core, pl.ds(start, part)] = hidden[:, 0:128]
            most = pl.ds(0, half - part)
            if owners > 1:
                arrived(out.at[core, most], recv_sem.at[layer, ZA])
            arrived(out.at[1 - core], recv_sem.at[layer, ZB])

    for copy in shares:
        copy.wait_send()
    for layer in range(LAYERS):
        for ref, phase in (
            (rs_r.at[layer, others], RS),
            (sq_r.at[layer, others], SQ),
            (rl_r.at[layer, others], RL),
            (sl_r.at[layer, others], SL),
            (px_r.at[layer], PX),
            (ho_r.at[layer, others], HO),
            (ll_r.at[layer, others], LL),
            (zr_r.at[layer, pl.ds(0, nz - 1)], ZR),
        ):
            arrived(ref, send_sem.at[layer, phase])
        if layer + 1 < LAYERS:
            arrived(lz_r.at[0, pl.ds(0, nz - 1)], send_sem.at[layer, LZ])
            arrived(lz_r.at[1], send_sem.at[layer, LW])
            if owners > 1:
                arrived(x_half.at[layer + 1, pl.ds(0, owners - 1)], send_sem.at[layer, ZA])
        else:
            if owners > 1:
                arrived(out.at[core, most], send_sem.at[layer, ZA])
            arrived(out.at[1 - core], send_sem.at[layer, ZB])


def finish(hidden, new_keys, new_values, out, out_keys, out_values, sem):
    copies = [
        pltpu.make_async_copy(hidden.at[0], out.at[:, 0], sem.at[0]),
        pltpu.make_async_copy(hidden.at[1], out.at[:, 1], sem.at[1]),
        pltpu.make_async_copy(new_keys, out_keys, sem.at[2]),
        pltpu.make_async_copy(new_values, out_values, sem.at[3]),
    ]
    for copy in copies:
        copy.start()
    for copy in copies:
        copy.wait()


def on_device(
    n_chip, side, nz, width,
    hidden_in, norm_gain, q_gain, k_gain, w_query, w_key, w_value, w_out,
    cache_keys, cache_values, lengths, block_owner, block_fill,
):
    half = 8 * n_chip
    owners = nz // 2
    part = half // owners
    blocks = cache_keys.shape[1]
    total = hidden_in.shape[0]
    heads = w_query.shape[2]
    exponent = np.concatenate([np.arange(64), np.arange(64)]) * 2.0 / 128
    frequency = jnp.asarray((THETA**-exponent).astype(np.float32)[None, :])
    vmem, sem = pltpu.VMEM, pltpu.SemaphoreType.DMA
    anywhere = pl.BlockSpec(memory_space=pl.ANY)
    both = (LAYERS, n_chip)
    onchip = pl.BlockSpec(memory_space=pltpu.VMEM)
    news = jax.ShapeDtypeStruct((LAYERS, 8, 128), BF16)
    chip_news = vmem((LAYERS, 8, 128), BF16)
    hidden, new_keys, new_values = pl.pallas_call(
        functools.partial(kernel, n_chip, side, nz, float(width)),
        out_shape=(vmem((2, half, 128), BF16), chip_news, chip_news),
        in_specs=[anywhere] * 14,
        out_specs=(onchip, onchip, onchip),
        scratch_shapes=[
            vmem((total, 128), BF16),
            vmem((total, 128), BF16),
            vmem((LAYERS, 256), BF16),
            vmem((LAYERS, 128), BF16),
            vmem((LAYERS, 128), BF16),
            vmem((LAYERS, 256, heads), BF16),
            vmem((LAYERS, 256, 128), BF16),
            vmem((LAYERS, 256, 128), BF16),
            vmem((LAYERS, 2, heads, 128), BF16),
            vmem((LAYERS, blocks + 1, 128, 128), BF16),
            vmem((LAYERS, blocks + 1, 128, 128), BF16),
            vmem((1, total), jnp.int32),
            pltpu.SMEM((blocks,), jnp.int32),
            pltpu.SMEM((blocks,), jnp.int32),
            vmem((1, 128), F32),
            vmem((LAYERS, owners, part, 256), BF16),
            vmem((8, blocks * 128), F32),
            vmem((8, 128), F32),
            vmem((8, 9 * 128), F32),
            vmem((8, 128), F32),
            vmem((8, 128), F32),
            vmem((16, 128), F32),
            vmem((16, 128), F32),
            vmem((8, 128), F32),
            vmem((half, 16), BF16),
            vmem((*both, 16, 384), BF16),
            vmem((*both, 16, 384), BF16),
            vmem((LAYERS, 1, 128), F32),
            vmem((*both, 1, 128), F32),
            vmem((LAYERS, 16, 128), BF16),
            vmem((*both, 16, 128), BF16),
            vmem((LAYERS, 1, 128), F32),
            vmem((*both, 1, 128), F32),
            vmem((8, 128), BF16),
            vmem((2, nz, 8, 128), BF16),
            vmem((LAYERS, 32, 128), F32),
            vmem((LAYERS, 32, 128), F32),
            vmem((LAYERS, 48, 128), BF16),
            vmem((*both, 48, 128), BF16),
            vmem((LAYERS, 1, 128), F32),
            vmem((*both, 1, 128), F32),
            vmem((LAYERS, owners, part, 256), BF16),
            vmem((LAYERS, nz, part, 256), BF16),
            vmem((part, 256), BF16),
            vmem((2, part, 128), BF16),
            sem((16,)),
            sem((10,)),
            sem((10,)),
            sem((LAYERS, 12)),
            sem((LAYERS, 12)),
        ],
        compiler_params=pltpu.CompilerParams(
            collective_id=0, has_side_effects=True, vmem_limit_bytes=60000 * 1024
        ),
        name="attention_layers",
    )(
        hidden_in, norm_gain, q_gain, k_gain, w_query, w_key, w_value, w_out,
        cache_keys, cache_values, lengths.reshape(1, total), block_owner, block_fill, frequency,
    )
    out, new_keys, new_values = pl.pallas_call(
        finish,
        out_shape=(jax.ShapeDtypeStruct((n_chip, 2, 8, 128), BF16), news, news),
        in_specs=[onchip] * 3,
        out_specs=(anywhere, anywhere, anywhere),
        scratch_shapes=[sem((4,))],
        compiler_params=pltpu.CompilerParams(vmem_limit_bytes=1024 * 1024),
        name="finish",
    )(hidden.reshape(2, n_chip, 8, 128), new_keys, new_values)
    return out.reshape(total, 128), new_keys, new_values


def solution(mesh):
    n_req, nz = mesh.shape["req"], mesh.shape["kv"]
    n_chip = n_req // 2
    side = math.isqrt(n_chip)
    in_specs = (
        P(None, "req"),
        P(None, "req"),
        P(),
        P(),
        P(None, "req", "kv"),
        P(None, "req", "kv"),
        P(None, "req", "kv"),
        P(None, "kv", "req"),
        P(None, "req", None, "kv"),
        P(None, "req", None, "kv"),
        P(),
        P("req"),
        P("req"),
    )
    out_specs = (P(None, "req"), P(None, "req", "kv"), P(None, "req", "kv"))
    return jax.shard_map(
        functools.partial(on_device, n_chip, side, nz, 128 * n_req),
        mesh=mesh,
        in_specs=in_specs,
        out_specs=out_specs,
        check_vma=False,
    )
```

```python
import functools
import math

import jax
import jax.numpy as jnp
import numpy as np
from jax import lax
from jax.experimental import pallas as pl
from jax.experimental.pallas import tpu as pltpu
from jax.sharding import PartitionSpec as P

LAYERS = 2
EPS = 1e-06
THETA = 1000000.0
FLOOR = -1e30
CEIL = -1e29
TINY = 1e-30
MESH = pl.DeviceIdType.MESH
F32 = jnp.float32
BF16 = jnp.bfloat16

RS, SQ, RL, SL, LZ, LW, PX, HO, LL, ZR, ZA, ZB = range(12)


def dot(a, b):
    return jnp.dot(a, b, preferred_element_type=F32)


def dot_nt(a, b):
    return lax.dot_general(a, b, (((1,), (1,)), ((), ())), preferred_element_type=F32)


def iota(shape, dim):
    return lax.broadcasted_iota(jnp.int32, shape, dim)


def kernel(
    n_chip,
    side,
    nz,
    width,
    x_in, norm_gain, q_gain, k_gain, w_query, w_key, w_value, w_out,
    cache_keys, cache_values, lengths, block_owner, block_fill, frequency,
    out, out_keys, out_values,
    x_own, x_sib, gains, q_gains, k_gains, wq, wk, wv, wo, keys, values,
    lens, owner, fill, freq,
    x_half, long_bias, new_bias, home_bias, own_cos, own_sin, long_cos, long_sin, own_pick, spread,
    rs_s, rs_r, sq_s, sq_r, rl_s, rl_r, sl_s, sl_r, lz_s, lz_r, px_s, px_r,
    ho_s, ho_r, ll_s, ll_r, zr_s, zr_r, za_s, fin_s,
    load_sem, init_send, init_recv, send_sem, recv_sem,
):
    half = 8 * n_chip
    owners = nz // 2
    part = half // owners
    blocks = cache_keys.shape[1]
    total = lens.shape[1]
    me = lax.axis_index("req")
    my_z = lax.axis_index("kv")
    core = lax.rem(me, 2)
    chip = lax.div(me, 2)
    chip_x, chip_y = lax.div(chip, side), lax.rem(chip, side)
    sib = me + 1 - 2 * core
    my_part = lax.rem(my_z, owners)

    def ring(d, n):
        return min(d, n - d)

    steps = sorted(
        [(dx, dy) for dx in range(side) for dy in range(side) if dx or dy],
        key=lambda d: -ring(d[0], side) - ring(d[1], side),
    )
    at_x = [lax.rem(chip_x + d, side) * side for d in range(side)]
    at_y = [lax.rem(chip_y + d, side) for d in range(side)]
    chips = [at_x[dx] + at_y[dy] for dx, dy in steps]
    peers = [2 * c + core for c in chips]
    strangers = [2 * c + 1 - core for c in chips] + [sib]
    z_at = [lax.rem(my_z + d, nz) for d in range(nz)]
    z_far = sorted(range(1, nz), key=lambda d: -ring(d, nz))
    z_near = {8: (6, 2, 7, 1), 2: ()}[nz]

    barrier = pltpu.get_barrier_semaphore()

    def greet(req, kv):
        pl.semaphore_signal(
            barrier, inc=1, device_id={"req": req, "kv": kv}, device_id_type=MESH
        )

    for req in peers + strangers:
        greet(req, my_z)
    for d in z_far:
        greet(me, z_at[d])
        greet(sib, z_at[d])

    loads = [
        pltpu.make_async_copy(src, dst, load_sem.at[at])
        for at, (src, dst) in enumerate(
            [
                (lengths, lens),
                (frequency, freq),
                (norm_gain, gains.at[:, pl.ds(0, 128)]),
                (q_gain, q_gains),
                (k_gain, k_gains),
                (x_in, x_own),
                (w_query, wq.at[:, pl.ds(0, 128)]),
                (w_key, wk.at[:, pl.ds(0, 128)]),
                (w_value, wv.at[:, pl.ds(0, 128)]),
                (block_owner, owner),
                (block_fill, fill),
                (cache_keys.at[0], keys.at[0, pl.ds(0, blocks)]),
                (cache_values.at[0], values.at[0, pl.ds(0, blocks)]),
                (w_out, wo.at[:, 0]),
                (cache_keys.at[1], keys.at[1, pl.ds(0, blocks)]),
                (cache_values.at[1], values.at[1, pl.ds(0, blocks)]),
            ]
        )
    ]
    for copy in loads:
        copy.start()

    row16 = iota((16, 128), 0)
    lane16 = iota((16, 128), 1)
    sub8 = iota((8, 128), 0)
    lane8 = iota((8, 128), 1)

    def twice(t):
        return jnp.where(iota(t[0].shape, 0) < 4, t[0], pltpu.roll(t[1], 4, 0))

    loads[0].wait()
    loads[1].wait()
    length_row = lens[...].astype(F32)
    request_row = iota((8, total), 1).astype(F32)
    is_long = jnp.where(length_row > 128.0, 1.0, 0.0)
    before = jnp.where(iota((total, total), 0) < iota((total, total), 1), 1.0, 0.0).astype(BF16)
    rank = dot(jnp.broadcast_to(is_long, (8, total)).astype(BF16), before)
    slot8 = iota((8, total), 0)
    long_hot = jnp.where(
        (rank.astype(jnp.int32) == slot8) & (slot8 < 4),
        jnp.broadcast_to(is_long, (8, total)),
        0.0,
    )
    own_hot = jnp.where(iota((8, total), 1) == 8 * me + slot8, 1.0, 0.0)
    long_id = jnp.sum(long_hot * request_row, axis=1, keepdims=True)
    long_at = jnp.sum(long_hot * length_row, axis=1, keepdims=True)
    own_at = jnp.sum(own_hot * length_row, axis=1, keepdims=True)
    own_keep = jnp.where(own_at > 128.0, 0.0, 1.0)
    row_of = iota((total, 128), 1)
    to_half = jnp.where(
        (iota((total, 128), 0) == (row_of // 8) * 16 + 8 * core + row_of % 8) & (row_of < half),
        1.0,
        0.0,
    ).astype(BF16)
    long_half = dot(long_hot.astype(BF16), to_half)
    own_pick[...] = jnp.where(lane8 == 8 * chip + sub8, 1.0, 0.0)
    four = twice([long_half, long_half])
    eye = jnp.where(iota((half, 128), 0) == iota((half, 128), 1), 1.0, 0.0)
    spread[...] = dot_nt(
        eye.astype(BF16), jnp.concatenate([four, four], axis=0).astype(BF16)
    ).astype(BF16)
    long_sel = jnp.concatenate([long_half, jnp.zeros((8, 128), F32)], axis=0).astype(BF16)
    long_sel = long_sel[:, :half]
    long_any = jnp.concatenate([long_hot, jnp.zeros((8, total), F32)], axis=0).astype(BF16)
    long_pick = jnp.where(lane16 == row16 % 4, 1.0, 0.0)

    def turns(at, cos_ref, sin_ref):
        angle = at * freq[...]
        rows = angle.shape[0]
        sin = jnp.sin(angle)
        cos_ref[...] = jnp.cos(angle)
        sin_ref[...] = jnp.where(iota((rows, 128), 1) < 64, -sin, sin)

    turns(own_at, own_cos, own_sin)
    at4 = twice([jnp.broadcast_to(long_at, (8, 128))] * 2)
    turns(jnp.concatenate([at4, at4], axis=0), long_cos, long_sin)

    def half_of(ref):
        rows = ref[...].astype(F32).reshape(n_chip, 2, 8, 128)
        return jnp.where(core == 0, rows[:, 0], rows[:, 1]).reshape(half, 128)

    loads[5].wait()
    x_first = half_of(x_own)
    long_first = dot(long_any, x_own[...])

    def as_row(column, mask):
        return jnp.sum(jnp.where(mask, column, 0.0), axis=0, keepdims=True)

    def long_message(layer, rows, columns, slot):
        square = jnp.sum(rows * rows, axis=1, keepdims=True)
        square_row = as_row(square, row16 == lane16)
        sl_s[layer] = square_row
        sl_r[layer, slot] = square_row
        gain = gains[pl.ds(layer, 1), 0:columns].astype(F32)
        q = dot((rows * gain).astype(BF16), wq[layer, 0:columns])[0:8]
        q = [q[:, 128 * g : 128 * g + 128] for g in range(4)]
        q = jnp.concatenate([twice(q[0:2]), twice(q[2:4])], axis=0).astype(BF16)
        rl_s[layer] = q
        rl_r[layer, slot] = q

    loads[2].wait()
    loads[6].wait()
    long_message(0, long_first, 128, me)

    pl.semaphore_wait(barrier, len(peers) + len(strangers) + 2 * len(z_far))

    def remote(src, dst, send, recv, req, kv):
        return pltpu.make_async_remote_copy(
            src_ref=src,
            dst_ref=dst,
            send_sem=send,
            recv_sem=recv,
            device_id={"req": req, "kv": kv},
            device_id_type=MESH,
        )

    shares = [
        remote(src, dst, init_send.at[at], init_recv.at[at], sib, my_z)
        for at, (src, dst) in enumerate(
            [
                (x_in, x_sib),
                (norm_gain, gains.at[:, pl.ds(128, 128)]),
                (w_query.at[0], wq.at[0, pl.ds(128, 128)]),
                (w_key.at[0], wk.at[0, pl.ds(128, 128)]),
                (w_value.at[0], wv.at[0, pl.ds(128, 128)]),
                (w_out.at[0], wo.at[0, 1]),
                (w_query.at[1], wq.at[1, pl.ds(128, 128)]),
                (w_key.at[1], wk.at[1, pl.ds(128, 128)]),
                (w_value.at[1], wv.at[1, pl.ds(128, 128)]),
                (w_out.at[1], wo.at[1, 1]),
            ]
        )
    ]
    for copy in shares:
        copy.start()

    def send_long(layer, slot, everyone):
        for req in everyone:
            for src, dst, phase in (
                (rl_s.at[layer], rl_r.at[layer, slot], RL),
                (sl_s.at[layer], sl_r.at[layer, slot], SL),
            ):
                remote(
                    src, dst, send_sem.at[layer, phase], recv_sem.at[layer, phase], req, my_z
                ).start()

    send_long(0, me, peers + strangers)
    long_slots = (2 * n_chip, n_chip)

    for at in (3, 4, 7, 8):
        loads[at].wait()
    shares[0].wait_recv()
    shares[1].wait_recv()
    x_half[0] = (
        jnp.concatenate([x_first, half_of(x_sib)], axis=1).astype(BF16).reshape(owners, part, 256)
    )
    long_x = jnp.concatenate([long_first, dot(long_any, x_sib[...])], axis=1)
    for at in (2, 3, 4):
        shares[at].wait_recv()

    def normed_turned(t, gain, cos, sin):
        t = t * lax.rsqrt(jnp.mean(t * t, axis=1, keepdims=True) + EPS) * gain
        return t * cos + pltpu.roll(t, 64, 1) * sin

    def arrived(ref, sem):
        pltpu.make_async_copy(ref, ref, sem).wait()

    def to_chips(pairs, layer):
        for to, req in zip(chips, peers):
            for src, dst, phase in pairs(to):
                remote(
                    src, dst, send_sem.at[layer, phase], recv_sem.at[layer, phase], req, my_z
                ).start()

    def to_sib(src, dst, phase, layer):
        copy = remote(
            src, dst, send_sem.at[layer, phase], recv_sem.at[layer, phase], sib, my_z
        )
        copy.start()
        return copy

    def softmax_mean(s, v):
        top = jnp.maximum(jnp.max(s, axis=1, keepdims=True), CEIL)
        p = jnp.exp(s - top)
        den = jnp.sum(p, axis=1, keepdims=True)
        num = dot(p.astype(BF16), v)
        level = jnp.where(den > 0.0, top + jnp.log(jnp.maximum(den, TINY)), FLOOR)
        return num / jnp.maximum(den, TINY), jnp.broadcast_to(level, (16, 128))

    logit = 1.0 / math.sqrt(128)
    others = pl.ds(0, n_chip - 1)
    on_diagonal = iota((half, 128), 0) == iota((half, 128), 1)

    for layer in range(LAYERS):
        x = x_half[layer].reshape(half, 256)
        x = x.astype(F32)
        square = jnp.sum(x * x, axis=1, keepdims=True)
        square_row = as_row(square, on_diagonal)
        sq_s[layer] = square_row
        sq_r[layer, chip] = square_row
        xg = (x * gains[pl.ds(layer, 1), :].astype(F32)).astype(BF16)
        q = dot(xg, wq[layer])
        upper = q[:, 0:384].reshape(n_chip, 8, 384)
        lower = jnp.concatenate(
            [q[:, 384:512], dot(xg, wk[layer]), dot(xg, wv[layer])], axis=1
        ).reshape(n_chip, 8, 384)
        rs_s[layer] = jnp.concatenate([upper, lower], axis=1).astype(BF16)
        to_chips(
            lambda to: [
                (rs_s.at[layer, to], rs_r.at[layer, chip], RS),
                (sq_s.at[layer], sq_r.at[layer, chip], SQ),
            ],
            layer,
        )
        rs_r[layer, chip] = rs_s[layer, chip]

        if layer == 0:
            loads[9].wait()
            loads[10].wait()

            def block_masks(b, carry):
                live = (lane8 < fill[b]) & (long_id == owner[b].astype(F32)) & (sub8 < 4)
                bias = jnp.where(live, 0.0, FLOOR)
                long_bias[:, pl.ds(pl.multiple_of(b * 128, 128), 128)] = twice([bias, bias])
                return carry

            lax.fori_loop(0, blocks, block_masks, 0)
            live = (long_id == (8 * me + lane8).astype(F32)) & (lane8 < 8) & (sub8 < 4)
            bias = jnp.where(live, 0.0, FLOOR)
            new_bias[...] = twice([bias, bias])
            for b in range(8):
                home_bias[:, pl.ds(b * 128, 128)] = jnp.where(
                    (sub8 == b) & (lane8 < fill[b]), 0.0, FLOOR
                )
            home_bias[:, pl.ds(1024, 128)] = jnp.where(sub8 == lane8, 0.0, FLOOR)
            zero = jnp.zeros((LAYERS, 128, 128), BF16)
            keys[:, blocks] = zero
            values[:, blocks] = zero
            loads[11].wait()
            loads[12].wait()
        else:
            loads[14].wait()
            loads[15].wait()

        q_gain_row = q_gains[pl.ds(layer, 1), :].astype(F32)
        slots = long_slots[layer]
        arrived(sl_r.at[layer, pl.ds(0, slots - 1)], recv_sem.at[layer, SL])
        arrived(rl_r.at[layer, pl.ds(0, slots - 1)], recv_sem.at[layer, RL])
        scale = lax.rsqrt(
            jnp.sum(long_pick * jnp.sum(sl_r[layer, 0:slots], axis=0), axis=1, keepdims=True)
            / width
            + EPS
        )
        q_long = normed_turned(
            jnp.sum(rl_r[layer, 0:slots].astype(F32), axis=0) * scale,
            q_gain_row,
            long_cos[...],
            long_sin[...],
        ).astype(BF16)
        s = dot_nt(q_long, keys[layer, 0:blocks].reshape(blocks * 128, 128))
        s = s * logit + jnp.concatenate([long_bias[...]] * 2, axis=0)
        mean, level = softmax_mean(s, values[layer, 0:blocks].reshape(blocks * 128, 128))
        px_s[layer] = jnp.concatenate([mean, level], axis=0)
        p_share = to_sib(px_s.at[layer], px_r.at[layer], PX, layer)

        arrived(sq_r.at[layer, others], recv_sem.at[layer, SQ])
        arrived(rs_r.at[layer, others], recv_sem.at[layer, RS])
        sums = jnp.sum(rs_r[layer].astype(F32), axis=0)
        scale = lax.rsqrt(
            jnp.sum(own_pick[...] * jnp.sum(sq_r[layer], axis=0), axis=1, keepdims=True) / width
            + EPS
        )
        new_key = normed_turned(
            sums[8:16, 128:256] * scale,
            k_gains[pl.ds(layer, 1), :].astype(F32),
            own_cos[...],
            own_sin[...],
        )
        new_value = sums[8:16, 256:384] * scale
        pad = jnp.zeros((8, 128), F32)
        keys[layer, blocks, 0:16] = jnp.concatenate([new_key, pad], axis=0).astype(BF16)
        values[layer, blocks, 0:16] = jnp.concatenate([new_value, pad], axis=0).astype(BF16)
        out_keys[layer] = new_key.astype(BF16)
        out_values[layer] = new_value.astype(BF16)
        q_own = [
            normed_turned(t * scale, q_gain_row, own_cos[...], own_sin[...])
            for t in (
                sums[0:8, 0:128], sums[0:8, 128:256], sums[0:8, 256:384], sums[8:16, 0:128]
            )
        ]
        q_own = jnp.concatenate(q_own, axis=0).astype(BF16)

        s = dot_nt(q_long, keys[layer, blocks])
        s = s * logit + jnp.concatenate([new_bias[...]] * 2, axis=0)
        new_mean, new_level = softmax_mean(s, values[layer, blocks])

        s = jnp.concatenate(
            [
                dot_nt(q_own, keys[layer, 0:8].reshape(1024, 128)),
                dot_nt(q_own, keys[layer, blocks]),
            ],
            axis=1,
        )
        s = s * logit + jnp.concatenate([home_bias[...]] * 4, axis=0)
        p = jnp.exp(s - jnp.max(s, axis=1, keepdims=True))
        den = jnp.sum(p, axis=1, keepdims=True)
        p = p.astype(BF16)
        num = dot(p[:, 0:1024], values[layer, 0:8].reshape(1024, 128)) + dot(
            p[:, 1024:1152], values[layer, blocks]
        )
        attended = (num * (jnp.concatenate([own_keep] * 4, axis=0) / den)).astype(BF16)
        ho_s[layer, 0:32] = attended
        ho_r[layer, chip, 0:32] = attended

        p_share.wait_recv()
        other_mean, other_level = px_r[layer, 0:16], px_r[layer, 16:32]
        top = jnp.maximum(jnp.maximum(level, new_level), other_level)
        mine, fresh = jnp.exp(level - top), jnp.exp(new_level - top)
        theirs = jnp.exp(other_level - top)
        every = mine + fresh + theirs
        mean = ((mean * mine + new_mean * fresh + other_mean * theirs) / every).astype(BF16)
        level_row = as_row(top + jnp.log(every), row16 == lane16)
        ho_s[layer, 32:48] = mean
        ho_r[layer, chip, 32:48] = mean
        ll_s[layer] = level_row
        ll_r[layer, chip] = level_row
        to_chips(
            lambda to: [
                (ho_s.at[layer], ho_r.at[layer, chip], HO),
                (ll_s.at[layer], ll_r.at[layer, chip], LL),
            ],
            layer,
        )

        if layer == 0:
            loads[13].wait()
        shares[5 if layer == 0 else 9].wait_recv()
        arrived(ho_r.at[layer, others], recv_sem.at[layer, HO])
        homes = ho_r[layer, :, 0:32].astype(F32)
        homes = jnp.concatenate(
            [homes[:, 8 * g : 8 * g + 8].reshape(half, 128) for g in range(4)], axis=1
        )
        arrived(ll_r.at[layer, others], recv_sem.at[layer, LL])
        levels = ll_r[layer]
        weight = jnp.exp(levels - jnp.max(levels, axis=0, keepdims=True))
        weight = weight / jnp.sum(weight, axis=0, keepdims=True)
        weight = jnp.sum(
            jnp.where(
                iota((n_chip, 16, 128), 1) == iota((n_chip, 16, 128), 2),
                jnp.broadcast_to(weight, (n_chip, 16, 128)),
                0.0,
            ),
            axis=2,
            keepdims=True,
        )
        merged = jnp.sum(weight * ho_r[layer, :, 32:48].astype(F32), axis=0)
        merged = jnp.concatenate(
            [jnp.where(row16 // 4 == g, merged, 0.0) for g in range(4)], axis=1
        ).astype(BF16)
        attended = (homes + dot(spread[...], merged)).astype(BF16)

        branch = jnp.concatenate(
            [dot(attended, wo[layer, 0]), dot(attended, wo[layer, 1])], axis=1
        )
        branch = branch.astype(BF16)
        zr_s[layer] = branch.reshape(owners, part, 256)
        if layer + 1 < LAYERS:
            long_branch = dot(long_sel, branch)[0:8]
            long_branch = twice([long_branch[:, 0:128], long_branch[:, 128:256]]).astype(BF16)
            lz_s[...] = long_branch
            lz_r[0, my_z] = long_branch
        for d in z_far:
            remote(
                zr_s.at[layer, lax.rem(z_at[d], owners)], zr_r.at[layer, my_z],
                send_sem.at[layer, ZR], recv_sem.at[layer, ZR], me, z_at[d],
            ).start()
        if layer + 1 < LAYERS:
            for d in z_far:
                remote(
                    lz_s, lz_r.at[0, my_z],
                    send_sem.at[layer, LZ], recv_sem.at[layer, LZ], me, z_at[d],
                ).start()
                remote(
                    lz_s, lz_r.at[1, my_z],
                    send_sem.at[layer, LW], recv_sem.at[layer, LW], sib, z_at[d],
                ).start()
            remote(
                lz_s, lz_r.at[1, my_z],
                send_sem.at[layer, LW], recv_sem.at[layer, LW], sib, my_z,
            ).start()
        zr_r[layer, my_z] = zr_s[layer, my_part]
        arrived(zr_r.at[layer, pl.ds(0, nz - 1)], recv_sem.at[layer, ZR])
        hidden = (
            x_half[layer, my_part].astype(F32) + jnp.sum(zr_r[layer].astype(F32), axis=0)
        ).astype(BF16)

        mid = part // 2
        rows_for = {1: (0, part), 7: (0, part), 6: (0, mid), 2: (mid, mid)}
        if layer + 1 < LAYERS:
            za_s[...] = hidden
            x_half[layer + 1, my_part] = hidden
            for d in z_near:
                rows = pl.ds(*rows_for[d])
                remote(
                    za_s.at[rows], x_half.at[layer + 1, my_part, rows],
                    send_sem.at[layer, ZA], recv_sem.at[layer, ZA], me, z_at[d],
                ).start()
            arrived(lz_r.at[0, pl.ds(0, nz - 1)], recv_sem.at[layer, LZ])
            arrived(lz_r.at[1], recv_sem.at[layer, LW])
            mine = jnp.sum(lz_r[0].astype(F32), axis=0)
            theirs = jnp.sum(lz_r[1].astype(F32), axis=0)
            far = pltpu.roll(theirs, 4, 0)
            near = pltpu.roll(mine, 4, 0)
            gained = jnp.concatenate([mine + far, near + theirs], axis=1)
            gained = jnp.where(iota((8, 256), 0) < 4, gained, 0.0)
            long_x = long_x + jnp.concatenate([gained, jnp.zeros((8, 256), F32)], axis=0)
            for at in (6, 7, 8):
                shares[at].wait_recv()
            long_message(layer + 1, long_x.astype(BF16).astype(F32), 256, chip)
            send_long(layer + 1, chip, peers)
            if owners > 1:
                arrived(x_half.at[layer + 1, pl.ds(0, owners - 1)], recv_sem.at[layer, ZA])
        else:
            fin_s[0] = hidden[:, 0:128]
            fin_s[1] = hidden[:, 128:256]
            start = pl.multiple_of(my_part * part, part)
            for d in z_near:
                first, count = rows_for[d]
                rows = pl.ds(first, count)
                to = out.at[core, pl.ds(pl.multiple_of(start + first, count), count)]
                remote(
                    fin_s.at[1, rows], to,
                    send_sem.at[layer, ZB], recv_sem.at[layer, ZB], sib, z_at[d],
                ).start()
                remote(
                    fin_s.at[0, rows], to,
                    send_sem.at[layer, ZA], recv_sem.at[layer, ZA], me, z_at[d],
                ).start()
            to = out.at[core, pl.ds(start, part)]
            remote(
                fin_s.at[1], to,
                send_sem.at[layer, ZB], recv_sem.at[layer, ZB], sib, my_z,
            ).start()
            out[core, pl.ds(start, part)] = hidden[:, 0:128]
            most = pl.ds(0, half - part)
            if owners > 1:
                arrived(out.at[core, most], recv_sem.at[layer, ZA])
            arrived(out.at[1 - core], recv_sem.at[layer, ZB])

    for copy in shares:
        copy.wait_send()
    for layer in range(LAYERS):
        for ref, phase in (
            (rs_r.at[layer, others], RS),
            (sq_r.at[layer, others], SQ),
            (rl_r.at[layer, pl.ds(0, long_slots[layer] - 1)], RL),
            (sl_r.at[layer, pl.ds(0, long_slots[layer] - 1)], SL),
            (px_r.at[layer], PX),
            (ho_r.at[layer, others], HO),
            (ll_r.at[layer, others], LL),
            (zr_r.at[layer, pl.ds(0, nz - 1)], ZR),
        ):
            arrived(ref, send_sem.at[layer, phase])
        if layer + 1 < LAYERS:
            arrived(lz_r.at[0, pl.ds(0, nz - 1)], send_sem.at[layer, LZ])
            arrived(lz_r.at[1], send_sem.at[layer, LW])
            if owners > 1:
                arrived(x_half.at[layer + 1, pl.ds(0, owners - 1)], send_sem.at[layer, ZA])
        else:
            if owners > 1:
                arrived(out.at[core, most], send_sem.at[layer, ZA])
            arrived(out.at[1 - core], send_sem.at[layer, ZB])


def finish(hidden, new_keys, new_values, out, out_keys, out_values, sem):
    copies = [
        pltpu.make_async_copy(hidden.at[0], out.at[:, 0], sem.at[0]),
        pltpu.make_async_copy(hidden.at[1], out.at[:, 1], sem.at[1]),
        pltpu.make_async_copy(new_keys, out_keys, sem.at[2]),
        pltpu.make_async_copy(new_values, out_values, sem.at[3]),
    ]
    for copy in copies:
        copy.start()
    for copy in copies:
        copy.wait()


def on_device(
    n_chip, side, nz, width,
    hidden_in, norm_gain, q_gain, k_gain, w_query, w_key, w_value, w_out,
    cache_keys, cache_values, lengths, block_owner, block_fill,
):
    half = 8 * n_chip
    owners = nz // 2
    part = half // owners
    blocks = cache_keys.shape[1]
    total = hidden_in.shape[0]
    heads = w_query.shape[2]
    exponent = np.concatenate([np.arange(64), np.arange(64)]) * 2.0 / 128
    frequency = jnp.asarray((THETA**-exponent).astype(np.float32)[None, :])
    vmem, sem = pltpu.VMEM, pltpu.SemaphoreType.DMA
    anywhere = pl.BlockSpec(memory_space=pl.ANY)
    both = (LAYERS, n_chip)
    onchip = pl.BlockSpec(memory_space=pltpu.VMEM)
    news = jax.ShapeDtypeStruct((LAYERS, 8, 128), BF16)
    chip_news = vmem((LAYERS, 8, 128), BF16)
    hidden, new_keys, new_values = pl.pallas_call(
        functools.partial(kernel, n_chip, side, nz, float(width)),
        out_shape=(vmem((2, half, 128), BF16), chip_news, chip_news),
        in_specs=[anywhere] * 14,
        out_specs=(onchip, onchip, onchip),
        scratch_shapes=[
            vmem((total, 128), BF16),
            vmem((total, 128), BF16),
            vmem((LAYERS, 256), BF16),
            vmem((LAYERS, 128), BF16),
            vmem((LAYERS, 128), BF16),
            vmem((LAYERS, 256, heads), BF16),
            vmem((LAYERS, 256, 128), BF16),
            vmem((LAYERS, 256, 128), BF16),
            vmem((LAYERS, 2, heads, 128), BF16),
            vmem((LAYERS, blocks + 1, 128, 128), BF16),
            vmem((LAYERS, blocks + 1, 128, 128), BF16),
            vmem((1, total), jnp.int32),
            pltpu.SMEM((blocks,), jnp.int32),
            pltpu.SMEM((blocks,), jnp.int32),
            vmem((1, 128), F32),
            vmem((LAYERS, owners, part, 256), BF16),
            vmem((8, blocks * 128), F32),
            vmem((8, 128), F32),
            vmem((8, 9 * 128), F32),
            vmem((8, 128), F32),
            vmem((8, 128), F32),
            vmem((16, 128), F32),
            vmem((16, 128), F32),
            vmem((8, 128), F32),
            vmem((half, 16), BF16),
            vmem((*both, 16, 384), BF16),
            vmem((*both, 16, 384), BF16),
            vmem((LAYERS, 1, 128), F32),
            vmem((*both, 1, 128), F32),
            vmem((LAYERS, 16, 128), BF16),
            vmem((LAYERS, 2 * n_chip, 16, 128), BF16),
            vmem((LAYERS, 1, 128), F32),
            vmem((LAYERS, 2 * n_chip, 1, 128), F32),
            vmem((8, 128), BF16),
            vmem((2, nz, 8, 128), BF16),
            vmem((LAYERS, 32, 128), F32),
            vmem((LAYERS, 32, 128), F32),
            vmem((LAYERS, 48, 128), BF16),
            vmem((*both, 48, 128), BF16),
            vmem((LAYERS, 1, 128), F32),
            vmem((*both, 1, 128), F32),
            vmem((LAYERS, owners, part, 256), BF16),
            vmem((LAYERS, nz, part, 256), BF16),
            vmem((part, 256), BF16),
            vmem((2, part, 128), BF16),
            sem((16,)),
            sem((10,)),
            sem((10,)),
            sem((LAYERS, 12)),
            sem((LAYERS, 12)),
        ],
        compiler_params=pltpu.CompilerParams(
            collective_id=0, has_side_effects=True, vmem_limit_bytes=60000 * 1024
        ),
        name="attention_layers",
    )(
        hidden_in, norm_gain, q_gain, k_gain, w_query, w_key, w_value, w_out,
        cache_keys, cache_values, lengths.reshape(1, total), block_owner, block_fill, frequency,
    )
    out, new_keys, new_values = pl.pallas_call(
        finish,
        out_shape=(jax.ShapeDtypeStruct((n_chip, 2, 8, 128), BF16), news, news),
        in_specs=[onchip] * 3,
        out_specs=(anywhere, anywhere, anywhere),
        scratch_shapes=[sem((4,))],
        compiler_params=pltpu.CompilerParams(vmem_limit_bytes=1024 * 1024),
        name="finish",
    )(hidden.reshape(2, n_chip, 8, 128), new_keys, new_values)
    return out.reshape(total, 128), new_keys, new_values


def solution(mesh):
    n_req, nz = mesh.shape["req"], mesh.shape["kv"]
    n_chip = n_req // 2
    side = math.isqrt(n_chip)
    in_specs = (
        P(None, "req"),
        P(None, "req"),
        P(),
        P(),
        P(None, "req", "kv"),
        P(None, "req", "kv"),
        P(None, "req", "kv"),
        P(None, "kv", "req"),
        P(None, "req", None, "kv"),
        P(None, "req", None, "kv"),
        P(),
        P("req"),
        P("req"),
    )
    out_specs = (P(None, "req"), P(None, "req", "kv"), P(None, "req", "kv"))
    return jax.shard_map(
        functools.partial(on_device, n_chip, side, nz, 128 * n_req),
        mesh=mesh,
        in_specs=in_specs,
        out_specs=out_specs,
        check_vma=False,
    )
```

```python
import functools
import math

import jax
import jax.numpy as jnp
import numpy as np
from jax import lax
from jax.experimental import pallas as pl
from jax.experimental.pallas import tpu as pltpu
from jax.sharding import PartitionSpec as P

LAYERS = 2
EPS = 1e-06
THETA = 1000000.0
FLOOR = -1e30
CEIL = -1e29
TINY = 1e-30
MESH = pl.DeviceIdType.MESH
F32 = jnp.float32
BF16 = jnp.bfloat16

RS, SQ, RL, SL, LZ, LW, PX, HO, LL, ZR, ZA, ZB = range(12)


def dot(a, b):
    return jnp.dot(a, b, preferred_element_type=F32)


def dot_nt(a, b):
    return lax.dot_general(a, b, (((1,), (1,)), ((), ())), preferred_element_type=F32)


def iota(shape, dim):
    return lax.broadcasted_iota(jnp.int32, shape, dim)


def kernel(
    n_chip,
    side,
    nz,
    width,
    x_in, norm_gain, q_gain, k_gain, w_query, w_key, w_value, w_out,
    cache_keys, cache_values, lengths, block_owner, block_fill, frequency,
    out, out_keys, out_values,
    x_own, x_sib, gains, q_gains, k_gains, wq, wk, wv, wo, keys, values,
    lens, owner, fill, freq,
    x_half, long_bias, new_bias, home_bias, own_cos, own_sin, long_cos, long_sin, own_pick, spread,
    rs_s, rs_r, sq_s, sq_r, rl_s, rl_r, sl_s, sl_r, lz_s, lz_r, px_s, px_r,
    ho_s, ho_r, ll_s, ll_r, zr_s, zr_r, za_s, fin_s,
    load_sem, init_send, init_recv, send_sem, recv_sem,
):
    half = 8 * n_chip
    owners = nz // 2
    part = half // owners
    blocks = cache_keys.shape[1]
    total = lens.shape[1]
    me = lax.axis_index("req")
    my_z = lax.axis_index("kv")
    core = lax.rem(me, 2)
    chip = lax.div(me, 2)
    chip_x, chip_y = lax.div(chip, side), lax.rem(chip, side)
    sib = me + 1 - 2 * core
    my_part = lax.rem(my_z, owners)

    def ring(d, n):
        return min(d, n - d)

    steps = sorted(
        [(dx, dy) for dx in range(side) for dy in range(side) if dx or dy],
        key=lambda d: (
            -ring(d[0], side) - ring(d[1], side),
            -max(ring(d[0], side), ring(d[1], side)),
        ),
    )
    at_x = [lax.rem(chip_x + d, side) * side for d in range(side)]
    at_y = [lax.rem(chip_y + d, side) for d in range(side)]
    chips = [at_x[dx] + at_y[dy] for dx, dy in steps]
    peers = [2 * c + core for c in chips]
    strangers = [2 * c + 1 - core for c in chips] + [sib]
    z_at = [lax.rem(my_z + d, nz) for d in range(nz)]
    z_far = sorted(range(1, nz), key=lambda d: -ring(d, nz))
    z_near = {8: (6, 2, 7, 1), 2: ()}[nz]

    barrier = pltpu.get_barrier_semaphore()

    def greet(req, kv):
        pl.semaphore_signal(
            barrier, inc=1, device_id={"req": req, "kv": kv}, device_id_type=MESH
        )

    for req in peers + strangers:
        greet(req, my_z)
    for d in z_far:
        greet(me, z_at[d])
        greet(sib, z_at[d])

    loads = [
        pltpu.make_async_copy(src, dst, load_sem.at[at])
        for at, (src, dst) in enumerate(
            [
                (lengths, lens),
                (frequency, freq),
                (norm_gain, gains.at[:, pl.ds(0, 128)]),
                (q_gain, q_gains),
                (k_gain, k_gains),
                (x_in, x_own),
                (w_query, wq.at[:, pl.ds(0, 128)]),
                (w_key, wk.at[:, pl.ds(0, 128)]),
                (w_value, wv.at[:, pl.ds(0, 128)]),
                (block_owner, owner),
                (block_fill, fill),
                (cache_keys.at[0], keys.at[0, pl.ds(0, blocks)]),
                (cache_values.at[0], values.at[0, pl.ds(0, blocks)]),
                (w_out, wo.at[:, 0]),
                (cache_keys.at[1], keys.at[1, pl.ds(0, blocks)]),
                (cache_values.at[1], values.at[1, pl.ds(0, blocks)]),
            ]
        )
    ]
    for copy in loads:
        copy.start()

    row16 = iota((16, 128), 0)
    lane16 = iota((16, 128), 1)
    sub8 = iota((8, 128), 0)
    lane8 = iota((8, 128), 1)

    def twice(t):
        return jnp.where(iota(t[0].shape, 0) < 4, t[0], pltpu.roll(t[1], 4, 0))

    loads[0].wait()
    loads[1].wait()
    length_row = lens[...].astype(F32)
    request_row = iota((8, total), 1).astype(F32)
    is_long = jnp.where(length_row > 128.0, 1.0, 0.0)
    before = jnp.where(iota((total, total), 0) < iota((total, total), 1), 1.0, 0.0).astype(BF16)
    rank = dot(jnp.broadcast_to(is_long, (8, total)).astype(BF16), before)
    slot8 = iota((8, total), 0)
    long_hot = jnp.where(
        (rank.astype(jnp.int32) == slot8) & (slot8 < 4),
        jnp.broadcast_to(is_long, (8, total)),
        0.0,
    )
    own_hot = jnp.where(iota((8, total), 1) == 8 * me + slot8, 1.0, 0.0)
    long_id = jnp.sum(long_hot * request_row, axis=1, keepdims=True)
    long_at = jnp.sum(long_hot * length_row, axis=1, keepdims=True)
    own_at = jnp.sum(own_hot * length_row, axis=1, keepdims=True)
    own_keep = jnp.where(own_at > 128.0, 0.0, 1.0)
    row_of = iota((total, 128), 1)
    to_half = jnp.where(
        (iota((total, 128), 0) == (row_of // 8) * 16 + 8 * core + row_of % 8) & (row_of < half),
        1.0,
        0.0,
    ).astype(BF16)
    long_half = dot(long_hot.astype(BF16), to_half)
    own_pick[...] = jnp.where(lane8 == 8 * chip + sub8, 1.0, 0.0)
    four = twice([long_half, long_half])
    eye = jnp.where(iota((half, 128), 0) == iota((half, 128), 1), 1.0, 0.0)
    spread[...] = dot_nt(
        eye.astype(BF16), jnp.concatenate([four, four], axis=0).astype(BF16)
    ).astype(BF16)
    long_sel = jnp.concatenate([long_half, jnp.zeros((8, 128), F32)], axis=0).astype(BF16)
    long_sel = long_sel[:, :half]
    long_any = jnp.concatenate([long_hot, jnp.zeros((8, total), F32)], axis=0).astype(BF16)
    long_pick = jnp.where(lane16 == row16 % 4, 1.0, 0.0)

    def turns(at, cos_ref, sin_ref):
        angle = at * freq[...]
        rows = angle.shape[0]
        sin = jnp.sin(angle)
        cos_ref[...] = jnp.cos(angle)
        sin_ref[...] = jnp.where(iota((rows, 128), 1) < 64, -sin, sin)

    turns(own_at, own_cos, own_sin)
    at4 = twice([jnp.broadcast_to(long_at, (8, 128))] * 2)
    turns(jnp.concatenate([at4, at4], axis=0), long_cos, long_sin)

    def half_of(ref):
        rows = ref[...].astype(F32).reshape(n_chip, 2, 8, 128)
        return jnp.where(core == 0, rows[:, 0], rows[:, 1]).reshape(half, 128)

    loads[5].wait()
    x_first = half_of(x_own)
    long_first = dot(long_any, x_own[...])

    def as_row(column, mask):
        return jnp.sum(jnp.where(mask, column, 0.0), axis=0, keepdims=True)

    def long_message(layer, rows, columns, slot):
        square = jnp.sum(rows * rows, axis=1, keepdims=True)
        square_row = as_row(square, row16 == lane16)
        sl_s[layer] = square_row
        sl_r[layer, slot] = square_row
        gain = gains[pl.ds(layer, 1), 0:columns].astype(F32)
        q = dot((rows * gain).astype(BF16), wq[layer, 0:columns])[0:8]
        q = [q[:, 128 * g : 128 * g + 128] for g in range(4)]
        q = jnp.concatenate([twice(q[0:2]), twice(q[2:4])], axis=0).astype(BF16)
        rl_s[layer] = q
        rl_r[layer, slot] = q

    for at in (2, 6, 7, 8):
        loads[at].wait()
    long_message(0, long_first, 128, me)

    pl.semaphore_wait(barrier, len(peers) + len(strangers) + 2 * len(z_far))

    def remote(src, dst, send, recv, req, kv):
        return pltpu.make_async_remote_copy(
            src_ref=src,
            dst_ref=dst,
            send_sem=send,
            recv_sem=recv,
            device_id={"req": req, "kv": kv},
            device_id_type=MESH,
        )

    shares = [
        remote(src, dst, init_send.at[at], init_recv.at[at], sib, my_z)
        for at, (src, dst) in enumerate(
            [
                (x_own, x_sib),
                (gains.at[:, pl.ds(0, 128)], gains.at[:, pl.ds(128, 128)]),
                (wq.at[0, pl.ds(0, 128)], wq.at[0, pl.ds(128, 128)]),
                (wk.at[0, pl.ds(0, 128)], wk.at[0, pl.ds(128, 128)]),
                (wv.at[0, pl.ds(0, 128)], wv.at[0, pl.ds(128, 128)]),
                (w_out.at[0], wo.at[0, 1]),
                (w_query.at[1], wq.at[1, pl.ds(128, 128)]),
                (w_key.at[1], wk.at[1, pl.ds(128, 128)]),
                (w_value.at[1], wv.at[1, pl.ds(128, 128)]),
                (w_out.at[1], wo.at[1, 1]),
            ]
        )
    ]
    for copy in shares[:5]:
        copy.start()

    def send_long(layer, slot, everyone):
        for req in everyone:
            for src, dst, phase in (
                (rl_s.at[layer], rl_r.at[layer, slot], RL),
                (sl_s.at[layer], sl_r.at[layer, slot], SL),
            ):
                remote(
                    src, dst, send_sem.at[layer, phase], recv_sem.at[layer, phase], req, my_z
                ).start()

    in_turn = [req for pair in zip(peers, strangers) for req in pair] + [sib]
    send_long(0, me, in_turn)
    long_slots = (2 * n_chip, n_chip)

    for at in (3, 4):
        loads[at].wait()
    shares[0].wait_recv()
    shares[1].wait_recv()
    x_half[0] = (
        jnp.concatenate([x_first, half_of(x_sib)], axis=1).astype(BF16).reshape(owners, part, 256)
    )
    long_x = jnp.concatenate([long_first, dot(long_any, x_sib[...])], axis=1)
    for at in (2, 3, 4):
        shares[at].wait_recv()

    def normed_turned(t, gain, cos, sin):
        t = t * lax.rsqrt(jnp.mean(t * t, axis=1, keepdims=True) + EPS) * gain
        return t * cos + pltpu.roll(t, 64, 1) * sin

    def arrived(ref, sem):
        pltpu.make_async_copy(ref, ref, sem).wait()

    def to_chips(pairs, layer):
        for to, req in zip(chips, peers):
            for src, dst, phase in pairs(to):
                remote(
                    src, dst, send_sem.at[layer, phase], recv_sem.at[layer, phase], req, my_z
                ).start()

    def to_sib(src, dst, phase, layer):
        copy = remote(
            src, dst, send_sem.at[layer, phase], recv_sem.at[layer, phase], sib, my_z
        )
        copy.start()
        return copy

    def softmax_mean(s, v):
        top = jnp.maximum(jnp.max(s, axis=1, keepdims=True), CEIL)
        p = jnp.exp(s - top)
        den = jnp.sum(p, axis=1, keepdims=True)
        num = dot(p.astype(BF16), v)
        level = jnp.where(den > 0.0, top + jnp.log(jnp.maximum(den, TINY)), FLOOR)
        return num / jnp.maximum(den, TINY), jnp.broadcast_to(level, (16, 128))

    logit = 1.0 / math.sqrt(128)
    others = pl.ds(0, n_chip - 1)
    on_diagonal = iota((half, 128), 0) == iota((half, 128), 1)

    for layer in range(LAYERS):
        x = x_half[layer].reshape(half, 256)
        x = x.astype(F32)
        square = jnp.sum(x * x, axis=1, keepdims=True)
        square_row = as_row(square, on_diagonal)
        sq_s[layer] = square_row
        sq_r[layer, chip] = square_row
        xg = (x * gains[pl.ds(layer, 1), :].astype(F32)).astype(BF16)
        q = dot(xg, wq[layer])
        upper = q[:, 0:384].reshape(n_chip, 8, 384)
        lower = jnp.concatenate(
            [q[:, 384:512], dot(xg, wk[layer]), dot(xg, wv[layer])], axis=1
        ).reshape(n_chip, 8, 384)
        rs_s[layer] = jnp.concatenate([upper, lower], axis=1).astype(BF16)
        to_chips(
            lambda to: [
                (rs_s.at[layer, to], rs_r.at[layer, chip], RS),
                (sq_s.at[layer], sq_r.at[layer, chip], SQ),
            ],
            layer,
        )
        rs_r[layer, chip] = rs_s[layer, chip]

        if layer == 0:
            for copy in shares[5:]:
                copy.start()

            loads[9].wait()
            loads[10].wait()

            def block_masks(b, carry):
                live = (lane8 < fill[b]) & (long_id == owner[b].astype(F32)) & (sub8 < 4)
                bias = jnp.where(live, 0.0, FLOOR)
                long_bias[:, pl.ds(pl.multiple_of(b * 128, 128), 128)] = twice([bias, bias])
                return carry

            lax.fori_loop(0, blocks, block_masks, 0)
            live = (long_id == (8 * me + lane8).astype(F32)) & (lane8 < 8) & (sub8 < 4)
            bias = jnp.where(live, 0.0, FLOOR)
            new_bias[...] = twice([bias, bias])
            for b in range(8):
                home_bias[:, pl.ds(b * 128, 128)] = jnp.where(
                    (sub8 == b) & (lane8 < fill[b]), 0.0, FLOOR
                )
            home_bias[:, pl.ds(1024, 128)] = jnp.where(sub8 == lane8, 0.0, FLOOR)
            zero = jnp.zeros((LAYERS, 128, 128), BF16)
            keys[:, blocks] = zero
            values[:, blocks] = zero
            loads[11].wait()
            loads[12].wait()
        else:
            loads[14].wait()
            loads[15].wait()

        q_gain_row = q_gains[pl.ds(layer, 1), :].astype(F32)
        slots = long_slots[layer]
        arrived(sl_r.at[layer, pl.ds(0, slots - 1)], recv_sem.at[layer, SL])
        arrived(rl_r.at[layer, pl.ds(0, slots - 1)], recv_sem.at[layer, RL])
        scale = lax.rsqrt(
            jnp.sum(long_pick * jnp.sum(sl_r[layer, 0:slots], axis=0), axis=1, keepdims=True)
            / width
            + EPS
        )
        q_long = normed_turned(
            jnp.sum(rl_r[layer, 0:slots].astype(F32), axis=0) * scale,
            q_gain_row,
            long_cos[...],
            long_sin[...],
        ).astype(BF16)
        s = dot_nt(q_long, keys[layer, 0:blocks].reshape(blocks * 128, 128))
        s = s * logit + jnp.concatenate([long_bias[...]] * 2, axis=0)
        mean, level = softmax_mean(s, values[layer, 0:blocks].reshape(blocks * 128, 128))
        px_s[layer] = jnp.concatenate([mean, level], axis=0)
        p_share = to_sib(px_s.at[layer], px_r.at[layer], PX, layer)

        arrived(sq_r.at[layer, others], recv_sem.at[layer, SQ])
        arrived(rs_r.at[layer, others], recv_sem.at[layer, RS])
        sums = jnp.sum(rs_r[layer].astype(F32), axis=0)
        scale = lax.rsqrt(
            jnp.sum(own_pick[...] * jnp.sum(sq_r[layer], axis=0), axis=1, keepdims=True) / width
            + EPS
        )
        new_key = normed_turned(
            sums[8:16, 128:256] * scale,
            k_gains[pl.ds(layer, 1), :].astype(F32),
            own_cos[...],
            own_sin[...],
        )
        new_value = sums[8:16, 256:384] * scale
        pad = jnp.zeros((8, 128), F32)
        keys[layer, blocks, 0:16] = jnp.concatenate([new_key, pad], axis=0).astype(BF16)
        values[layer, blocks, 0:16] = jnp.concatenate([new_value, pad], axis=0).astype(BF16)
        out_keys[layer] = new_key.astype(BF16)
        out_values[layer] = new_value.astype(BF16)
        q_own = [
            normed_turned(t * scale, q_gain_row, own_cos[...], own_sin[...])
            for t in (
                sums[0:8, 0:128], sums[0:8, 128:256], sums[0:8, 256:384], sums[8:16, 0:128]
            )
        ]
        q_own = jnp.concatenate(q_own, axis=0).astype(BF16)

        s = dot_nt(q_long, keys[layer, blocks])
        s = s * logit + jnp.concatenate([new_bias[...]] * 2, axis=0)
        new_mean, new_level = softmax_mean(s, values[layer, blocks])

        s = jnp.concatenate(
            [
                dot_nt(q_own, keys[layer, 0:8].reshape(1024, 128)),
                dot_nt(q_own, keys[layer, blocks]),
            ],
            axis=1,
        )
        s = s * logit + jnp.concatenate([home_bias[...]] * 4, axis=0)
        p = jnp.exp(s - jnp.max(s, axis=1, keepdims=True))
        den = jnp.sum(p, axis=1, keepdims=True)
        p = p.astype(BF16)
        num = dot(p[:, 0:1024], values[layer, 0:8].reshape(1024, 128)) + dot(
            p[:, 1024:1152], values[layer, blocks]
        )
        attended = (num * (jnp.concatenate([own_keep] * 4, axis=0) / den)).astype(BF16)
        ho_s[layer, 0:32] = attended
        ho_r[layer, chip, 0:32] = attended

        p_share.wait_recv()
        other_mean, other_level = px_r[layer, 0:16], px_r[layer, 16:32]
        top = jnp.maximum(jnp.maximum(level, new_level), other_level)
        mine, fresh = jnp.exp(level - top), jnp.exp(new_level - top)
        theirs = jnp.exp(other_level - top)
        every = mine + fresh + theirs
        mean = ((mean * mine + new_mean * fresh + other_mean * theirs) / every).astype(BF16)
        level_row = as_row(top + jnp.log(every), row16 == lane16)
        ho_s[layer, 32:48] = mean
        ho_r[layer, chip, 32:48] = mean
        ll_s[layer] = level_row
        ll_r[layer, chip] = level_row
        to_chips(
            lambda to: [
                (ho_s.at[layer], ho_r.at[layer, chip], HO),
                (ll_s.at[layer], ll_r.at[layer, chip], LL),
            ],
            layer,
        )

        if layer == 0:
            loads[13].wait()
        shares[5 if layer == 0 else 9].wait_recv()
        arrived(ho_r.at[layer, others], recv_sem.at[layer, HO])
        homes = ho_r[layer, :, 0:32].astype(F32)
        homes = jnp.concatenate(
            [homes[:, 8 * g : 8 * g + 8].reshape(half, 128) for g in range(4)], axis=1
        )
        arrived(ll_r.at[layer, others], recv_sem.at[layer, LL])
        levels = ll_r[layer]
        weight = jnp.exp(levels - jnp.max(levels, axis=0, keepdims=True))
        weight = weight / jnp.sum(weight, axis=0, keepdims=True)
        weight = jnp.sum(
            jnp.where(
                iota((n_chip, 16, 128), 1) == iota((n_chip, 16, 128), 2),
                jnp.broadcast_to(weight, (n_chip, 16, 128)),
                0.0,
            ),
            axis=2,
            keepdims=True,
        )
        merged = jnp.sum(weight * ho_r[layer, :, 32:48].astype(F32), axis=0)
        merged = jnp.concatenate(
            [jnp.where(row16 // 4 == g, merged, 0.0) for g in range(4)], axis=1
        ).astype(BF16)
        attended = (homes + dot(spread[...], merged)).astype(BF16)

        branch = jnp.concatenate(
            [dot(attended, wo[layer, 0]), dot(attended, wo[layer, 1])], axis=1
        )
        branch = branch.astype(BF16)
        zr_s[layer] = branch.reshape(owners, part, 256)
        if layer + 1 < LAYERS:
            long_branch = dot(long_sel, branch)[0:8]
            long_branch = twice([long_branch[:, 0:128], long_branch[:, 128:256]]).astype(BF16)
            lz_s[...] = long_branch
            lz_r[0, my_z] = long_branch
        for d in z_far:
            remote(
                zr_s.at[layer, lax.rem(z_at[d], owners)], zr_r.at[layer, my_z],
                send_sem.at[layer, ZR], recv_sem.at[layer, ZR], me, z_at[d],
            ).start()
        if layer + 1 < LAYERS:
            for d in z_far:
                remote(
                    lz_s, lz_r.at[0, my_z],
                    send_sem.at[layer, LZ], recv_sem.at[layer, LZ], me, z_at[d],
                ).start()
                remote(
                    lz_s, lz_r.at[1, my_z],
                    send_sem.at[layer, LW], recv_sem.at[layer, LW], sib, z_at[d],
                ).start()
            remote(
                lz_s, lz_r.at[1, my_z],
                send_sem.at[layer, LW], recv_sem.at[layer, LW], sib, my_z,
            ).start()
        zr_r[layer, my_z] = zr_s[layer, my_part]
        arrived(zr_r.at[layer, pl.ds(0, nz - 1)], recv_sem.at[layer, ZR])
        hidden = (
            x_half[layer, my_part].astype(F32) + jnp.sum(zr_r[layer].astype(F32), axis=0)
        ).astype(BF16)

        mid = part // 2
        rows_for = {1: (0, part), 7: (0, part), 6: (0, mid), 2: (mid, mid)}
        if layer + 1 < LAYERS:
            za_s[...] = hidden
            x_half[layer + 1, my_part] = hidden
            for d in z_near:
                rows = pl.ds(*rows_for[d])
                remote(
                    za_s.at[rows], x_half.at[layer + 1, my_part, rows],
                    send_sem.at[layer, ZA], recv_sem.at[layer, ZA], me, z_at[d],
                ).start()
            arrived(lz_r.at[0, pl.ds(0, nz - 1)], recv_sem.at[layer, LZ])
            arrived(lz_r.at[1], recv_sem.at[layer, LW])
            mine = jnp.sum(lz_r[0].astype(F32), axis=0)
            theirs = jnp.sum(lz_r[1].astype(F32), axis=0)
            far = pltpu.roll(theirs, 4, 0)
            near = pltpu.roll(mine, 4, 0)
            gained = jnp.concatenate([mine + far, near + theirs], axis=1)
            gained = jnp.where(iota((8, 256), 0) < 4, gained, 0.0)
            long_x = long_x + jnp.concatenate([gained, jnp.zeros((8, 256), F32)], axis=0)
            for at in (6, 7, 8):
                shares[at].wait_recv()
            long_message(layer + 1, long_x.astype(BF16).astype(F32), 256, chip)
            send_long(layer + 1, chip, peers)
            if owners > 1:
                arrived(x_half.at[layer + 1, pl.ds(0, owners - 1)], recv_sem.at[layer, ZA])
        else:
            fin_s[0] = hidden[:, 0:128]
            fin_s[1] = hidden[:, 128:256]
            start = pl.multiple_of(my_part * part, part)
            for d in z_near:
                first, count = rows_for[d]
                rows = pl.ds(first, count)
                to = out.at[core, pl.ds(pl.multiple_of(start + first, count), count)]
                remote(
                    fin_s.at[1, rows], to,
                    send_sem.at[layer, ZB], recv_sem.at[layer, ZB], sib, z_at[d],
                ).start()
                remote(
                    fin_s.at[0, rows], to,
                    send_sem.at[layer, ZA], recv_sem.at[layer, ZA], me, z_at[d],
                ).start()
            to = out.at[core, pl.ds(start, part)]
            remote(
                fin_s.at[1], to,
                send_sem.at[layer, ZB], recv_sem.at[layer, ZB], sib, my_z,
            ).start()
            out[core, pl.ds(start, part)] = hidden[:, 0:128]
            most = pl.ds(0, half - part)
            if owners > 1:
                arrived(out.at[core, most], recv_sem.at[layer, ZA])
            arrived(out.at[1 - core], recv_sem.at[layer, ZB])

    for copy in shares:
        copy.wait_send()
    for layer in range(LAYERS):
        for ref, phase in (
            (rs_r.at[layer, others], RS),
            (sq_r.at[layer, others], SQ),
            (rl_r.at[layer, pl.ds(0, long_slots[layer] - 1)], RL),
            (sl_r.at[layer, pl.ds(0, long_slots[layer] - 1)], SL),
            (px_r.at[layer], PX),
            (ho_r.at[layer, others], HO),
            (ll_r.at[layer, others], LL),
            (zr_r.at[layer, pl.ds(0, nz - 1)], ZR),
        ):
            arrived(ref, send_sem.at[layer, phase])
        if layer + 1 < LAYERS:
            arrived(lz_r.at[0, pl.ds(0, nz - 1)], send_sem.at[layer, LZ])
            arrived(lz_r.at[1], send_sem.at[layer, LW])
            if owners > 1:
                arrived(x_half.at[layer + 1, pl.ds(0, owners - 1)], send_sem.at[layer, ZA])
        else:
            if owners > 1:
                arrived(out.at[core, most], send_sem.at[layer, ZA])
            arrived(out.at[1 - core], send_sem.at[layer, ZB])


def finish(hidden, new_keys, new_values, out, out_keys, out_values, sem):
    copies = [
        pltpu.make_async_copy(hidden.at[0], out.at[:, 0], sem.at[0]),
        pltpu.make_async_copy(hidden.at[1], out.at[:, 1], sem.at[1]),
        pltpu.make_async_copy(new_keys, out_keys, sem.at[2]),
        pltpu.make_async_copy(new_values, out_values, sem.at[3]),
    ]
    for copy in copies:
        copy.start()
    for copy in copies:
        copy.wait()


def on_device(
    n_chip, side, nz, width,
    hidden_in, norm_gain, q_gain, k_gain, w_query, w_key, w_value, w_out,
    cache_keys, cache_values, lengths, block_owner, block_fill,
):
    half = 8 * n_chip
    owners = nz // 2
    part = half // owners
    blocks = cache_keys.shape[1]
    total = hidden_in.shape[0]
    heads = w_query.shape[2]
    exponent = np.concatenate([np.arange(64), np.arange(64)]) * 2.0 / 128
    frequency = jnp.asarray((THETA**-exponent).astype(np.float32)[None, :])
    vmem, sem = pltpu.VMEM, pltpu.SemaphoreType.DMA
    anywhere = pl.BlockSpec(memory_space=pl.ANY)
    both = (LAYERS, n_chip)
    onchip = pl.BlockSpec(memory_space=pltpu.VMEM)
    news = jax.ShapeDtypeStruct((LAYERS, 8, 128), BF16)
    chip_news = vmem((LAYERS, 8, 128), BF16)
    hidden, new_keys, new_values = pl.pallas_call(
        functools.partial(kernel, n_chip, side, nz, float(width)),
        out_shape=(vmem((2, half, 128), BF16), chip_news, chip_news),
        in_specs=[anywhere] * 14,
        out_specs=(onchip, onchip, onchip),
        scratch_shapes=[
            vmem((total, 128), BF16),
            vmem((total, 128), BF16),
            vmem((LAYERS, 256), BF16),
            vmem((LAYERS, 128), BF16),
            vmem((LAYERS, 128), BF16),
            vmem((LAYERS, 256, heads), BF16),
            vmem((LAYERS, 256, 128), BF16),
            vmem((LAYERS, 256, 128), BF16),
            vmem((LAYERS, 2, heads, 128), BF16),
            vmem((LAYERS, blocks + 1, 128, 128), BF16),
            vmem((LAYERS, blocks + 1, 128, 128), BF16),
            vmem((1, total), jnp.int32),
            pltpu.SMEM((blocks,), jnp.int32),
            pltpu.SMEM((blocks,), jnp.int32),
            vmem((1, 128), F32),
            vmem((LAYERS, owners, part, 256), BF16),
            vmem((8, blocks * 128), F32),
            vmem((8, 128), F32),
            vmem((8, 9 * 128), F32),
            vmem((8, 128), F32),
            vmem((8, 128), F32),
            vmem((16, 128), F32),
            vmem((16, 128), F32),
            vmem((8, 128), F32),
            vmem((half, 16), BF16),
            vmem((*both, 16, 384), BF16),
            vmem((*both, 16, 384), BF16),
            vmem((LAYERS, 1, 128), F32),
            vmem((*both, 1, 128), F32),
            vmem((LAYERS, 16, 128), BF16),
            vmem((LAYERS, 2 * n_chip, 16, 128), BF16),
            vmem((LAYERS, 1, 128), F32),
            vmem((LAYERS, 2 * n_chip, 1, 128), F32),
            vmem((8, 128), BF16),
            vmem((2, nz, 8, 128), BF16),
            vmem((LAYERS, 32, 128), F32),
            vmem((LAYERS, 32, 128), F32),
            vmem((LAYERS, 48, 128), BF16),
            vmem((*both, 48, 128), BF16),
            vmem((LAYERS, 1, 128), F32),
            vmem((*both, 1, 128), F32),
            vmem((LAYERS, owners, part, 256), BF16),
            vmem((LAYERS, nz, part, 256), BF16),
            vmem((part, 256), BF16),
            vmem((2, part, 128), BF16),
            sem((16,)),
            sem((10,)),
            sem((10,)),
            sem((LAYERS, 12)),
            sem((LAYERS, 12)),
        ],
        compiler_params=pltpu.CompilerParams(
            collective_id=0, has_side_effects=True, vmem_limit_bytes=60000 * 1024
        ),
        name="attention_layers",
    )(
        hidden_in, norm_gain, q_gain, k_gain, w_query, w_key, w_value, w_out,
        cache_keys, cache_values, lengths.reshape(1, total), block_owner, block_fill, frequency,
    )
    out, new_keys, new_values = pl.pallas_call(
        finish,
        out_shape=(jax.ShapeDtypeStruct((n_chip, 2, 8, 128), BF16), news, news),
        in_specs=[onchip] * 3,
        out_specs=(anywhere, anywhere, anywhere),
        scratch_shapes=[sem((4,))],
        compiler_params=pltpu.CompilerParams(vmem_limit_bytes=1024 * 1024),
        name="finish",
    )(hidden.reshape(2, n_chip, 8, 128), new_keys, new_values)
    return out.reshape(total, 128), new_keys, new_values


def solution(mesh):
    n_req, nz = mesh.shape["req"], mesh.shape["kv"]
    n_chip = n_req // 2
    side = math.isqrt(n_chip)
    in_specs = (
        P(None, "req"),
        P(None, "req"),
        P(),
        P(),
        P(None, "req", "kv"),
        P(None, "req", "kv"),
        P(None, "req", "kv"),
        P(None, "kv", "req"),
        P(None, "req", None, "kv"),
        P(None, "req", None, "kv"),
        P(),
        P("req"),
        P("req"),
    )
    out_specs = (P(None, "req"), P(None, "req", "kv"), P(None, "req", "kv"))
    return jax.shard_map(
        functools.partial(on_device, n_chip, side, nz, 128 * n_req),
        mesh=mesh,
        in_specs=in_specs,
        out_specs=out_specs,
        check_vma=False,
    )
```
